32 devices in a mesh: fsdp: 16 (over z, y, core), seq: 2 (over x).
Axes of the slice: x: 2, y: 2, z: 4, core: 2. Of those that a mesh axis runs over, the one named last changes fastest.
Arguments:
- stream: bfloat16 [6144, 1024], P(('fsdp', 'seq')), may hold values from -6 to 6
- cotangent: bfloat16 [6144, 1024], P(('fsdp', 'seq')), may hold values from -6 to 6
- doc_lengths: int32 [10], replicated, may hold values from 1 to 1153, 6144 in all
- attention_gain: bfloat16 [1024], P('fsdp'), may hold values from 0.5 to 1.5
- query_weight: bfloat16 [1024, 1024], P('fsdp'), may hold values from -0.1875 to 0.1875
- key_matrix: bfloat16 [1024, 512], P('fsdp'), may hold values from -0.1875 to 0.1875
- value_matrix: bfloat16 [1024, 512], P('fsdp'), may hold values from -0.1875 to 0.1875
- query_gain: bfloat16 [64], P('fsdp'), may hold values from 0.5 to 1.5
- key_gain: bfloat16 [64], P('fsdp'), may hold values from 0.5 to 1.5
- output_weight: bfloat16 [1024, 1024], P('fsdp'), may hold values from -3 to 3
- feedforward_gain: bfloat16 [1024], P('fsdp'), may hold values from 0.5 to 1.5
- gate_weight: bfloat16 [1024, 4608], P('fsdp'), may hold values from -0.1875 to 0.1875
- up_weight: bfloat16 [1024, 4608], P('fsdp'), may hold values from -0.1875 to 0.1875
- down_weight: bfloat16 [4608, 1024], P('fsdp'), may hold values from -0.09375 to 0.09375
Outputs:
- result: bfloat16 [6144, 1024], P(('fsdp', 'seq'))
- grad_stream: bfloat16 [6144, 1024], P(('fsdp', 'seq'))
- grad_attention_gain: float32 [1024], P('fsdp')
- grad_query: float32 [1024, 1024], P('fsdp')
- grad_key: float32 [1024, 512], P('fsdp')
- grad_value: float32 [1024, 512], P('fsdp')
- grad_query_gain: float32 [64], P('fsdp')
- grad_key_gain: float32 [64], P('fsdp')
- grad_output: float32 [1024, 1024], P('fsdp')
- grad_feedforward_gain: float32 [1024], P('fsdp')
- grad_gate: float32 [1024, 4608], P('fsdp')
- grad_up: float32 [1024, 4608], P('fsdp')
- grad_down: float32 [4608, 1024], P('fsdp')
The draws below stay inside these ranges and needn't reach their ends.
Inputs may be any that keep to these rules, and one draw needn't show every extreme that they name: `doc_lengths`: they sum to 6144, and the longest has exactly 1153 tokens.
All inputs are finite; a program needn't handle non-finite values.
Results may differ from the reference program's by a relative error of at most 0.03.
Values may be sent and summed in bfloat16 or wider, within the bound.
No kernel may reach another device: no remote copies, remote signals or barrier semaphores. Data moves between devices by JAX's collectives and lax.ppermute only.
A program may use at most 192 MiB of HBM per device.

```python
import math
import jax
import jax.numpy as jnp
import numpy as np
from jax import lax

MODEL_WIDTH = 1024
QUERY_HEAD_COUNT = 16
KEY_VALUE_HEADS = 8
HEAD_SIZE = 64
FF = 4608
BLOCK = 384
LOOKBACK = 3
MAXDOC = 1153
TOKENS = 6144
DOCS = 10


def block_levels(own_key, dims, cuts, low, top_value):
    loudness, own = 1.0, jax.random.fold_in(own_key, 6)
    for axis_at, shards_of in cuts:
        draws = jnp.exp(jax.random.uniform(jax.random.fold_in(own, axis_at), (shards_of,), jnp.float32, low / len(cuts), top_value / len(cuts)))
        loudness = loudness * jnp.repeat(draws, dims[axis_at] // shards_of).reshape([-1 if axis == axis_at else 1 for axis in range(len(dims))])
    return loudness


def length_profile(count, total, bound, skew):
    loads = [(1 << 20) // math.isqrt(grade ** skew) + 1 for grade in range(2, count + 1)]
    surplus, holding = total - bound - (count - 1), [1] * (count - 1)
    while surplus > 0:
        movable = [i for i in range(count - 1) if holding[i] < bound]
        whole, budget = sum([loads[i] for i in movable]), surplus
        for i in movable:
            more = min(bound - holding[i], max(1, budget * loads[i] // whole), surplus)
            holding[i] = holding[i] + more
            surplus = surplus - more
    return np.array([bound] + holding)


def uneven_parts(own_key, count, total, most, lean):
    if count == 2:
        one = jax.random.randint(own_key, (), max(1, total - most), min(most, total - 1) + 1)
        return jnp.stack([one, total - one])
    tallies = jnp.asarray(length_profile(count, total, most, lean), jnp.int32)
    couples = (count - 1) // 2
    donor, sink = tallies[1:1 + 2 * couples:2], tallies[2:2 + 2 * couples:2]
    margin = jnp.minimum(donor - 1, most - sink)
    passed = jax.random.randint(jax.random.fold_in(own_key, 1), (couples,), 0, 1 << 20) % (margin + 1)
    tallies = tallies.at[1:1 + 2 * couples:2].set(donor - passed).at[2:2 + 2 * couples:2].set(sink + passed)
    return tallies[jax.random.permutation(jax.random.fold_in(own_key, 2), count)]


def centred(key, dims, spread, most, cuts=(), kind=jnp.bfloat16):
    factor_of = block_levels(key, dims, cuts, -0.22, 0.18) if cuts else 1.0
    result = jax.random.normal(key, dims, jnp.float32) * spread * factor_of
    return jnp.minimum(jnp.maximum(result, -most), most).astype(kind)


def setup_inputs(seed: int = 0) -> dict:
    splits = jax.random.split(jax.random.key(seed), 15)
    stream = centred(splits[0], (TOKENS, MODEL_WIDTH), 1.0, 6.0, ((0, 32),))
    cotangent = centred(splits[1], (TOKENS, MODEL_WIDTH), 1.0, 6.0, ((0, 32),))
    doc_lengths = uneven_parts(splits[2], DOCS, TOKENS, MAXDOC, 2).astype(jnp.int32)
    attention_gain = jnp.clip(1.0 + 0.1 * jax.random.normal(splits[3], (MODEL_WIDTH,), jnp.float32), 0.5, 1.5).astype(jnp.bfloat16)
    query_weight = centred(splits[4], (MODEL_WIDTH, QUERY_HEAD_COUNT * HEAD_SIZE), MODEL_WIDTH ** -0.5, 0.1875, ((0, 16),))
    key_matrix = centred(splits[5], (MODEL_WIDTH, KEY_VALUE_HEADS * HEAD_SIZE), MODEL_WIDTH ** -0.5, 0.1875, ((0, 16),))
    value_matrix = centred(splits[6], (MODEL_WIDTH, KEY_VALUE_HEADS * HEAD_SIZE), MODEL_WIDTH ** -0.5, 0.1875, ((0, 16),))
    query_gain = jnp.clip(1.0 + 0.1 * jax.random.normal(splits[7], (HEAD_SIZE,), jnp.float32), 0.5, 1.5).astype(jnp.bfloat16)
    key_gain = jnp.clip(1.0 + 0.1 * jax.random.normal(splits[8], (HEAD_SIZE,), jnp.float32), 0.5, 1.5).astype(jnp.bfloat16)
    output_weight = centred(splits[9], (QUERY_HEAD_COUNT * HEAD_SIZE, MODEL_WIDTH), (max(MODEL_WIDTH // 256, 1)) ** -0.5, 3.0, ((0, 16),))
    feedforward_gain = jnp.clip(1.0 + 0.1 * jax.random.normal(splits[10], (MODEL_WIDTH,), jnp.float32), 0.5, 1.5).astype(jnp.bfloat16)
    gate_weight = centred(splits[11], (MODEL_WIDTH, FF), MODEL_WIDTH ** -0.5, 0.1875, ((0, 16),))
    up_weight = centred(splits[12], (MODEL_WIDTH, FF), MODEL_WIDTH ** -0.5, 0.1875, ((0, 16),))
    down_weight = centred(splits[13], (FF, MODEL_WIDTH), FF ** -0.5, 0.09375, ((0, 16),))
    return {"stream": stream, "cotangent": cotangent, "doc_lengths": doc_lengths, "attention_gain": attention_gain, "query_weight": query_weight, "key_matrix": key_matrix, "value_matrix": value_matrix, "query_gain": query_gain, "key_gain": key_gain, "output_weight": output_weight, "feedforward_gain": feedforward_gain, "gate_weight": gate_weight, "up_weight": up_weight, "down_weight": down_weight}


@jax.custom_vjp
def lower_bound(v):
    return lax.optimization_barrier(v.astype(jnp.bfloat16)).astype(jnp.float32)

@jax.custom_vjp
def lower_bound_backward(v):
    return v

def low_keep(v):
    return (lower_bound(v), None)

def low_pass(kept, grad):
    return (grad,)

def back_keep(v):
    return (v, None)

def back_low(kept, grad):
    return (lower_bound(grad),)
lower_bound.defvjp(low_keep, low_pass)
lower_bound_backward.defvjp(back_keep, back_low)
EPS = 1e-05
THETA = 1000000.0
NEGATIVE = -1e+30
HIGHEST = lax.Precision.HIGHEST

def product(left, right):
    return jnp.dot(left, right, precision=HIGHEST, preferred_element_type=jnp.float32)

def doc_start(starts, places):
    inside = starts[None, :] <= places[:, None]
    return lax.optimization_barrier(jnp.max(jnp.where(inside, starts[None, :], -1), axis=1)).astype(jnp.int32)

def rotate(values, start_offset):
    half = values.shape[-1] // 2
    ladder = jnp.arange(half, dtype=jnp.float32) * (2.0 / values.shape[-1])
    freq = jnp.power(THETA, -ladder)
    angle = start_offset.astype(jnp.float32)[:, None] * freq[None, :]
    cosine = jnp.cos(angle)[:, None, :]
    sine = jnp.sin(angle)[:, None, :]
    front = values[..., :half]
    behind = values[..., half:]
    return jnp.concatenate([front * cosine - behind * sine, behind * cosine + front * sine], axis=-1)

def prepare_heads(linear_map, norm_gain, start_offset, heads):
    count = linear_map.shape[0]
    split = linear_map.reshape(count, heads, -1)
    normed = split * lax.rsqrt(lax.optimization_barrier(jnp.mean(split * split, axis=-1, keepdims=True)) + EPS) * norm_gain
    return rotate(normed, start_offset).reshape(count, -1)

def row_norm(values, norm_gain):
    return values * lax.rsqrt(lax.optimization_barrier(jnp.mean(values * values, axis=-1, keepdims=True)) + EPS) * norm_gain

def reference(stream, cotangent, doc_lengths, attention_gain, query_weight, key_matrix, value_matrix, query_gain, key_gain, output_weight, feedforward_gain, gate_weight, up_weight, down_weight):
    lengths = doc_lengths.astype(jnp.int32)
    starts = (jnp.cumsum(lengths) - lengths).astype(jnp.int32)
    places = jnp.arange(TOKENS, dtype=jnp.int32)
    tok_start = doc_start(starts, places)
    start_offset = places - tok_start
    query_row_count = math.gcd(512, TOKENS)
    span_width = -(-(LOOKBACK * BLOCK) // query_row_count) * query_row_count
    frows = math.gcd(4096, TOKENS)
    group_size = QUERY_HEAD_COUNT // KEY_VALUE_HEADS
    scale = HEAD_SIZE ** (-0.5)
    key_start = jnp.concatenate([jnp.full((span_width,), -1, jnp.int32), tok_start])

    def forward(inputs, gain_one, weight_q, weight_k, weight_v, gain_q, key_norm_gain, weight_o, gain_two, weight_g, weight_u, weight_d):
        hidden_in = lower_bound(row_norm(inputs, gain_one))
        query_lin = lower_bound_backward(product(hidden_in, weight_q))
        key_linear = lower_bound_backward(product(hidden_in, weight_k))
        query_rows = lower_bound(lower_bound_backward(prepare_heads(query_lin, gain_q, start_offset, QUERY_HEAD_COUNT)))
        key_rows = lower_bound(lower_bound_backward(prepare_heads(key_linear, key_norm_gain, start_offset, KEY_VALUE_HEADS)))
        values = lower_bound(lower_bound_backward(product(hidden_in, weight_v)))
        pad_amount = jnp.zeros((span_width, KEY_VALUE_HEADS * HEAD_SIZE), jnp.float32)
        key_padded = jnp.concatenate([pad_amount, key_rows])
        value_padded = jnp.concatenate([pad_amount, values])

        def attend(index):
            begin_offset = (index * query_row_count).astype(jnp.int32)
            query_tile = lax.dynamic_slice_in_dim(query_rows, begin_offset, query_row_count, 0).reshape(query_row_count, KEY_VALUE_HEADS, group_size, HEAD_SIZE)
            key_tile = lax.dynamic_slice_in_dim(key_padded, begin_offset, span_width + query_row_count, 0).reshape(span_width + query_row_count, KEY_VALUE_HEADS, HEAD_SIZE)
            value_tile = lax.dynamic_slice_in_dim(value_padded, begin_offset, span_width + query_row_count, 0).reshape(span_width + query_row_count, KEY_VALUE_HEADS, HEAD_SIZE)
            query_start = lax.dynamic_slice_in_dim(tok_start, begin_offset, query_row_count, 0)
            block_start = lax.dynamic_slice_in_dim(key_start, begin_offset, span_width + query_row_count, 0)
            query_place = begin_offset + jnp.arange(query_row_count, dtype=jnp.int32)
            key_place = begin_offset - span_width + jnp.arange(span_width + query_row_count, dtype=jnp.int32)
            allowed = (block_start[None, :] == query_start[:, None]) & (key_place[None, :] <= query_place[:, None])
            score = jnp.einsum('qhgd,khd->hgqk', query_tile, key_tile, precision=HIGHEST) * scale
            score = lower_bound_backward(jnp.where(allowed, score, NEGATIVE))
            weight = lower_bound(jax.nn.softmax(score, axis=-1))
            mixed = jnp.einsum('hgqk,khd->qhgd', weight, value_tile, precision=HIGHEST)
            return lower_bound(lower_bound_backward(mixed.reshape(query_row_count, QUERY_HEAD_COUNT * HEAD_SIZE)))
        attended = lax.map(jax.checkpoint(attend), jnp.arange(TOKENS // query_row_count, dtype=jnp.int32)).reshape(TOKENS, QUERY_HEAD_COUNT * HEAD_SIZE)
        middle = inputs + lower_bound_backward(product(attended, weight_o))
        hidden_two = lower_bound(row_norm(middle, gain_two))

        def feed(rows_in):
            gate = lower_bound_backward(product(rows_in, weight_g))
            upward = lower_bound_backward(product(rows_in, weight_u))
            inner = lower_bound(jax.nn.silu(gate) * upward)
            return lower_bound_backward(product(inner, weight_d))
        fed = lax.map(jax.checkpoint(feed), hidden_two.reshape(TOKENS // frows, frows, MODEL_WIDTH)).reshape(TOKENS, MODEL_WIDTH)
        return middle + fed
    arrays = tuple((item.astype(jnp.float32) for item in (stream, attention_gain, query_weight, key_matrix, value_matrix, query_gain, key_gain, output_weight, feedforward_gain, gate_weight, up_weight, down_weight)))
    output, pullback = jax.vjp(forward, *arrays)
    grads = pullback(cotangent.astype(jnp.float32))
    return (output.astype(jnp.bfloat16), grads[0].astype(jnp.bfloat16), grads[1], grads[2], grads[3], grads[4], grads[5], grads[6], grads[7], grads[8], grads[9], grads[10], grads[11])
```

```python
import functools

import jax
import jax.numpy as jnp
from jax import lax
from jax.experimental import pallas as pl
from jax.experimental.pallas import tpu as pltpu
from jax.sharding import Mesh, PartitionSpec as P

QUERY_HEAD_COUNT = 16
KEY_VALUE_HEADS = 8
HEAD_SIZE = 64
DOC_MIN = 1024
EPS = 1e-05
THETA = 1000000.0
GROUP = 8
BF16 = jnp.bfloat16
F32 = jnp.float32
VMEM_LIMIT = 60 * 1024 * 1024

VM = pl.BlockSpec(memory_space=pltpu.VMEM)
SM = pl.BlockSpec(memory_space=pltpu.SMEM)


def nn(left, right):
    return lax.dot_general(left, right, (((1,), (0,)), ((), ())), preferred_element_type=F32)


def nt(left, right):
    return lax.dot_general(left, right, (((1,), (1,)), ((), ())), preferred_element_type=F32)


def tn(left, right):
    return lax.dot_general(left, right, (((0,), (0,)), ((), ())), preferred_element_type=F32)


def call(kernel, outs, n_smem, args, flops, name, scratch=()):
    bytes_moved = sum(a.size * a.dtype.itemsize for a in args) + sum(
        o.size * o.dtype.itemsize for o in outs
    )
    return pl.pallas_call(
        kernel,
        out_shape=outs,
        in_specs=[SM] * n_smem + [VM] * (len(args) - n_smem),
        out_specs=[VM] * len(outs),
        scratch_shapes=list(scratch),
        compiler_params=pltpu.CompilerParams(vmem_limit_bytes=VMEM_LIMIT),
        cost_estimate=pl.CostEstimate(flops=flops, bytes_accessed=bytes_moved, transcendentals=0),
        name=name,
    )(*args)


def shape(dims, dtype):
    return jax.ShapeDtypeStruct(dims, dtype)


def rotated(x, lane):
    return jnp.where(lane % 64 < 32, -pltpu.roll(x, 96, 1), pltpu.roll(x, 32, 1))


def head_sum(x, low):
    first = jnp.sum(jnp.where(low, x, 0.0), axis=1, keepdims=True)
    second = jnp.sum(jnp.where(low, 0.0, x), axis=1, keepdims=True)
    return jnp.where(low, first, second)


def packed_weights(w_ref):
    shards, rows = w_ref.shape[0], w_ref.shape[1] - 16
    weights = w_ref[:, :rows, :].reshape(shards * rows, w_ref.shape[2])
    gains = jnp.sum(w_ref[:, rows : rows + 16, :].astype(F32), axis=0)[0:1]
    return weights, gains


def prepare_kernel(meta, *refs):
    blocks, (w_ref, cos_ref, sin_ref, q_ref, kv_ref, lin_ref) = refs[:GROUP], refs[GROUP:]
    weights, gains = packed_weights(w_ref)
    rows = blocks[0].shape[0]
    lane = lax.broadcasted_iota(jnp.int32, (rows, 128), 1)
    low = lane < 64
    for k in range(GROUP):
        at = pl.ds(pl.multiple_of((meta[0] ^ k) * rows, rows & -rows), rows)
        lin = nn(blocks[k][...], weights)
        lin_ref[at, :] = lin
        cosine, sine = cos_ref[at, :], sin_ref[at, :]
        front, back = lin[:, :128], lin[:, 128:]
        head = front * lax.rsqrt(head_sum(front * front, low) * (1 / 64) + EPS) * gains[:, :128]
        head = (head * cosine + rotated(head, lane) * sine) * (HEAD_SIZE**-0.5)
        q_ref[0, at, :] = jnp.where(low, head, 0.0).astype(BF16)
        q_ref[1, at, :] = jnp.where(low, pltpu.roll(head, 64, 1), 0.0).astype(BF16)
        key = back * lax.rsqrt(head_sum(back * back, low) * (1 / 64) + EPS) * gains[:, 128:]
        key = key * cosine + rotated(key, lane) * sine
        kv_ref[at, :] = jnp.where(low, key, back).astype(BF16)


def query_bounds(lengths, first, count):
    lane = lax.broadcasted_iota(jnp.int32, (1, 2 * count), 1)
    place = first + jnp.where(lane >= count, lane - count, lane)
    start = jnp.zeros((1, 2 * count), jnp.int32)
    begin, lowest = jnp.int32(0), jnp.int32(0)
    for d in range(lengths.shape[0]):
        start = jnp.where(place >= begin, begin, start)
        lowest = jnp.where(first >= begin, begin, lowest)
        begin = begin + lengths[d]
    return place, start, lowest


def attend_kernel(halo, span, meta, lengths, q_ref, kv_ref, out_ref, log_ref):
    step = pl.program_id(0)
    base = meta[1] - halo
    place, start, lowest = query_bounds(lengths, meta[1] + step * span, span)
    queries = q_ref[...].reshape(2 * span, 128)
    iota = lax.broadcasted_iota(jnp.int32, (span, 2 * span), 0)
    first = jnp.maximum(lowest - base, 0) // span

    def body(at, carry):
        total, mixed = carry
        offset = pl.multiple_of(at * span, span)
        keys = kv_ref[pl.ds(offset, span), :]
        score = nt(keys, queries)
        moved = base + offset
        weight = jnp.where((iota >= start - moved) & (iota <= place - moved), jnp.exp(score), 0.0)
        total = total + jnp.sum(weight, axis=0, keepdims=True)
        mixed = mixed + tn(keys, weight.astype(BF16))
        return total, mixed

    total, mixed = lax.fori_loop(
        first,
        step + halo // span + 1,
        body,
        (jnp.zeros((1, 2 * span), F32), jnp.zeros((128, 2 * span), F32)),
    )
    mixed = mixed * (1.0 / total)
    side = jnp.concatenate([mixed[64:, :span], mixed[64:, span:]], axis=0)
    out_ref[...] = side.T.astype(BF16)
    log_ref[...] = jnp.broadcast_to(jnp.log(total), (8, 2 * span))


def attend_back_kernel(
    halo, span, meta, lengths, q_ref, kv_ref, grad_ref, out_ref, log_ref, dq_ref, dkv_ref
):
    step = pl.program_id(0)
    base = meta[1] - halo

    @pl.when(step == 0)
    def _():
        dkv_ref[...] = jnp.zeros_like(dkv_ref)

    place, start, lowest = query_bounds(lengths, meta[1] + step * span, span)
    queries = q_ref[...].reshape(2 * span, 128)
    grad = grad_ref[...].astype(F32)
    low = lax.broadcasted_iota(jnp.int32, (span, 128), 1) < 64
    grads = jnp.concatenate(
        [jnp.where(low, 0.0, pltpu.roll(grad, 64, 1)), jnp.where(low, 0.0, grad)], axis=0
    ).astype(BF16)
    both = (grad * out_ref[...].astype(F32)).T
    row_sum = jnp.concatenate(
        [jnp.sum(both[:64], axis=0, keepdims=True), jnp.sum(both[64:], axis=0, keepdims=True)],
        axis=1,
    )
    logs = log_ref[0:1, :]
    iota = lax.broadcasted_iota(jnp.int32, (span, 2 * span), 0)
    first = jnp.maximum(lowest - base, 0) // span

    def body(at, dq):
        offset = pl.multiple_of(at * span, span)
        keys = kv_ref[pl.ds(offset, span), :]
        moved = base + offset
        weight = jnp.where(
            (iota >= start - moved) & (iota <= place - moved),
            jnp.exp(nt(keys, queries) - logs),
            0.0,
        )
        d_score = (weight * (nt(keys, grads) - row_sum)).astype(BF16)
        dkv_ref[pl.ds(offset, span), :] += nn(d_score, queries) + nn(weight.astype(BF16), grads)
        return dq + tn(keys, d_score)

    dq = lax.fori_loop(
        first, step + halo // span + 1, body, jnp.zeros((128, 2 * span), F32)
    ) * (HEAD_SIZE**-0.5)
    dq_ref[...] = jnp.concatenate([dq[:64, :span], dq[:64, span:]], axis=0).T.astype(BF16)


def project_kernel(meta, att_ref, w_ref, *outs):
    rows = outs[0].shape[0]
    for k in range(GROUP):
        at = pl.ds(pl.multiple_of((meta[0] ^ k) * rows, rows & -rows), rows)
        outs[k][...] = nn(att_ref[at, :], w_ref[...]).astype(BF16)


def unproject_kernel(meta, *refs):
    blocks, (w_ref, out_ref) = refs[:GROUP], refs[GROUP:]
    rows = blocks[0].shape[0]
    for k in range(GROUP):
        at = pl.ds(pl.multiple_of((meta[0] ^ k) * rows, rows & -rows), rows)
        out_ref[at, :] = nt(blocks[k][...], w_ref[...]).astype(BF16)


def finish_kernel(meta, dq_ref, dkv_ref, lin_ref, cos_ref, sin_ref, w_ref, *outs):
    hidden, (dlin_ref, gain_ref) = outs[:GROUP], outs[GROUP:]
    weights, gains = packed_weights(w_ref)
    rows = hidden[0].shape[0]
    lane = lax.broadcasted_iota(jnp.int32, (rows, 128), 1)
    low = lane < 64
    gain_sums = [jnp.zeros((1, 128), F32), jnp.zeros((1, 128), F32)]
    for k in range(GROUP):
        at = pl.ds(pl.multiple_of((meta[0] ^ k) * rows, rows & -rows), rows)
        cosine, sine = cos_ref[at, :], sin_ref[at, :]
        parts = []
        for side, source in enumerate((dq_ref, dkv_ref)):
            lin = lin_ref[at, 128 * side : 128 * side + 128]
            factor = lax.rsqrt(head_sum(lin * lin, low) * (1 / 64) + EPS)
            plain = lin * factor
            given = source[at, :].astype(F32)
            turned = given * cosine - rotated(given, lane) * sine
            gain_sums[side] = gain_sums[side] + jnp.sum(turned * plain, axis=0, keepdims=True)
            scaled = turned * gains[:, 128 * side : 128 * side + 128]
            grad = factor * (scaled - plain * (head_sum(scaled * plain, low) * (1 / 64)))
            parts.append(jnp.where(low, grad, given) if side else grad)
        dlin = jnp.concatenate(parts, axis=1).astype(BF16)
        dlin_ref[k * rows : k * rows + rows, :] = dlin
        hidden[k][...] = nt(dlin, weights).astype(BF16)
    gain_ref[...] = jnp.broadcast_to(jnp.concatenate(gain_sums, axis=1), gain_ref.shape)


def feed_kernel(ha, hb, ca, cb, wgu_ref, wd_ref, fed_a, fed_b, two_a, two_b, inner_ref, dgu_ref):
    rows = ha.shape[0]
    main = wgu_ref.shape[1] // 2 - 64
    hidden = jnp.concatenate([ha[...], hb[...]], axis=0)
    cotangent = jnp.concatenate([ca[...], cb[...]], axis=0)
    both = nn(hidden, wgu_ref[...])
    d_inner = nt(cotangent, wd_ref[...])
    low = lax.broadcasted_iota(jnp.int32, (2 * rows, 128), 1) < 64

    def piece(gate, up, given):
        sigma = 1.0 / (1.0 + jnp.exp(-gate))
        act = gate * sigma
        return act * up, given * up * (sigma * (1.0 + gate * (1.0 - sigma))), given * act

    tile = both[:, main : main + 128]
    inner_m, dg_m, du_m = piece(both[:, :main], both[:, main + 128 :], d_inner[:, :main])
    inner_t, dg_t, du_t = piece(tile, pltpu.roll(tile, 64, 1), d_inner[:, main:])
    inner = jnp.concatenate([inner_m, jnp.where(low, inner_t, 0.0)], axis=1).astype(BF16)
    d_tile = jnp.where(low, dg_t, pltpu.roll(du_t, 64, 1))
    dgu = jnp.concatenate([dg_m, d_tile, du_m], axis=1).astype(BF16)
    inner_ref[...] = inner
    dgu_ref[...] = dgu
    two = nt(dgu, wgu_ref[...]).astype(BF16)
    two_a[...] = two[:rows]
    two_b[...] = two[rows:]
    fed = nn(inner, wd_ref[...]).astype(BF16)
    fed_a[...] = fed[:rows]
    fed_b[...] = fed[rows:]


def swap(value, mask):
    return lax.ppermute(value, ("i", "s"), [(r, r ^ mask) for r in range(GROUP)])


def gather_blocks(value):
    blocks = {0: value}
    for k in (1, 4, 5):
        blocks[k] = swap(value, k)
    for k in (0, 1, 4, 5):
        blocks[k ^ 2] = swap(blocks[k], 2)
    return [blocks[k] for k in range(GROUP)]


def scatter_sum(parts):
    near = {k: parts[k].astype(F32) + swap(parts[k ^ 2], 2).astype(F32) for k in (5, 4, 1, 0)}
    total = near[0]
    for k in (5, 4, 1):
        total = total + swap(near[k].astype(BF16), k).astype(F32)
    return total


def gather_seq(value, count, place):
    if count != 2:
        return lax.all_gather(value, "s", axis=0)
    other = lax.ppermute(value, "s", [(0, 1), (1, 0)])
    return jnp.where(
        place == 0, jnp.stack([value, other]), jnp.stack([other, value])
    )


def normalized(values):
    factor = lax.rsqrt(jnp.mean(values * values, axis=-1, keepdims=True) + EPS)
    return values * factor, factor


def norm_back(grad, plain, factor):
    return factor * (grad - plain * jnp.mean(grad * plain, axis=-1, keepdims=True))


def on_device(
    stream,
    cotangent,
    doc_lengths,
    attention_gain,
    query_weight,
    key_matrix,
    value_matrix,
    query_gain,
    key_gain,
    output_weight,
    feedforward_gain,
    gate_weight,
    up_weight,
    down_weight,
):
    rows, width = stream.shape
    outer, inner_count, seq = (lax.axis_size(a) for a in ("o", "i", "s"))
    o, i, s = (lax.axis_index(a) for a in ("o", "i", "s"))
    shards = outer * inner_count
    me = i * seq + s
    tokens = GROUP * rows
    block = rows * seq
    lookback = max(2, -(-DOC_MIN // block))
    halo = lookback * block
    span = 2 * rows
    k_rows = query_weight.shape[0]
    o_rows = output_weight.shape[0]
    ff_rows = down_weight.shape[0] // seq
    ff_local = outer * ff_rows
    main = ff_local - 64

    def kv_head(i_at, s_at):
        if inner_count == 1:
            return s_at
        return 4 * s_at + 2 * (i_at % 2) + i_at // 2

    shard = o * inner_count + i
    meta = jnp.stack([me, o * tokens]).astype(jnp.int32)
    lengths = doc_lengths.astype(jnp.int32)
    stream_f = stream.astype(F32)
    plain_one, factor_one = normalized(stream_f)
    own_n = plain_one.astype(BF16)

    gain_one = attention_gain.astype(F32)[:, None]
    scaled_q = (query_weight.astype(F32) * gain_one).astype(BF16)
    scaled_k = (key_matrix.astype(F32) * gain_one).astype(BF16)
    scaled_v = (value_matrix.astype(F32) * gain_one).astype(BF16)
    lane = jnp.arange(HEAD_SIZE, dtype=jnp.int32)
    per = query_gain.shape[0]
    own_lane = lane // per == shard
    spread_q = jnp.where(own_lane, jnp.tile(query_gain, shards), 0)
    spread_k = jnp.where(own_lane, jnp.tile(key_gain, shards), 0)
    gain_row = jnp.concatenate([spread_q, spread_q, spread_k, jnp.zeros_like(spread_k)])
    gain_rows = jnp.pad(gain_row[None, :], ((0, 15), (0, 0)))
    pieces = []
    for i_at in range(inner_count):
        options = []
        for s_at in range(seq):
            t = kv_head(i_at, s_at)
            options.append(
                jnp.concatenate(
                    [
                        scaled_q[:, 128 * t : 128 * t + 128],
                        scaled_k[:, 64 * t : 64 * t + 64],
                        scaled_v[:, 64 * t : 64 * t + 64],
                    ],
                    axis=1,
                )
            )
        chosen = options[0]
        for s_at in range(1, seq):
            chosen = jnp.where(s == s_at, options[s_at], chosen)
        pieces.append(jnp.concatenate([chosen, gain_rows]))
    packed = jnp.stack(pieces)
    if inner_count > 1:
        packed = lax.all_to_all(packed, "i", split_axis=0, concat_axis=0, tiled=True)
    w_qkv = lax.all_gather(packed, "o", axis=0, tiled=True)

    n_blocks = gather_blocks(own_n)
    own_c, _ = lax.optimization_barrier((cotangent, n_blocks[7]))
    c_blocks = gather_blocks(own_c)

    own_down = lax.dynamic_slice_in_dim(down_weight, s * ff_rows, ff_rows, 0)
    rest = lax.all_gather(jnp.concatenate([own_down, output_weight]), "o", axis=0)
    w_down = jnp.pad(rest[:, :ff_rows].reshape(ff_local, width), ((0, 64), (0, 0)))
    out_rows = rest[:, ff_rows:]
    core = i % 2
    if inner_count == 1:
        w_out = lax.dynamic_slice_in_dim(out_rows.reshape(shards * o_rows, width), s * 128, 128, 0)
    else:
        mine = lax.dynamic_index_in_dim(out_rows, 2 * s + core, 0, keepdims=False)
        given = swap(lax.dynamic_index_in_dim(out_rows, 2 * s + 1 - core, 0, keepdims=False), 2)
        w_out = jnp.where(
            core == 0, jnp.concatenate([mine, given]), jnp.concatenate([given, mine])
        )

    gain_two = feedforward_gain.astype(F32)[:, None]

    def columns(weight):
        scaled = (weight.astype(F32) * gain_two).astype(BF16)
        split = scaled.reshape(k_rows, outer, inner_count, seq, ff_rows)
        chosen = lax.dynamic_index_in_dim(split, s, 3, keepdims=False)
        return chosen.transpose(2, 0, 1, 3).reshape(inner_count, k_rows, ff_local)

    gate_c, up_c = columns(gate_weight), columns(up_weight)
    packed_gu = jnp.concatenate(
        [gate_c[..., :main], gate_c[..., main:], up_c[..., main:], up_c[..., :main]], axis=-1
    )
    if inner_count > 1:
        packed_gu = lax.all_to_all(packed_gu, "i", split_axis=0, concat_axis=0, tiled=True)
    w_gu = lax.all_gather(
        packed_gu.reshape(inner_count * k_rows, 2 * ff_local), "o", axis=0, tiled=True
    )

    starts = jnp.cumsum(lengths) - lengths
    places = o * tokens + jnp.arange(tokens, dtype=jnp.int32)
    begin = jnp.max(jnp.where(starts[None, :] <= places[:, None], starts[None, :], -1), axis=1)
    half = HEAD_SIZE // 2
    freq = jnp.power(THETA, -(jnp.arange(half, dtype=F32) * (2.0 / HEAD_SIZE)))
    angle = (places - begin).astype(F32)[:, None] * freq[None, :]
    cosine = jnp.tile(jnp.cos(angle), (1, 4))
    sine = jnp.tile(jnp.sin(angle), (1, 4))

    queries, kv, lin = call(
        prepare_kernel,
        [
            shape((2, tokens, 128), BF16),
            shape((tokens, 128), BF16),
            shape((tokens, 256), F32),
        ],
        1,
        [meta, *n_blocks, w_qkv, cosine, sine],
        2 * tokens * width * 256,
        "prepare",
    )
    hops = -(-halo // tokens)
    earlier = []
    for hop in range(hops, 0, -1):
        tail = kv[tokens - (halo - (hops - 1) * tokens) :] if hop == hops else kv
        earlier.append(
            lax.ppermute(tail, "o", [(at, at + hop) for at in range(max(0, outer - hop))])
        )
    kv_all = jnp.concatenate([*earlier, kv])
    steps = tokens // span
    reach = halo + tokens
    pair_flops = 4 * tokens * (span + halo // 2) * 128

    def attention(kernel, ins, outs, flops, name):
        return pl.pallas_call(
            functools.partial(kernel, halo, span),
            grid=(steps,),
            in_specs=[SM, SM] + [spec for _, spec in ins],
            out_specs=[spec for _, spec in outs],
            out_shape=[dims for dims, _ in outs],
            compiler_params=pltpu.CompilerParams(
                vmem_limit_bytes=VMEM_LIMIT, dimension_semantics=("arbitrary",)
            ),
            cost_estimate=pl.CostEstimate(
                flops=flops, bytes_accessed=4 * reach * 256, transcendentals=0
            ),
            name=name,
        )(meta, lengths, *[value for value, _ in ins])

    q_spec = pl.BlockSpec((2, span, 128), lambda j: (0, j, 0))
    kv_spec = pl.BlockSpec((reach, 128), lambda j: (0, 0))
    row_spec = pl.BlockSpec((span, 128), lambda j: (j, 0))
    log_spec = pl.BlockSpec((8, 2 * span), lambda j: (j, 0))
    attended, logs = attention(
        attend_kernel,
        [(queries, q_spec), (kv_all, kv_spec)],
        [
            (shape((tokens, 128), BF16), row_spec),
            (shape((8 * steps, 2 * span), F32), log_spec),
        ],
        pair_flops,
        "attend",
    )

    parts = call(
        project_kernel,
        [shape((rows, width), BF16)] * GROUP,
        1,
        [meta, attended, w_out],
        2 * tokens * 128 * width,
        "project",
    )
    middle = stream_f + scatter_sum(parts)
    plain_two, factor_two = normalized(middle)
    h_blocks = gather_blocks(plain_two.astype(BF16))

    fed, two, inner, dgu = {}, {}, {}, {}
    for k in (0, 1, 4, 5):
        fed[k], fed[k ^ 2], two[k], two[k ^ 2], inner[k], dgu[k] = call(
            feed_kernel,
            [shape((rows, width), BF16)] * 4
            + [shape((span, ff_local + 64), BF16), shape((span, 2 * ff_local), BF16)],
            0,
            [h_blocks[k], h_blocks[k ^ 2], c_blocks[k], c_blocks[k ^ 2], w_gu, w_down],
            12 * span * width * ff_local,
            "feed",
        )
    order = (0, 2, 1, 3, 4, 6, 5, 7)
    h_all = jnp.concatenate([h_blocks[k] for k in order])
    c_all = jnp.concatenate([c_blocks[k] for k in order])
    dgu_all = jnp.concatenate([dgu[k] for k in (0, 1, 4, 5)])
    inner_all = jnp.concatenate([inner[k] for k in (0, 1, 4, 5)])
    d_mid_f = cotangent.astype(F32) + norm_back(scatter_sum(two), plain_two, factor_two)
    d_mid = d_mid_f.astype(BF16)
    m_blocks = gather_blocks(d_mid)
    result = (middle + scatter_sum(fed)).astype(BF16)

    grad_gu = tn(h_all, dgu_all).astype(BF16)
    grad_gu = lax.psum_scatter(grad_gu, "o", scatter_dimension=0, tiled=True)
    grad_dn = tn(inner_all, c_all)[:ff_local].astype(BF16)

    (d_attended,) = call(
        unproject_kernel,
        [shape((tokens, 128), BF16)],
        1,
        [meta, *m_blocks, w_out],
        2 * tokens * 128 * width,
        "unproject",
    )
    dq, dkv = attention(
        attend_back_kernel,
        [
            (queries, q_spec),
            (kv_all, kv_spec),
            (d_attended, row_spec),
            (attended, row_spec),
            (logs, log_spec),
        ],
        [(shape((tokens, 128), BF16), row_spec), (shape((reach, 128), F32), kv_spec)],
        3 * pair_flops,
        "attend_back",
    )
    d_own = dkv[halo:]
    for at, hop in enumerate(range(hops, 0, -1)):
        tail = halo - (hops - 1) * tokens
        begin_at = 0 if at == 0 else tail + (at - 1) * tokens
        size = tail if at == 0 else tokens
        back = lax.ppermute(
            dkv[begin_at : begin_at + size].astype(BF16),
            "o",
            [(p + hop, p) for p in range(max(0, outer - hop))],
        ).astype(F32)
        d_own = d_own + jnp.pad(back, ((tokens - size, 0), (0, 0)))
    *hidden_parts, dlin, gain_part = call(
        finish_kernel,
        [shape((rows, width), BF16)] * GROUP + [shape((tokens, 256), BF16), shape((8, 256), F32)],
        1,
        [meta, dq, d_own.astype(BF16), lin, cosine, sine, w_qkv],
        2 * tokens * width * 256,
        "finish",
    )
    d_stream = norm_back(scatter_sum(hidden_parts), plain_one, factor_one)
    grad_stream = (d_mid_f + d_stream).astype(BF16)

    at_abs = [lax.dynamic_slice_in_dim(attended, (me ^ k) * rows, rows, 0) for k in range(GROUP)]
    grad_out = tn(jnp.concatenate(at_abs), jnp.concatenate(m_blocks)).astype(BF16)
    spot = jnp.zeros((outer, o_rows, width), BF16)
    if inner_count == 1:
        spot = lax.dynamic_update_slice_in_dim(
            spot.reshape(shards * o_rows, width), grad_out, s * 128, 0
        ).reshape(outer, o_rows, width)
    else:
        kept = lax.dynamic_slice_in_dim(grad_out, core * 64, 64, 0)
        taken = swap(lax.dynamic_slice_in_dim(grad_out, (1 - core) * 64, 64, 0), 2)
        spot = lax.dynamic_update_slice_in_dim(spot, kept[None], 2 * s + core, 0)
        spot = lax.dynamic_update_slice_in_dim(spot, taken[None], 2 * s + 1 - core, 0)
    grad_rest = jnp.concatenate([grad_dn.reshape(outer, ff_rows, width), spot], axis=1)
    grad_rest = lax.psum_scatter(
        grad_rest.reshape(outer * (ff_rows + o_rows), width), "o", scatter_dimension=0, tiled=True
    )
    grad_rest = gather_seq(grad_rest, seq, s)
    grad_down = grad_rest[:, :ff_rows].reshape(seq * ff_rows, width).astype(F32)
    grad_output = jnp.sum(grad_rest[:, ff_rows:].astype(F32), axis=0)

    def to_owners(value, height):
        value = value.reshape(inner_count, height, -1)
        held = {0: lax.dynamic_index_in_dim(value, i, 0, keepdims=False)}
        for m in range(1, inner_count):
            piece = lax.dynamic_index_in_dim(value, i ^ m, 0, keepdims=False)
            held[m] = lax.ppermute(piece, "i", [(r, r ^ m) for r in range(inner_count)])
        return gather_seq(jnp.stack([held[m] for m in range(inner_count)]), seq, s)

    def by_rank(value):
        if inner_count == 1:
            return value.transpose(1, 0, 2, 3)
        at = jnp.arange(inner_count) ^ i
        return jnp.take(value, at, axis=1).transpose(1, 0, 2, 3)

    gu = by_rank(to_owners(grad_gu, k_rows)).astype(F32)

    def wide(value):
        split = value.reshape(inner_count, seq, k_rows, outer, ff_rows)
        return split.transpose(2, 3, 0, 1, 4).reshape(k_rows, -1)

    raw_gate = wide(gu[..., :ff_local])
    raw_up = wide(jnp.concatenate([gu[..., ff_local + 64 :], gu[..., ff_local : ff_local + 64]], axis=-1))
    grad_feedforward_gain = jnp.sum(
        raw_gate * gate_weight.astype(F32) + raw_up * up_weight.astype(F32), axis=1
    )
    grad_gate, grad_up = raw_gate * gain_two, raw_up * gain_two

    n_all = jnp.concatenate(n_blocks)
    grad_p = tn(n_all, dlin).astype(BF16).reshape(outer, inner_count, k_rows, 256)
    extra = jnp.broadcast_to(
        jnp.pad(gain_part[:1], ((0, 15), (0, 0))).astype(BF16), (outer, inner_count, 16, 256)
    )
    grad_p = jnp.concatenate([grad_p, extra], axis=2).reshape(outer, -1, 256)
    if outer <= 4:
        total = lax.dynamic_index_in_dim(grad_p, o, 0, keepdims=False).astype(F32)
        for m in range(1, outer):
            piece = lax.dynamic_index_in_dim(grad_p, o ^ m, 0, keepdims=False)
            total = total + lax.ppermute(
                piece, "o", [(r, r ^ m) for r in range(outer)]
            ).astype(F32)
        grad_p = total.astype(BF16)
    else:
        grad_p = lax.psum_scatter(grad_p, "o", scatter_dimension=0, tiled=True)[0]
    owned = by_rank(to_owners(grad_p, k_rows + 16)).astype(F32)
    sums = jnp.sum(owned[:, :, k_rows], axis=(0, 1))
    raw = {kv_head(a, b): owned[a, b, :k_rows] for a in range(inner_count) for b in range(seq)}
    raw_q = jnp.concatenate([raw[t][:, :128] for t in range(GROUP)], axis=1)
    raw_k = jnp.concatenate([raw[t][:, 128:192] for t in range(GROUP)], axis=1)
    raw_v = jnp.concatenate([raw[t][:, 192:] for t in range(GROUP)], axis=1)
    grad_attention_gain = (
        jnp.sum(raw_q * query_weight.astype(F32), axis=1)
        + jnp.sum(raw_k * key_matrix.astype(F32), axis=1)
        + jnp.sum(raw_v * value_matrix.astype(F32), axis=1)
    )
    grad_query_gain = lax.dynamic_slice_in_dim(sums[:64] + sums[64:128], shard * per, per, 0)
    grad_key_gain = lax.dynamic_slice_in_dim(sums[128:192], shard * per, per, 0)
    return (
        result,
        grad_stream,
        grad_attention_gain,
        raw_q * gain_one,
        raw_k * gain_one,
        raw_v * gain_one,
        grad_query_gain,
        grad_key_gain,
        grad_output,
        grad_feedforward_gain,
        grad_gate,
        grad_up,
        grad_down,
    )


def solution(mesh):
    fsdp, seq = mesh.shape["fsdp"], mesh.shape["seq"]
    inner = GROUP // seq
    split = Mesh(mesh.devices.reshape(fsdp // inner, inner, seq), ("o", "i", "s"))
    both = ("o", "i")
    tokens, matrix, vector = P(("o", "i", "s"), None), P(both, None), P(both)
    placed = (
        tokens,
        tokens,
        P(),
        vector,
        matrix,
        matrix,
        matrix,
        vector,
        vector,
        matrix,
        vector,
        matrix,
        matrix,
        matrix,
    )
    return jax.shard_map(
        on_device,
        mesh=split,
        in_specs=placed,
        out_specs=(
            tokens,
            tokens,
            vector,
            matrix,
            matrix,
            matrix,
            vector,
            vector,
            matrix,
            vector,
            matrix,
            matrix,
            matrix,
        ),
        check_vma=False,
    )
```

```python
import functools

import jax
import jax.numpy as jnp
from jax import lax
from jax.experimental import pallas as pl
from jax.experimental.pallas import tpu as pltpu
from jax.sharding import Mesh, PartitionSpec as P

QUERY_HEAD_COUNT = 16
KEY_VALUE_HEADS = 8
HEAD_SIZE = 64
DOC_MIN = 1024
EPS = 1e-05
THETA = 1000000.0
GROUP = 8
BF16 = jnp.bfloat16
F32 = jnp.float32
VMEM_LIMIT = 60 * 1024 * 1024

VM = pl.BlockSpec(memory_space=pltpu.VMEM)
SM = pl.BlockSpec(memory_space=pltpu.SMEM)


def nn(left, right):
    return lax.dot_general(left, right, (((1,), (0,)), ((), ())), preferred_element_type=F32)


def nt(left, right):
    return lax.dot_general(left, right, (((1,), (1,)), ((), ())), preferred_element_type=F32)


def tn(left, right):
    return lax.dot_general(left, right, (((0,), (0,)), ((), ())), preferred_element_type=F32)


def call(kernel, outs, n_smem, args, flops, name, scratch=()):
    bytes_moved = sum(a.size * a.dtype.itemsize for a in args) + sum(
        o.size * o.dtype.itemsize for o in outs
    )
    return pl.pallas_call(
        kernel,
        out_shape=outs,
        in_specs=[SM] * n_smem + [VM] * (len(args) - n_smem),
        out_specs=[VM] * len(outs),
        scratch_shapes=list(scratch),
        compiler_params=pltpu.CompilerParams(vmem_limit_bytes=VMEM_LIMIT),
        cost_estimate=pl.CostEstimate(flops=flops, bytes_accessed=bytes_moved, transcendentals=0),
        name=name,
    )(*args)


def shape(dims, dtype):
    return jax.ShapeDtypeStruct(dims, dtype)


def rotated(x, lane):
    return jnp.where(lane % 64 < 32, -pltpu.roll(x, 96, 1), pltpu.roll(x, 32, 1))


def head_sum(x, low):
    first = jnp.sum(jnp.where(low, x, 0.0), axis=1, keepdims=True)
    second = jnp.sum(jnp.where(low, 0.0, x), axis=1, keepdims=True)
    return jnp.where(low, first, second)


def pack_heads_kernel(kv_head, seq, meta, gains, q_ref, k_ref, v_ref, scale_ref, out_ref):
    count, rows = out_ref.shape[0], q_ref.shape[0]
    per = gains.shape[0] // 2
    scale = scale_ref[...]
    lane = lax.broadcasted_iota(jnp.int32, (16, 256), 1)
    row = lax.broadcasted_iota(jnp.int32, (16, 256), 0)
    extra = jnp.zeros((16, 256), F32)
    for j in range(per):
        spot = (lane % 64 == meta[2] * per + j) & (row == 0)
        extra = jnp.where(spot & (lane < 128), gains[j], extra)
        extra = jnp.where(spot & (lane >= 128) & (lane < 192), gains[per + j], extra)
    extra = extra.astype(BF16)
    for s_at in range(seq):

        @pl.when(meta[3] == s_at)
        def _():
            for i_at in range(count):
                t = kv_head(i_at, s_at)
                out_ref[i_at, :rows, :128] = (
                    q_ref[:, 128 * t : 128 * t + 128].astype(F32) * scale
                ).astype(BF16)
                pair = 128 * (t // 2)
                key = k_ref[:, pair : pair + 128].astype(F32) * scale
                value = v_ref[:, pair : pair + 128].astype(F32) * scale
                if t % 2:
                    key = pltpu.roll(key, 64, 1)
                else:
                    value = pltpu.roll(value, 64, 1)
                low = lax.broadcasted_iota(jnp.int32, key.shape, 1) < 64
                out_ref[i_at, :rows, 128:] = jnp.where(low, key, value).astype(BF16)

    for i_at in range(count):
        out_ref[i_at, rows:, :] = extra


def pack_kernel(
    kv_head, seq, outer, count, meta, gains, q_ref, k_ref, v_ref, one_ref, gate_ref, up_ref,
    two_ref, *refs
):
    *outs, heads, wide = refs
    pack_heads_kernel(kv_head, seq, meta, gains, q_ref, k_ref, v_ref, one_ref, heads)
    rows = q_ref.shape[0]
    piece = gate_ref.shape[1] // (outer * count * seq)
    local = outer * piece
    main = local - 64
    scale = two_ref[...]
    for m, out_ref in enumerate(outs):
        out_ref[:, 2 * local :] = heads[meta[4] ^ m]
        out_ref[rows:, : 2 * local] = jnp.zeros((16, 2 * local), BF16)
        for s_at in range(seq):
            for i_at in range(count):

                @pl.when((meta[3] == s_at) & (meta[4] ^ m == i_at))
                def _():
                    for side, source in enumerate((gate_ref, up_ref)):
                        for o_at in range(outer):
                            at = ((o_at * count + i_at) * seq + s_at) * piece
                            wide[side, :, o_at * piece : (o_at + 1) * piece] = (
                                source[:, at : at + piece].astype(F32) * scale
                            )
                    out_ref[:rows, :main] = wide[0, :, :main].astype(BF16)
                    out_ref[:rows, main : main + 128] = jnp.concatenate(
                        [wide[0, :, main:], wide[1, :, main:]], axis=1
                    ).astype(BF16)
                    out_ref[:rows, main + 128 : 2 * local] = wide[1, :, :main].astype(BF16)


def unpack_wide_kernel(outer, got_ref, gate_w, up_w, scale_ref, gate_ref, up_ref, gain_ref):
    ranks, rows = got_ref.shape[0], got_ref.shape[1]
    local = got_ref.shape[2] // 2
    piece, main = local // outer, local - 64
    for rank in range(ranks):
        got = got_ref[rank].astype(F32)
        up = jnp.concatenate([got[:, local + 64 :], got[:, local : local + 64]], axis=1)
        for value, out in ((got[:, :local], gate_ref), (up, up_ref)):
            for o_at in range(outer):
                at = (o_at * ranks + rank) * piece
                out[:, at : at + piece] = value[:, o_at * piece : (o_at + 1) * piece]
    scale = scale_ref[...]
    total = jnp.zeros((rows, 1), F32)
    for weight, out in ((gate_w, gate_ref), (up_w, up_ref)):
        raw = out[...]
        total = total + jnp.sum(raw * weight[...].astype(F32), axis=1, keepdims=True)
        out[...] = raw * scale
    gain_ref[...] = jnp.broadcast_to(total, gain_ref.shape)


def owners_kernel(
    kv_head, seq, per, meta, got_ref, q_w, k_w, v_w, scale_ref, q_ref, k_ref, v_ref, gain_ref, head_ref
):
    ranks, rows = got_ref.shape[0], q_w.shape[0]
    scale = scale_ref[...]
    total = jnp.zeros((rows, 1), F32)
    sums = jnp.zeros((16, 256), F32)
    low = lax.broadcasted_iota(jnp.int32, (rows, 128), 1) < 64
    back = {}
    for rank in range(ranks):
        t = kv_head(rank // seq, rank % seq)
        there = slice(128 * t, 128 * t + 128)
        part = got_ref[rank, :rows, :128].astype(F32)
        total = total + jnp.sum(part * q_w[:, there].astype(F32), axis=1, keepdims=True)
        q_ref[:, there] = part * scale
        back[t] = got_ref[rank, :rows, 128:].astype(F32)
        sums = sums + got_ref[rank, rows:, :].astype(F32)
    for t in range(0, ranks, 2):
        there = slice(64 * t, 64 * t + 128)
        key = jnp.where(low, back[t], pltpu.roll(back[t + 1], 64, 1))
        value = jnp.where(low, pltpu.roll(back[t], 64, 1), back[t + 1])
        for part, weight, out in ((key, k_w, k_ref), (value, v_w, v_ref)):
            total = total + jnp.sum(part * weight[:, there].astype(F32), axis=1, keepdims=True)
            out[:, there] = part * scale
    gain_ref[...] = jnp.broadcast_to(total, gain_ref.shape)
    row = sums[0:1, :128]
    row = row + pltpu.roll(row, 64, 1)
    row = jnp.concatenate([row, sums[0:1, 128:]], axis=1)
    lane = lax.broadcasted_iota(jnp.int32, (8, 128), 1)
    out = jnp.zeros((8, 128), F32)
    for j in range(per):
        here = lax.broadcasted_iota(jnp.int32, (1, 256), 1) % 128 == meta[2] * per + j
        picked = jnp.where(here, row, 0.0)
        q_j = jnp.sum(picked[:, :128], axis=1, keepdims=True)
        k_j = jnp.sum(picked[:, 128:], axis=1, keepdims=True)
        out = jnp.where(lane == j, q_j, out)
        out = jnp.where(lane == 64 + j, k_j, out)
    head_ref[...] = out


def prepare_kernel(meta, *refs):
    blocks, refs = refs[:GROUP], refs[GROUP:]
    sources = refs[:-9]
    cos_ref, sin_ref, q_ref, kv_ref, tail_ref, lin_ref, all_ref, w_ref, gain_ref = refs[-9:]
    rows = blocks[0].shape[0]
    gains = jnp.zeros((1, 256), F32)
    for m, source in enumerate(sources):
        parts, k_rows = source.shape[0], source.shape[1] - 16
        at = pl.multiple_of((meta[5] ^ m) * (parts * k_rows), parts * k_rows & -(parts * k_rows))
        if len(sources) == 1:
            at = 0
        w_ref[pl.ds(at, parts * k_rows), :] = source[:, :k_rows, :].reshape(parts * k_rows, 256)
        gains = gains + jnp.sum(source[:, k_rows:, :].astype(F32), axis=0)[0:1]
    gain_ref[...] = jnp.broadcast_to(gains, gain_ref.shape)
    weights = w_ref[...]
    lane = lax.broadcasted_iota(jnp.int32, (rows, 128), 1)
    low = lane < 64
    for k in range(GROUP):
        at = pl.ds(pl.multiple_of((meta[0] ^ k) * rows, rows & -rows), rows)
        own = blocks[k][...]
        all_ref[k * rows : (k + 1) * rows, :] = own
        lin = nn(own, weights)
        lin_ref[at, :] = lin
        cosine, sine = cos_ref[at, :], sin_ref[at, :]
        front, back = lin[:, :128], lin[:, 128:]
        head = front * lax.rsqrt(head_sum(front * front, low) * (1 / 64) + EPS) * gains[:, :128]
        head = (head * cosine + rotated(head, lane) * sine) * (HEAD_SIZE**-0.5)
        q_ref[0, at, :] = jnp.where(low, head, 0.0).astype(BF16)
        q_ref[1, at, :] = jnp.where(low, pltpu.roll(head, 64, 1), 0.0).astype(BF16)
        key = back * lax.rsqrt(head_sum(back * back, low) * (1 / 64) + EPS) * gains[:, 128:]
        key = key * cosine + rotated(key, lane) * sine
        kv_ref[at, :] = jnp.where(low, key, back).astype(BF16)
    tail_ref[...] = kv_ref[kv_ref.shape[0] - tail_ref.shape[0] :, :]


def query_bounds(lengths, first, count):
    lane = lax.broadcasted_iota(jnp.int32, (1, 2 * count), 1)
    place = first + jnp.where(lane >= count, lane - count, lane)
    start = jnp.zeros((1, 2 * count), jnp.int32)
    begin, lowest = jnp.int32(0), jnp.int32(0)
    for d in range(lengths.shape[0]):
        start = jnp.where(place >= begin, begin, start)
        lowest = jnp.where(first >= begin, begin, lowest)
        begin = begin + lengths[d]
    return place, start, lowest


def fill_keys(parts, keys_ref):
    @pl.when(pl.program_id(0) == 0)
    def _():
        at = 0
        for part in parts:
            keys_ref[at : at + part.shape[0], :] = part[...]
            at += part.shape[0]


def attend_kernel(halo, span, meta, lengths, q_ref, *refs):
    *parts, out_ref, log_ref, kv_ref = refs
    step = pl.program_id(0)
    base = meta[1] - halo
    fill_keys(parts, kv_ref)
    place, start, lowest = query_bounds(lengths, meta[1] + step * span, span)
    queries = q_ref[...].reshape(2 * span, 128)
    iota = lax.broadcasted_iota(jnp.int32, (span, 2 * span), 0)
    first = jnp.maximum(lowest - base, 0) // span

    def body(at, carry):
        total, mixed = carry
        offset = pl.multiple_of(at * span, span)
        keys = kv_ref[pl.ds(offset, span), :]
        score = nt(keys, queries)
        moved = base + offset
        weight = jnp.where((iota >= start - moved) & (iota <= place - moved), jnp.exp(score), 0.0)
        total = total + jnp.sum(weight, axis=0, keepdims=True)
        mixed = mixed + tn(keys, weight.astype(BF16))
        return total, mixed

    total, mixed = lax.fori_loop(
        first,
        step + halo // span + 1,
        body,
        (jnp.zeros((1, 2 * span), F32), jnp.zeros((128, 2 * span), F32)),
    )
    mixed = mixed * (1.0 / total)
    side = jnp.concatenate([mixed[64:, :span], mixed[64:, span:]], axis=0)
    out_ref[...] = side.T.astype(BF16)
    log_ref[...] = jnp.broadcast_to(jnp.log(total), (8, 2 * span))


def attend_back_kernel(halo, span, meta, lengths, q_ref, *refs):
    *parts, grad_ref, out_ref, log_ref, dq_ref, early_ref, own_ref, kv_ref, dkv_ref = refs
    step = pl.program_id(0)
    base = meta[1] - halo
    fill_keys(parts, kv_ref)

    @pl.when(step == 0)
    def _():
        dkv_ref[...] = jnp.zeros_like(dkv_ref)

    place, start, lowest = query_bounds(lengths, meta[1] + step * span, span)
    queries = q_ref[...].reshape(2 * span, 128)
    grad = grad_ref[...].astype(F32)
    low = lax.broadcasted_iota(jnp.int32, (span, 128), 1) < 64
    grads = jnp.concatenate(
        [jnp.where(low, 0.0, pltpu.roll(grad, 64, 1)), jnp.where(low, 0.0, grad)], axis=0
    ).astype(BF16)
    both = (grad * out_ref[...].astype(F32)).T
    row_sum = jnp.concatenate(
        [jnp.sum(both[:64], axis=0, keepdims=True), jnp.sum(both[64:], axis=0, keepdims=True)],
        axis=1,
    )
    logs = log_ref[0:1, :]
    iota = lax.broadcasted_iota(jnp.int32, (span, 2 * span), 0)
    first = jnp.maximum(lowest - base, 0) // span

    def body(at, dq):
        offset = pl.multiple_of(at * span, span)
        keys = kv_ref[pl.ds(offset, span), :]
        moved = base + offset
        weight = jnp.where(
            (iota >= start - moved) & (iota <= place - moved),
            jnp.exp(nt(keys, queries) - logs),
            0.0,
        )
        d_score = (weight * (nt(keys, grads) - row_sum)).astype(BF16)
        dkv_ref[pl.ds(offset, span), :] += nn(d_score, queries) + nn(weight.astype(BF16), grads)
        return dq + tn(keys, d_score)

    dq = lax.fori_loop(
        first, step + halo // span + 1, body, jnp.zeros((128, 2 * span), F32)
    ) * (HEAD_SIZE**-0.5)
    dq_ref[...] = jnp.concatenate([dq[:64, :span], dq[:64, span:]], axis=0).T.astype(BF16)

    @pl.when(step == pl.num_programs(0) - 1)
    def _():
        early_ref[...] = dkv_ref[:halo, :].astype(BF16)
        own_ref[...] = dkv_ref[halo:, :]


def project_kernel(meta, att_ref, w_ref, *outs):
    rows = outs[0].shape[0]
    for k in range(GROUP):
        at = pl.ds(pl.multiple_of((meta[0] ^ k) * rows, rows & -rows), rows)
        outs[k][...] = nn(att_ref[at, :], w_ref[...]).astype(BF16)


def unproject_kernel(meta, *refs):
    blocks, (w_ref, att_ref, out_ref, grad_ref) = refs[:GROUP], refs[GROUP:]
    unproject_body(meta, blocks, w_ref, att_ref, out_ref, grad_ref)


def unproject_into_kernel(meta, *refs):
    blocks, (w_ref, att_ref, _, out_ref, rest_ref, grad_ref, spot_ref, sem) = (
        refs[:GROUP],
        refs[GROUP:],
    )
    unproject_body(meta, blocks, w_ref, att_ref, out_ref, grad_ref)
    o_rows = spot_ref.shape[2]
    spot_ref[...] = jnp.zeros_like(spot_ref)
    for n in range(2):
        spot_ref[2 * meta[3] + meta[4] % 2, n] = grad_ref[n * o_rows : (n + 1) * o_rows, :]
    copy = pltpu.make_async_copy(
        spot_ref, rest_ref.at[:, :, pl.ds(rest_ref.shape[2] - o_rows, o_rows)], sem
    )
    copy.start()
    copy.wait()


def unproject_body(meta, blocks, w_ref, att_ref, out_ref, grad_ref):
    rows = blocks[0].shape[0]
    total = jnp.zeros(grad_ref.shape, F32)
    for k in range(GROUP):
        at = pl.ds(pl.multiple_of((meta[0] ^ k) * rows, rows & -rows), rows)
        own = blocks[k][...]
        out_ref[at, :] = nt(own, w_ref[...]).astype(BF16)
        total = total + tn(att_ref[at, :], own)
    grad_ref[...] = total.astype(BF16)


def finish_kernel(meta, dq_ref, own_ref, *refs):
    *backs, lin_ref, cos_ref, sin_ref, w_ref, gains_ref = refs[: -GROUP - 3]
    hidden, (dlin_ref, gain_ref, dkv_ref) = refs[-GROUP - 3 : -3], refs[-3:]
    dkv_ref[...] = own_ref[...]
    for back in backs:
        dkv_ref[dkv_ref.shape[0] - back.shape[0] :, :] += back[...].astype(F32)
    weights, gains = w_ref[...], gains_ref[0:1, :]
    rows = hidden[0].shape[0]
    lane = lax.broadcasted_iota(jnp.int32, (rows, 128), 1)
    low = lane < 64
    gain_sums = [jnp.zeros((1, 128), F32), jnp.zeros((1, 128), F32)]
    for k in range(GROUP):
        at = pl.ds(pl.multiple_of((meta[0] ^ k) * rows, rows & -rows), rows)
        cosine, sine = cos_ref[at, :], sin_ref[at, :]
        parts = []
        for side, source in enumerate((dq_ref, dkv_ref)):
            lin = lin_ref[at, 128 * side : 128 * side + 128]
            factor = lax.rsqrt(head_sum(lin * lin, low) * (1 / 64) + EPS)
            plain = lin * factor
            given = source[at, :].astype(BF16).astype(F32)
            turned = given * cosine - rotated(given, lane) * sine
            gain_sums[side] = gain_sums[side] + jnp.sum(turned * plain, axis=0, keepdims=True)
            scaled = turned * gains[:, 128 * side : 128 * side + 128]
            grad = factor * (scaled - plain * (head_sum(scaled * plain, low) * (1 / 64)))
            parts.append(jnp.where(low, grad, given) if side else grad)
        dlin = jnp.concatenate(parts, axis=1).astype(BF16)
        dlin_ref[k * rows : k * rows + rows, :] = dlin
        hidden[k][...] = nt(dlin, weights).astype(BF16)
    gain_ref[...] = jnp.broadcast_to(jnp.concatenate(gain_sums, axis=1), gain_ref.shape)


def project_grad_kernel(n_ref, d_ref, gain_ref, out_ref):
    rows = out_ref.shape[1] - 16
    grad = tn(n_ref[...], d_ref[...]).astype(BF16)
    extra = jnp.where(
        lax.broadcasted_iota(jnp.int32, (16, 256), 0) == 0, gain_ref[0:1, :], 0.0
    ).astype(BF16)
    for part in range(out_ref.shape[0]):
        out_ref[part, :rows, :] = grad[part * rows : (part + 1) * rows]
        out_ref[part, rows:, :] = extra


def spread_sum_kernel(seq, in_ref, out_ref):
    total = in_ref[0].astype(F32)
    for o_at in range(1, in_ref.shape[0]):
        total = total + in_ref[o_at].astype(F32)
    total = total.astype(BF16)
    for i_at in range(in_ref.shape[1]):
        for s_at in range(seq):
            out_ref[i_at * seq + s_at] = total[i_at]


def arrange_kernel(meta, *refs):
    *pieces, heads_ref, wide_ref = refs
    rows, columns = wide_ref.shape[1:]
    for m, piece in enumerate(pieces):
        heads_ref[meta[4] ^ m] = piece[:, columns:]
        wide_ref[meta[4] ^ m] = piece[:rows, :columns]


def wide_grad_kernel(h_ref, first_ref, second_ref, out_ref):
    rows = out_ref.shape[2]
    for n, ref in enumerate((first_ref, second_ref)):
        grad = tn(h_ref[...], ref[...]).astype(BF16)
        for o_at in range(out_ref.shape[0]):
            out_ref[o_at, n] = grad[o_at * rows : (o_at + 1) * rows]


def down_grad_kernel(rows, first_ref, second_ref, c_ref, out_ref):
    for n, ref in enumerate((first_ref, second_ref)):
        grad = tn(ref[...], c_ref[...]).astype(BF16)
        for o_at in range(out_ref.shape[0]):
            out_ref[o_at, n, :rows, :] = grad[o_at * rows : (o_at + 1) * rows]


def rest_out_kernel(meta, mine_ref, other_ref, down_ref, out_ref):
    rows = down_ref.shape[0] // 2
    mine, other = mine_ref[...].astype(F32), other_ref[...].astype(F32)
    out_ref[...] = mine[rows:] + other[rows:]
    first = meta[3] == 0
    down_ref[:rows, :] = jnp.where(first, mine[:rows], other[:rows])
    down_ref[rows:, :] = jnp.where(first, other[:rows], mine[:rows])


def near_kernel(*refs):
    for mine, far, out in zip(refs[:4], refs[4:8], refs[8:]):
        out[...] = (mine[...].astype(F32) + far[...].astype(F32)).astype(out.dtype)


def total_of(refs):
    total = refs[0][...].astype(F32)
    for ref in refs[1:]:
        total = total + ref[...].astype(F32)
    return total


def middle_kernel(*refs):
    *parts, middle_ref, plain_ref = refs
    middle = total_of(parts)
    middle_ref[...] = middle
    plain_ref[...] = normalized(middle)[0].astype(BF16)


def back_norm_kernel(*refs):
    source_ref, base_ref, *parts, full_ref, low_ref = refs
    plain, factor = normalized(source_ref[...].astype(F32))
    total = base_ref[...].astype(F32) + norm_back(total_of(parts), plain, factor)
    full_ref[...] = total
    low_ref[...] = total.astype(BF16)


def feed_kernel(count, down_rows, *refs):
    hs, cs, (wgu_in, wd_in), refs = refs[:count], refs[count : 2 * count], refs[2 * count :][:2], refs
    wgu_held, wd_held, sems = refs[-3:]
    fed_out, two_out = refs[-9 - 2 * count : -9 - count], refs[-9 - count : -9]
    h_ref, c_ref, *wide_refs = refs[-9:-3]
    up_rows = wgu_in.shape[2]
    copies = []
    for part in range(2):
        for n, (source, target, step) in enumerate(
            ((wgu_in, wgu_held, up_rows), (wd_in, wd_held, down_rows))
        ):
            copies.append(
                [
                    pltpu.make_async_copy(
                        source.at[o_at, part, pl.ds(0, step)],
                        target.at[part, pl.ds(o_at * step, step)],
                        sems.at[2 * part + n, o_at],
                    )
                    for o_at in range(source.shape[0])
                ]
            )
    for group in copies:
        for copy in group:
            copy.start()
    deep = wd_held.shape[1]
    for part in range(2):
        wd_held[part, deep - 64 :, :] = jnp.zeros((64, wd_held.shape[2]), BF16)
    rows = hs[0].shape[0]
    hidden = jnp.concatenate([h[...] for h in hs], axis=0)
    cotangent = jnp.concatenate([c[...] for c in cs], axis=0)
    h_ref[...] = hidden
    c_ref[...] = cotangent
    main = wgu_in.shape[3] // 2 - 64
    low = lax.broadcasted_iota(jnp.int32, (count * rows, 128), 1) < 64

    def piece(gate, up, given):
        sigma = 1.0 / (1.0 + jnp.exp(-gate))
        act = gate * sigma
        return act * up, given * up * (sigma * (1.0 + gate * (1.0 - sigma))), given * act

    two = fed = None
    for part in range(2):
        wgu_ref, wd_ref = wgu_held.at[part], wd_held.at[part]
        for copy in copies[2 * part]:
            copy.wait()
        both = nn(hidden, wgu_ref[...])
        for copy in copies[2 * part + 1]:
            copy.wait()
        d_inner = nt(cotangent, wd_ref[...])
        tile = both[:, main : main + 128]
        inner_m, dg_m, du_m = piece(both[:, :main], both[:, main + 128 :], d_inner[:, :main])
        inner_t, dg_t, du_t = piece(tile, pltpu.roll(tile, 64, 1), d_inner[:, main:])
        inner = jnp.concatenate([inner_m, jnp.where(low, inner_t, 0.0)], axis=1).astype(BF16)
        d_tile = jnp.where(low, dg_t, pltpu.roll(du_t, 64, 1))
        dgu = jnp.concatenate([dg_m, d_tile, du_m], axis=1).astype(BF16)
        wide_refs[2 * part][...] = dgu
        wide_refs[2 * part + 1][...] = inner
        more_two, more_fed = nt(dgu, wgu_ref[...]), nn(inner, wd_ref[...])
        two = more_two if two is None else two + more_two
        fed = more_fed if fed is None else fed + more_fed
    for n in range(count):
        two_out[n][...] = two[n * rows : (n + 1) * rows].astype(BF16)
        fed_out[n][...] = fed[n * rows : (n + 1) * rows].astype(BF16)


def feed(at, hs, cs, weights, down_rows, whole, tokens):
    count = len(hs)
    rows, width = hs[0].shape
    wide = weights[0].shape[3]
    deep = wide // 2 + 64
    widths = (width, width, wide, deep, wide, deep)

    def full(dims):
        return pl.BlockSpec(dims, lambda j: (0,) * len(dims))

    outs = pl.pallas_call(
        functools.partial(feed_kernel, count, down_rows),
        grid=(1,),
        in_specs=[full((rows, width))] * (2 * count)
        + [pl.BlockSpec(memory_space=pl.ANY)] * (2 + len(whole)),
        out_specs=[full((rows, width))] * (2 * count)
        + [pl.BlockSpec((count * rows, w), lambda j: (at, 0)) for w in widths],
        out_shape=[shape((rows, width), BF16)] * (2 * count)
        + [shape((tokens, w), BF16) for w in widths],
        scratch_shapes=[
            pltpu.VMEM((2, width, wide), BF16),
            pltpu.VMEM((2, deep, width), BF16),
            pltpu.SemaphoreType.DMA((4, max(w.shape[0] for w in weights))),
        ],
        input_output_aliases={2 * count + 2 + n: 2 * count + n for n in range(len(whole))},
        compiler_params=pltpu.CompilerParams(
            vmem_limit_bytes=VMEM_LIMIT, dimension_semantics=("arbitrary",)
        ),
        cost_estimate=pl.CostEstimate(
            flops=12 * count * rows * width * wide,
            bytes_accessed=2 * (3 * width * wide + 12 * count * rows * width),
            transcendentals=0,
        ),
        name="feed",
    )(*hs, *cs, *weights, *whole)
    return outs[:count], outs[count : 2 * count], outs[2 * count :]


def inner_swap(value, mask, count):
    return lax.ppermute(value, ("a", "b"), [(r, r ^ mask) for r in range(count)])


def swap(value, mask):
    return lax.ppermute(value, ("a", "b", "c"), [(r, r ^ mask) for r in range(GROUP)])


def after(value, *others):
    return lax.optimization_barrier((value, others))[0]


def gather_blocks(value):
    blocks = {0: value}
    for k in (1, 4, 5):
        blocks[k] = swap(value, k)
    for k in (0, 1, 4, 5):
        blocks[k ^ 2] = swap(blocks[k], 2)
    return [blocks[k] for k in range(GROUP)]


def near_sums(parts, first=None):
    order = (0, 1, 4, 5)
    far = [swap(parts[k ^ 2], 2) for k in order]
    if first is not None:
        far = list(after(tuple(far), first))
    block = parts[0].shape
    near = call(
        near_kernel,
        [shape(block, F32)] + [shape(block, BF16)] * 3,
        0,
        [*[parts[k] for k in order], *far],
        0,
        "near",
    )
    return [near[0]] + [swap(near[n], order[n]) for n in (1, 2, 3)]


def normalized(values):
    factor = lax.rsqrt(jnp.mean(values * values, axis=-1, keepdims=True) + EPS)
    return values * factor, factor


def norm_back(grad, plain, factor):
    return factor * (grad - plain * jnp.mean(grad * plain, axis=-1, keepdims=True))


def on_device(
    inner_count,
    stream,
    cotangent,
    doc_lengths,
    attention_gain,
    query_weight,
    key_matrix,
    value_matrix,
    query_gain,
    key_gain,
    output_weight,
    feedforward_gain,
    gate_weight,
    up_weight,
    down_weight,
):
    rows, width = stream.shape
    outer, seq = lax.axis_size("o"), GROUP // inner_count
    o = lax.axis_index("o")
    if inner_count == 1:
        i, s = jnp.int32(0), lax.axis_index(("a", "b", "c"))
    else:
        i, s = lax.axis_index(("a", "b")), lax.axis_index("c")
    shards = outer * inner_count
    me = i * seq + s
    tokens = GROUP * rows
    block = rows * seq
    lookback = max(2, -(-DOC_MIN // block))
    halo = lookback * block
    span = 2 * rows
    k_rows = query_weight.shape[0]
    o_rows = output_weight.shape[0]
    ff_rows = down_weight.shape[0] // seq
    ff_local = outer * ff_rows
    main = ff_local - 64
    few = outer <= 4

    def kv_head(i_at, s_at):
        if inner_count == 1:
            return s_at
        return 4 * s_at + 2 * (i_at % 2) + i_at // 2

    shard = o * inner_count + i
    per = query_gain.shape[0]
    meta = jnp.stack([me, o * tokens, shard, s, i, o]).astype(jnp.int32)
    lengths = doc_lengths.astype(jnp.int32)
    gain_one = attention_gain.astype(F32)[:, None]
    gain_two = feedforward_gain.astype(F32)[:, None]
    head_gains = jnp.concatenate([query_gain, key_gain]).astype(F32)

    def outer_gather(value):
        if not few:
            return lax.all_gather(value, "o", axis=0)
        value = jnp.broadcast_to(value[None], (outer, *value.shape))
        return lax.all_to_all(value, "o", split_axis=0, concat_axis=0, tiled=True)

    heads_in = [query_weight, key_matrix, value_matrix, gain_one]
    heads_shape = (inner_count, k_rows + 16, 256)
    chips = ("o", "b")
    if inner_count > 1:
        sent = call(
            functools.partial(pack_kernel, kv_head, seq, outer, inner_count),
            [shape((k_rows + 16, 2 * ff_local + 256), BF16)] * inner_count,
            2,
            [meta, head_gains, *heads_in, gate_weight, up_weight, gain_two],
            0,
            "pack",
            [pltpu.VMEM(heads_shape, BF16), pltpu.VMEM((2, k_rows, ff_local), F32)],
        )
        packed, packed_gu = call(
            arrange_kernel,
            [shape(heads_shape, BF16), shape((inner_count, k_rows, 2 * ff_local), BF16)],
            1,
            [meta, sent[0]] + [inner_swap(sent[m], m, inner_count) for m in range(1, inner_count)],
            0,
            "arrange",
        )
        half_down = lax.dynamic_slice_in_dim(down_weight, s * ff_rows, ff_rows, 0)
        w_rest = lax.all_gather(jnp.concatenate([half_down, output_weight]), chips, axis=0)
        w_rest = w_rest.reshape(outer, 2, ff_rows + o_rows, width)
        down_rows, w_down = ff_rows, w_rest
        w_out = lax.dynamic_index_in_dim(w_rest, 2 * s + i % 2, 0, keepdims=False)
        w_out = w_out[:, ff_rows:].reshape(128, width)
    else:
        (packed,) = call(
            functools.partial(pack_heads_kernel, kv_head, seq),
            [shape(heads_shape, BF16)],
            2,
            [meta, head_gains, *heads_in],
            0,
            "pack_heads",
        )

        def columns(weight):
            scaled = (weight.astype(F32) * gain_two).astype(BF16)
            split = scaled.reshape(k_rows, outer, seq, ff_rows)
            return lax.dynamic_index_in_dim(split, s, 2, keepdims=False).reshape(k_rows, ff_local)

        gate_c, up_c = columns(gate_weight), columns(up_weight)
        packed_gu = jnp.concatenate(
            [gate_c[:, :main], gate_c[:, main:], up_c[:, main:], up_c[:, :main]], axis=1
        )
        half_down = lax.dynamic_slice_in_dim(down_weight, s * ff_rows, ff_rows, 0)
        w_down = lax.all_gather(half_down, chips, axis=0).reshape(outer, 2, ff_rows, width)
        w_down = w_down.transpose(1, 0, 2, 3).reshape(1, 2, ff_local, width)
        down_rows = ff_local
        w_out = lax.all_gather(output_weight, "o", axis=0, tiled=True)
        w_out = lax.dynamic_slice_in_dim(w_out, s * 128, 128, 0)
    own_n = normalized(after(stream, packed).astype(F32))[0].astype(BF16)
    n_blocks = gather_blocks(own_n)
    near_n = (n_blocks[1], n_blocks[4], n_blocks[5])
    w_heads = outer_gather(packed.reshape(inner_count * (k_rows + 16), 256))
    w_heads = w_heads.reshape(shards, k_rows + 16, 256)
    packed_gu = after(packed_gu, near_n, w_heads)
    w_gu = lax.all_gather(
        packed_gu.reshape(inner_count * k_rows, 2 * ff_local), chips, axis=0
    ).reshape(outer, 2, inner_count * k_rows, 2 * ff_local)

    starts = jnp.cumsum(lengths) - lengths
    places = o * tokens + jnp.arange(tokens, dtype=jnp.int32)
    begin = jnp.max(jnp.where(starts[None, :] <= places[:, None], starts[None, :], -1), axis=1)
    half = HEAD_SIZE // 2
    freq = jnp.power(THETA, -(jnp.arange(half, dtype=F32) * (2.0 / HEAD_SIZE)))
    angle = (places - begin).astype(F32)[:, None] * freq[None, :]
    cosine = jnp.tile(jnp.cos(angle), (1, 4))
    sine = jnp.tile(jnp.sin(angle), (1, 4))

    own_c = after(cotangent, n_blocks[5])
    c_blocks = {0: own_c, 1: swap(own_c, 1), 4: swap(own_c, 4), 5: swap(own_c, 5)}
    hops = -(-halo // tokens)
    tail_rows = halo - (hops - 1) * tokens
    queries, kv, tail, lin, n_all, w_qkv, head_row = call(
        prepare_kernel,
        [
            shape((2, tokens, 128), BF16),
            shape((tokens, 128), BF16),
            shape((tail_rows, 128), BF16),
            shape((tokens, 256), F32),
            shape((tokens, width), BF16),
            shape((width, 256), BF16),
            shape((8, 256), F32),
        ],
        1,
        [meta, *n_blocks, w_heads, cosine, sine],
        2 * tokens * width * 256,
        "prepare",
    )
    keys = [
        lax.ppermute(
            tail if hop == hops else kv, "o", [(at, at + hop) for at in range(max(0, outer - hop))]
        )
        for hop in range(hops, 0, -1)
    ] + [kv]
    keys = list(after(tuple(keys), tuple(c_blocks.values())))
    steps = tokens // span
    reach = halo + tokens
    pair_flops = 4 * tokens * (span + halo // 2) * 128

    def attention(kernel, ins, outs, scratch, flops, name):
        return pl.pallas_call(
            functools.partial(kernel, halo, span),
            grid=(steps,),
            in_specs=[SM, SM] + [spec for _, spec in ins],
            out_specs=[spec for _, spec in outs],
            out_shape=[dims for dims, _ in outs],
            scratch_shapes=scratch,
            compiler_params=pltpu.CompilerParams(
                vmem_limit_bytes=VMEM_LIMIT, dimension_semantics=("arbitrary",)
            ),
            cost_estimate=pl.CostEstimate(
                flops=flops, bytes_accessed=4 * reach * 256, transcendentals=0
            ),
            name=name,
        )(meta, lengths, *[value for value, _ in ins])

    def still(value):
        return pl.BlockSpec(value.shape, lambda j: (0, 0))

    q_spec = pl.BlockSpec((2, span, 128), lambda j: (0, j, 0))
    row_spec = pl.BlockSpec((span, 128), lambda j: (j, 0))
    log_spec = pl.BlockSpec((8, 2 * span), lambda j: (j, 0))
    key_ins = [(part, still(part)) for part in keys]
    attended, logs = attention(
        attend_kernel,
        [(queries, q_spec), *key_ins],
        [
            (shape((tokens, 128), BF16), row_spec),
            (shape((8 * steps, 2 * span), F32), log_spec),
        ],
        [pltpu.VMEM((reach, 128), BF16)],
        pair_flops,
        "attend",
    )

    parts = call(
        project_kernel,
        [shape((rows, width), BF16)] * GROUP,
        1,
        [meta, attended, w_out],
        2 * tokens * 128 * width,
        "project",
    )
    near_parts = near_sums(parts)
    middle, plain_two = call(
        middle_kernel,
        [shape((rows, width), F32), shape((rows, width), BF16)],
        0,
        [stream, *near_parts],
        0,
        "middle",
    )

    h_blocks = {0: plain_two}
    for k in (1, 4, 5):
        h_blocks[k] = swap(h_blocks[0], k)
    fed, two, whole = {}, {}, []
    for at, ks in ((2, (0,)), (0, (1, 4)), (3, (5,))):
        fed_k, two_k, whole = feed(
            at,
            [h_blocks[k] for k in ks],
            [c_blocks[k] for k in ks],
            [w_gu, w_down],
            down_rows,
            whole,
            4 * rows,
        )
        for n, k in enumerate(ks):
            fed[k], two[k] = fed_k[n], two_k[n]
    h_all, c_all, dgu_0, inner_0, dgu_1, inner_1 = whole

    def from_chips(parts):
        return [parts[0]] + [swap(parts[k], k) for k in (1, 4, 5)]

    d_mid_f, d_mid = call(
        back_norm_kernel,
        [shape((rows, width), F32), shape((rows, width), BF16)],
        0,
        [middle, cotangent, *from_chips(two)],
        0,
        "back_two",
    )
    (grad_gu,) = call(
        wide_grad_kernel,
        [shape((outer, 2, inner_count * k_rows, 2 * ff_local), BF16)],
        0,
        [h_all, dgu_0, dgu_1],
        0,
        "wide_grad",
    )
    grad_gu = after(grad_gu, d_mid).reshape(-1, 2 * ff_local)
    grad_gu = lax.psum_scatter(grad_gu, chips, scatter_dimension=0, tiled=True)
    rest_rows = ff_rows + o_rows
    (grad_rest,) = call(
        functools.partial(down_grad_kernel, down_rows),
        [shape((outer, 2, rest_rows, width) if inner_count > 1 else (1, 2, ff_local, width), BF16)],
        0,
        [inner_0, inner_1, c_all],
        0,
        "down_grad",
    )
    m_blocks = gather_blocks(d_mid)
    if inner_count > 1:
        d_attended, grad_rest = pl.pallas_call(
            unproject_into_kernel,
            in_specs=[SM] + [VM] * (GROUP + 2) + [pl.BlockSpec(memory_space=pl.ANY)],
            out_specs=[VM, pl.BlockSpec(memory_space=pl.ANY)],
            out_shape=[shape((tokens, 128), BF16), shape(grad_rest.shape, BF16)],
            scratch_shapes=[
                pltpu.VMEM((128, width), BF16),
                pltpu.VMEM((outer, 2, o_rows, width), BF16),
                pltpu.SemaphoreType.DMA(()),
            ],
            input_output_aliases={GROUP + 3: 1},
            compiler_params=pltpu.CompilerParams(vmem_limit_bytes=VMEM_LIMIT),
            cost_estimate=pl.CostEstimate(
                flops=4 * tokens * 128 * width, bytes_accessed=8 << 20, transcendentals=0
            ),
            name="unproject",
        )(meta, *m_blocks, w_out, attended, grad_rest)
        grad_rest = lax.psum_scatter(
            grad_rest.reshape(-1, width), chips, scatter_dimension=0, tiled=True
        )
        grad_down, grad_output = call(
            rest_out_kernel,
            [shape((seq * ff_rows, width), F32), shape((o_rows, width), F32)],
            1,
            [meta, grad_rest, swap(grad_rest, 1)],
            0,
            "rest_out",
        )
    else:
        d_attended, grad_out = call(
            unproject_kernel,
            [shape((tokens, 128), BF16), shape((128, width), BF16)],
            1,
            [meta, *m_blocks, w_out, attended],
            4 * tokens * 128 * width,
            "unproject",
        )
        grad_rest = grad_rest.reshape(2, outer, ff_rows, width).transpose(1, 0, 2, 3)
        grad_rest = lax.psum_scatter(
            grad_rest.reshape(-1, width), chips, scatter_dimension=0, tiled=True
        )
        grad_down = lax.all_gather(grad_rest, ("a", "b", "c"), axis=0, tiled=True).astype(F32)
        spot = lax.dynamic_update_slice_in_dim(
            jnp.zeros((shards * o_rows, width), BF16), grad_out, s * 128, 0
        )
        spot = lax.psum_scatter(spot, "o", scatter_dimension=0, tiled=True)
        grad_output = lax.psum(spot, ("a", "b", "c")).astype(F32)

    def to_owners(value):
        value = jnp.repeat(value, seq, axis=0)
        return lax.all_to_all(value, ("a", "b", "c"), split_axis=0, concat_axis=0, tiled=True)

    got = to_owners(grad_gu.reshape(inner_count, k_rows, 2 * ff_local))
    dq, d_early, d_own = attention(
        attend_back_kernel,
        [
            (queries, q_spec),
            *key_ins,
            (d_attended, row_spec),
            (attended, row_spec),
            (logs, log_spec),
        ],
        [
            (shape((tokens, 128), BF16), row_spec),
            (shape((halo, 128), BF16), pl.BlockSpec((halo, 128), lambda j: (0, 0))),
            (shape((tokens, 128), F32), pl.BlockSpec((tokens, 128), lambda j: (0, 0))),
        ],
        [pltpu.VMEM((reach, 128), BF16), pltpu.VMEM((reach, 128), F32)],
        3 * pair_flops,
        "attend_back",
    )
    late = dict(zip(fed, after(tuple(fed.values()), m_blocks)))
    result = middle
    for part in from_chips(late):
        result = result + part.astype(F32)
    result = result.astype(BF16)
    d_early = after(d_early, result)
    backs = []
    for at, hop in enumerate(range(hops, 0, -1)):
        begin_at = 0 if at == 0 else tail_rows + (at - 1) * tokens
        size = tail_rows if at == 0 else tokens
        backs.append(
            lax.ppermute(
                d_early[begin_at : begin_at + size],
                "o",
                [(p + hop, p) for p in range(max(0, outer - hop))],
            )
        )
    *hidden_parts, dlin, gain_part = call(
        finish_kernel,
        [shape((rows, width), BF16)] * GROUP + [shape((tokens, 256), BF16), shape((8, 256), F32)],
        1,
        [meta, dq, d_own, *backs, lin, cosine, sine, w_qkv, head_row],
        2 * tokens * width * 256,
        "finish",
        [pltpu.VMEM((tokens, 128), F32)],
    )
    (grad_p,) = call(
        project_grad_kernel,
        [shape((shards, k_rows + 16, 256), BF16)],
        0,
        [n_all, dlin, gain_part],
        2 * tokens * width * 256,
        "project_grad",
    )
    near_h = near_sums(hidden_parts, grad_p)
    _, grad_stream = call(
        back_norm_kernel,
        [shape((rows, width), F32), shape((rows, width), BF16)],
        0,
        [stream, d_mid_f, *near_h],
        0,
        "back_one",
    )

    if inner_count > 1:
        grad_gate, grad_up, gain_sum = call(
            functools.partial(unpack_wide_kernel, outer),
            [shape((k_rows, GROUP * ff_local), F32)] * 2 + [shape((k_rows, 128), F32)],
            0,
            [got, gate_weight, up_weight, gain_two],
            0,
            "unpack_wide",
        )
        grad_feedforward_gain = gain_sum[:, 0]
    else:
        gu = got.astype(F32)

        def wide(value):
            split = value.reshape(inner_count, seq, k_rows, outer, ff_rows)
            return split.transpose(2, 3, 0, 1, 4).reshape(k_rows, -1)

        raw_gate = wide(gu[..., :ff_local])
        raw_up = wide(
            jnp.concatenate(
                [gu[..., ff_local + 64 :], gu[..., ff_local : ff_local + 64]], axis=-1
            )
        )
        grad_feedforward_gain = jnp.sum(
            raw_gate * gate_weight.astype(F32) + raw_up * up_weight.astype(F32), axis=1
        )
        grad_gate, grad_up = raw_gate * gain_two, raw_up * gain_two

    if few:
        grad_p = grad_p.reshape(outer, inner_count, k_rows + 16, 256)
        grad_p = lax.all_to_all(grad_p, "o", split_axis=0, concat_axis=0, tiled=True)
        grad_p = after(grad_p, near_h[0])
        (total,) = call(
            functools.partial(spread_sum_kernel, seq),
            [shape((GROUP, k_rows + 16, 256), BF16)],
            0,
            [grad_p],
            0,
            "spread_sum",
        )
        total = after(total, near_h[1:])
        owned = lax.all_to_all(total, ("a", "b", "c"), split_axis=0, concat_axis=0, tiled=True)
    else:
        owned = to_owners(lax.psum_scatter(grad_p, "o", scatter_dimension=0, tiled=True))
    grad_query, grad_key, grad_value, gain_sum, head_sums = call(
        functools.partial(owners_kernel, kv_head, seq, per),
        [
            shape(query_weight.shape, F32),
            shape(key_matrix.shape, F32),
            shape(value_matrix.shape, F32),
            shape((k_rows, 128), F32),
            shape((8, 128), F32),
        ],
        1,
        [meta, owned, query_weight, key_matrix, value_matrix, gain_one],
        0,
        "owners",
    )
    return (
        result,
        grad_stream,
        gain_sum[:, 0],
        grad_query,
        grad_key,
        grad_value,
        head_sums[0, :per],
        head_sums[0, 64 : 64 + per],
        grad_output,
        grad_feedforward_gain,
        grad_gate,
        grad_up,
        grad_down,
    )


def solution(mesh):
    fsdp, seq = mesh.shape["fsdp"], mesh.shape["seq"]
    inner = GROUP // seq
    split = Mesh(mesh.devices.reshape(fsdp // inner, 2, 2, 2), ("o", "a", "b", "c"))
    both = ("o", "a", "b") if inner > 1 else ("o",)
    tokens, matrix, vector = P(("o", "a", "b", "c"), None), P(both, None), P(both)
    placed = (
        tokens,
        tokens,
        P(),
        vector,
        matrix,
        matrix,
        matrix,
        vector,
        vector,
        matrix,
        vector,
        matrix,
        matrix,
        matrix,
    )
    return jax.shard_map(
        functools.partial(on_device, inner),
        mesh=split,
        in_specs=placed,
        out_specs=(
            tokens,
            tokens,
            vector,
            matrix,
            matrix,
            matrix,
            vector,
            vector,
            matrix,
            vector,
            matrix,
            matrix,
            matrix,
        ),
        check_vma=False,
    )
```

```python
import functools

import jax
import jax.numpy as jnp
from jax import lax
from jax.experimental import pallas as pl
from jax.experimental.pallas import tpu as pltpu
from jax.sharding import Mesh, PartitionSpec as P

QUERY_HEAD_COUNT = 16
KEY_VALUE_HEADS = 8
HEAD_SIZE = 64
DOC_MIN = 1024
EPS = 1e-05
THETA = 1000000.0
GROUP = 8
BF16 = jnp.bfloat16
F32 = jnp.float32
VMEM_LIMIT = 60 * 1024 * 1024

VM = pl.BlockSpec(memory_space=pltpu.VMEM)
SM = pl.BlockSpec(memory_space=pltpu.SMEM)
FAR = pl.BlockSpec(memory_space=pl.ANY)


def nn(left, right):
    return lax.dot_general(left, right, (((1,), (0,)), ((), ())), preferred_element_type=F32)


def nt(left, right):
    return lax.dot_general(left, right, (((1,), (1,)), ((), ())), preferred_element_type=F32)


def tn(left, right):
    return lax.dot_general(left, right, (((0,), (0,)), ((), ())), preferred_element_type=F32)


def call(kernel, outs, n_smem, args, flops, name, scratch=(), far_in=(), far_out=()):
    bytes_moved = sum(a.size * a.dtype.itemsize for a in args) + sum(
        o.size * o.dtype.itemsize for o in outs
    )
    return pl.pallas_call(
        kernel,
        out_shape=outs,
        in_specs=[
            SM if n < n_smem else FAR if n in far_in else VM for n in range(len(args))
        ],
        out_specs=[FAR if n in far_out else VM for n in range(len(outs))],
        scratch_shapes=list(scratch),
        compiler_params=pltpu.CompilerParams(vmem_limit_bytes=VMEM_LIMIT),
        cost_estimate=pl.CostEstimate(flops=flops, bytes_accessed=bytes_moved, transcendentals=0),
        name=name,
    )(*args)


def shape(dims, dtype):
    return jax.ShapeDtypeStruct(dims, dtype)


def rotated(x, lane):
    return jnp.where(lane % 64 < 32, -pltpu.roll(x, 96, 1), pltpu.roll(x, 32, 1))


def head_sum(x, low):
    first = jnp.sum(jnp.where(low, x, 0.0), axis=1, keepdims=True)
    second = jnp.sum(jnp.where(low, 0.0, x), axis=1, keepdims=True)
    return jnp.where(low, first, second)


def pack_heads_kernel(kv_head, seq, meta, gains, q_ref, k_ref, v_ref, scale_ref, out_ref):
    count, rows = out_ref.shape[0], q_ref.shape[0]
    per = gains.shape[0] // 2
    scale = scale_ref[...]
    lane = lax.broadcasted_iota(jnp.int32, (16, 256), 1)
    row = lax.broadcasted_iota(jnp.int32, (16, 256), 0)
    extra = jnp.zeros((16, 256), F32)
    for j in range(per):
        spot = (lane % 64 == meta[2] * per + j) & (row == 0)
        extra = jnp.where(spot & (lane < 128), gains[j], extra)
        extra = jnp.where(spot & (lane >= 128) & (lane < 192), gains[per + j], extra)
    extra = extra.astype(BF16)
    for s_at in range(seq):

        @pl.when(meta[3] == s_at)
        def _():
            for i_at in range(count):
                t = kv_head(i_at, s_at)
                out_ref[i_at, :rows, :128] = (
                    q_ref[:, 128 * t : 128 * t + 128].astype(F32) * scale
                ).astype(BF16)
                pair = 128 * (t // 2)
                key = k_ref[:, pair : pair + 128].astype(F32) * scale
                value = v_ref[:, pair : pair + 128].astype(F32) * scale
                if t % 2:
                    key = pltpu.roll(key, 64, 1)
                else:
                    value = pltpu.roll(value, 64, 1)
                low = lax.broadcasted_iota(jnp.int32, key.shape, 1) < 64
                out_ref[i_at, :rows, 128:] = jnp.where(low, key, value).astype(BF16)

    for i_at in range(count):
        out_ref[i_at, rows:, :] = extra


def send_heads_kernel(kv_head, seq, meta, gains, q_ref, k_ref, v_ref, scale_ref, *refs):
    *outs, heads = refs
    pack_heads_kernel(kv_head, seq, meta, gains, q_ref, k_ref, v_ref, scale_ref, heads)
    for m, out in enumerate(outs):
        out[...] = heads[meta[4] ^ m]


def send_wide_kernel(seq, outer, meta, gate_ref, up_ref, scale_ref, *refs):
    *outs, packed, wide = refs
    count = len(outs)
    piece = gate_ref.shape[1] // (outer * count * seq)
    local = outer * piece
    main = local - 64
    scale = scale_ref[...]
    for s_at in range(seq):

        @pl.when(meta[3] == s_at)
        def _():
            for i_at in range(count):
                for side, source in enumerate((gate_ref, up_ref)):
                    for o_at in range(outer):
                        at = ((o_at * count + i_at) * seq + s_at) * piece
                        wide[side, :, o_at * piece : (o_at + 1) * piece] = (
                            source[:, at : at + piece].astype(F32) * scale
                        )
                packed[i_at, :, :main] = wide[0, :, :main].astype(BF16)
                packed[i_at, :, main : main + 128] = jnp.concatenate(
                    [wide[0, :, main:], wide[1, :, main:]], axis=1
                ).astype(BF16)
                packed[i_at, :, main + 128 :] = wide[1, :, :main].astype(BF16)

    for m, out in enumerate(outs):
        out[...] = packed[meta[4] ^ m]


def unpack_wide_kernel(outer, got_ref, gate_w, up_w, scale_ref, gate_ref, up_ref, gain_ref):
    ranks, rows = got_ref.shape[0], got_ref.shape[1]
    local = got_ref.shape[2] // 2
    piece, main = local // outer, local - 64
    for rank in range(ranks):
        got = got_ref[rank].astype(F32)
        up = jnp.concatenate([got[:, local + 64 :], got[:, local : local + 64]], axis=1)
        for value, out in ((got[:, :local], gate_ref), (up, up_ref)):
            for o_at in range(outer):
                at = (o_at * ranks + rank) * piece
                out[:, at : at + piece] = value[:, o_at * piece : (o_at + 1) * piece]
    scale = scale_ref[...]
    total = jnp.zeros((rows, 1), F32)
    for weight, out in ((gate_w, gate_ref), (up_w, up_ref)):
        raw = out[...]
        total = total + jnp.sum(raw * weight[...].astype(F32), axis=1, keepdims=True)
        out[...] = raw * scale
    gain_ref[...] = jnp.broadcast_to(total, gain_ref.shape)


def owners_kernel(
    kv_head, seq, per, meta, got_ref, q_w, k_w, v_w, scale_ref, q_ref, k_ref, v_ref, gain_ref, head_ref
):
    ranks, rows = got_ref.shape[0], q_w.shape[0]
    scale = scale_ref[...]
    total = jnp.zeros((rows, 1), F32)
    sums = jnp.zeros((16, 256), F32)
    low = lax.broadcasted_iota(jnp.int32, (rows, 128), 1) < 64
    back = {}
    for rank in range(ranks):
        t = kv_head(rank // seq, rank % seq)
        there = slice(128 * t, 128 * t + 128)
        part = got_ref[rank, :rows, :128].astype(F32)
        total = total + jnp.sum(part * q_w[:, there].astype(F32), axis=1, keepdims=True)
        q_ref[:, there] = part * scale
        back[t] = got_ref[rank, :rows, 128:].astype(F32)
        sums = sums + got_ref[rank, rows:, :].astype(F32)
    for t in range(0, ranks, 2):
        there = slice(64 * t, 64 * t + 128)
        key = jnp.where(low, back[t], pltpu.roll(back[t + 1], 64, 1))
        value = jnp.where(low, pltpu.roll(back[t], 64, 1), back[t + 1])
        for part, weight, out in ((key, k_w, k_ref), (value, v_w, v_ref)):
            total = total + jnp.sum(part * weight[:, there].astype(F32), axis=1, keepdims=True)
            out[:, there] = part * scale
    gain_ref[...] = jnp.broadcast_to(total, gain_ref.shape)
    row = sums[0:1, :128]
    row = row + pltpu.roll(row, 64, 1)
    row = jnp.concatenate([row, sums[0:1, 128:]], axis=1)
    lane = lax.broadcasted_iota(jnp.int32, (8, 128), 1)
    out = jnp.zeros((8, 128), F32)
    for j in range(per):
        here = lax.broadcasted_iota(jnp.int32, (1, 256), 1) % 128 == meta[2] * per + j
        picked = jnp.where(here, row, 0.0)
        q_j = jnp.sum(picked[:, :128], axis=1, keepdims=True)
        k_j = jnp.sum(picked[:, 128:], axis=1, keepdims=True)
        out = jnp.where(lane == j, q_j, out)
        out = jnp.where(lane == 64 + j, k_j, out)
    head_ref[...] = out


def prepare_kernel(meta, *refs):
    blocks, refs = refs[:GROUP], refs[GROUP:]
    sources = refs[:-10]
    cos_ref, sin_ref, q_ref, kv_ref, tail_ref, lin_ref, all_ref, w_ref, gain_ref, sems = refs[-10:]
    rows = all_ref.shape[0] // GROUP
    copies = block_copies(blocks, [all_ref.at[pl.ds(k * rows, rows)] for k in range(GROUP)], sems)
    for copy in copies:
        copy.start()
    gains = jnp.zeros((1, 256), F32)
    for m, source in enumerate(sources):
        parts, k_rows = source.shape[0], source.shape[1] - 16
        at = pl.multiple_of((meta[5] ^ m) * (parts * k_rows), parts * k_rows & -(parts * k_rows))
        if len(sources) == 1:
            at = 0
        w_ref[pl.ds(at, parts * k_rows), :] = source[:, :k_rows, :].reshape(parts * k_rows, 256)
        gains = gains + jnp.sum(source[:, k_rows:, :].astype(F32), axis=0)[0:1]
    gain_ref[...] = jnp.broadcast_to(gains, gain_ref.shape)
    weights = w_ref[...]
    lane = lax.broadcasted_iota(jnp.int32, (rows, 128), 1)
    low = lane < 64

    @pl.loop(0, GROUP)
    def _(k):
        at = pl.ds(pl.multiple_of((meta[0] ^ k) * rows, rows & -rows), rows)
        at_step(k, copies, lambda copy: copy.wait())
        lin = nn(all_ref[pl.ds(pl.multiple_of(k * rows, rows & -rows), rows), :], weights)
        lin_ref[at, :] = lin
        cosine, sine = cos_ref[at, :], sin_ref[at, :]
        front, back = lin[:, :128], lin[:, 128:]
        head = front * lax.rsqrt(head_sum(front * front, low) * (1 / 64) + EPS) * gains[:, :128]
        head = (head * cosine + rotated(head, lane) * sine) * (HEAD_SIZE**-0.5)
        q_ref[0, at, :] = jnp.where(low, head, 0.0).astype(BF16)
        q_ref[1, at, :] = jnp.where(low, pltpu.roll(head, 64, 1), 0.0).astype(BF16)
        key = back * lax.rsqrt(head_sum(back * back, low) * (1 / 64) + EPS) * gains[:, 128:]
        key = key * cosine + rotated(key, lane) * sine
        kv_ref[at, :] = jnp.where(low, key, back).astype(BF16)
    tail_ref[...] = kv_ref[kv_ref.shape[0] - tail_ref.shape[0] :, :]


def query_bounds(lengths, first, count):
    lane = lax.broadcasted_iota(jnp.int32, (1, 2 * count), 1)
    place = first + jnp.where(lane >= count, lane - count, lane)
    start = jnp.zeros((1, 2 * count), jnp.int32)
    begin, lowest = jnp.int32(0), jnp.int32(0)
    for d in range(lengths.shape[0]):
        start = jnp.where(place >= begin, begin, start)
        lowest = jnp.where(first >= begin, begin, lowest)
        begin = begin + lengths[d]
    return place, start, lowest


def fill_keys(parts, keys_ref):
    @pl.when(pl.program_id(0) == 0)
    def _():
        at = 0
        for part in parts:
            keys_ref[at : at + part.shape[0], :] = part[...]
            at += part.shape[0]


def attend_kernel(halo, span, meta, lengths, q_ref, *refs):
    *parts, out_ref, log_ref, kv_ref = refs
    step = pl.program_id(0)
    base = meta[1] - halo
    fill_keys(parts, kv_ref)
    place, start, lowest = query_bounds(lengths, meta[1] + step * span, span)
    queries = q_ref[...].reshape(2 * span, 128)
    iota = lax.broadcasted_iota(jnp.int32, (span, 2 * span), 0)
    first = jnp.maximum(lowest - base, 0) // span

    def body(at, carry):
        total, mixed = carry
        offset = pl.multiple_of(at * span, span)
        keys = kv_ref[pl.ds(offset, span), :]
        score = nt(keys, queries)
        moved = base + offset
        weight = jnp.where((iota >= start - moved) & (iota <= place - moved), jnp.exp(score), 0.0)
        total = total + jnp.sum(weight, axis=0, keepdims=True)
        mixed = mixed + tn(keys, weight.astype(BF16))
        return total, mixed

    total, mixed = lax.fori_loop(
        first,
        step + halo // span + 1,
        body,
        (jnp.zeros((1, 2 * span), F32), jnp.zeros((128, 2 * span), F32)),
    )
    mixed = mixed * (1.0 / total)
    side = jnp.concatenate([mixed[64:, :span], mixed[64:, span:]], axis=0)
    out_ref[...] = side.T.astype(BF16)
    log_ref[...] = jnp.broadcast_to(jnp.log(total), (8, 2 * span))


def attend_back_kernel(halo, span, meta, lengths, q_ref, *refs):
    *parts, grad_ref, out_ref, log_ref, dq_ref, early_ref, own_ref, kv_ref, dkv_ref = refs
    step = pl.program_id(0)
    base = meta[1] - halo
    fill_keys(parts, kv_ref)

    @pl.when(step == 0)
    def _():
        dkv_ref[...] = jnp.zeros_like(dkv_ref)

    place, start, lowest = query_bounds(lengths, meta[1] + step * span, span)
    queries = q_ref[...].reshape(2 * span, 128)
    grad = grad_ref[...].astype(F32)
    low = lax.broadcasted_iota(jnp.int32, (span, 128), 1) < 64
    grads = jnp.concatenate(
        [jnp.where(low, 0.0, pltpu.roll(grad, 64, 1)), jnp.where(low, 0.0, grad)], axis=0
    ).astype(BF16)
    both = (grad * out_ref[...].astype(F32)).T
    row_sum = jnp.concatenate(
        [jnp.sum(both[:64], axis=0, keepdims=True), jnp.sum(both[64:], axis=0, keepdims=True)],
        axis=1,
    )
    logs = log_ref[0:1, :]
    iota = lax.broadcasted_iota(jnp.int32, (span, 2 * span), 0)
    first = jnp.maximum(lowest - base, 0) // span

    def body(at, dq):
        offset = pl.multiple_of(at * span, span)
        keys = kv_ref[pl.ds(offset, span), :]
        moved = base + offset
        weight = jnp.where(
            (iota >= start - moved) & (iota <= place - moved),
            jnp.exp(nt(keys, queries) - logs),
            0.0,
        )
        d_score = (weight * (nt(keys, grads) - row_sum)).astype(BF16)
        dkv_ref[pl.ds(offset, span), :] += nn(d_score, queries) + nn(weight.astype(BF16), grads)
        return dq + tn(keys, d_score)

    dq = lax.fori_loop(
        first, step + halo // span + 1, body, jnp.zeros((128, 2 * span), F32)
    ) * (HEAD_SIZE**-0.5)
    dq_ref[...] = jnp.concatenate([dq[:64, :span], dq[:64, span:]], axis=0).T.astype(BF16)

    @pl.when(step == pl.num_programs(0) - 1)
    def _():
        early_ref[...] = dkv_ref[:halo, :].astype(BF16)
        own_ref[...] = dkv_ref[halo:, :]


def block_copies(sources, targets, sems):
    return [pltpu.make_async_copy(*pair, sems.at[n]) for n, pair in enumerate(zip(sources, targets))]


def at_step(step, copies, act):
    for n, copy in enumerate(copies):

        @pl.when(step == n)
        def _():
            act(copy)


def project_kernel(meta, att_ref, w_ref, *refs):
    *outs, held, sems = refs
    rows = held.shape[1]
    copies = block_copies([held.at[k] for k in range(GROUP)], outs, sems)

    @pl.loop(0, GROUP)
    def _(k):
        at = pl.ds(pl.multiple_of((meta[0] ^ k) * rows, rows & -rows), rows)
        held[k] = nn(att_ref[at, :], w_ref[...]).astype(BF16)
        at_step(k, copies, lambda copy: copy.start())

    for copy in copies:
        copy.wait()


def unproject_kernel(meta, *refs):
    blocks, refs = refs[:GROUP], refs[GROUP:]
    unproject_body(meta, blocks, *refs)


def unproject_into_kernel(meta, *refs):
    blocks, refs = refs[:GROUP], refs[GROUP:]
    w_ref, att_ref, _, out_ref, rest_ref, grad_ref, spot_ref, sem, held, sems = refs
    unproject_body(meta, blocks, w_ref, att_ref, out_ref, grad_ref, held, sems)
    o_rows = spot_ref.shape[2]
    spot_ref[...] = jnp.zeros_like(spot_ref)
    for n in range(2):
        spot_ref[2 * meta[3] + meta[4] % 2, n] = grad_ref[n * o_rows : (n + 1) * o_rows, :]
    copy = pltpu.make_async_copy(
        spot_ref, rest_ref.at[:, :, pl.ds(rest_ref.shape[2] - o_rows, o_rows)], sem
    )
    copy.start()
    copy.wait()


def unproject_body(meta, blocks, w_ref, att_ref, out_ref, grad_ref, held, sems):
    rows = held.shape[1]
    copies = block_copies(blocks, [held.at[k] for k in range(GROUP)], sems)
    for copy in copies:
        copy.start()

    def body(k, total):
        at_step(k, copies, lambda copy: copy.wait())
        at = pl.ds(pl.multiple_of((meta[0] ^ k) * rows, rows & -rows), rows)
        own = held[k]
        out_ref[at, :] = nt(own, w_ref[...]).astype(BF16)
        return total + tn(att_ref[at, :], own)

    grad_ref[...] = lax.fori_loop(
        0, GROUP, body, jnp.zeros(grad_ref.shape, F32)
    ).astype(BF16)


def finish_kernel(meta, dq_ref, own_ref, *refs):
    *backs, lin_ref, cos_ref, sin_ref, w_ref, gains_ref = refs[: -GROUP - 6]
    hidden = refs[-GROUP - 6 : -6]
    dlin_ref, gain_ref, dkv_ref, held_ref, hidden_held, sems = refs[-6:]
    dkv_ref[...] = own_ref[...]
    for back in backs:
        dkv_ref[dkv_ref.shape[0] - back.shape[0] :, :] += back[...].astype(F32)
    weights, gains = w_ref[...], gains_ref[0:1, :]
    rows = hidden_held.shape[1]
    lane = lax.broadcasted_iota(jnp.int32, (rows, 128), 1)
    low = lane < 64

    def body(block, gain_sums):
        at = pl.ds(pl.multiple_of(block * rows, rows & -rows), rows)
        cosine, sine = cos_ref[at, :], sin_ref[at, :]
        parts, sums = [], []
        for side, source in enumerate((dq_ref, dkv_ref)):
            lin = lin_ref[at, 128 * side : 128 * side + 128]
            factor = lax.rsqrt(head_sum(lin * lin, low) * (1 / 64) + EPS)
            plain = lin * factor
            given = source[at, :].astype(BF16).astype(F32)
            turned = given * cosine - rotated(given, lane) * sine
            sums.append(gain_sums[side] + jnp.sum(turned * plain, axis=0, keepdims=True))
            scaled = turned * gains[:, 128 * side : 128 * side + 128]
            grad = factor * (scaled - plain * (head_sum(scaled * plain, low) * (1 / 64)))
            parts.append(jnp.where(low, grad, given) if side else grad)
        held_ref[at, :] = jnp.concatenate(parts, axis=1).astype(BF16)
        return tuple(sums)

    gain_sums = lax.fori_loop(0, GROUP, body, (jnp.zeros((1, 128), F32),) * 2)
    copies = block_copies([hidden_held.at[k] for k in range(GROUP)], hidden, sems)

    @pl.loop(0, GROUP)
    def _(k):
        dlin = held_ref[pl.ds(pl.multiple_of((meta[0] ^ k) * rows, rows & -rows), rows), :]
        dlin_ref[pl.ds(pl.multiple_of(k * rows, rows & -rows), rows), :] = dlin
        hidden_held[k] = nt(dlin, weights).astype(BF16)
        at_step(k, copies, lambda copy: copy.start())

    for copy in copies:
        copy.wait()
    gain_ref[...] = jnp.broadcast_to(jnp.concatenate(gain_sums, axis=1), gain_ref.shape)


def project_grad_kernel(meta, n_ref, d_ref, gain_ref, *refs):
    *outs, grad_ref = refs
    parts, rows = outs[0].shape[0], outs[0].shape[1] - 16
    grad_ref[...] = tn(n_ref[...], d_ref[...]).astype(BF16)
    extra = jnp.where(
        lax.broadcasted_iota(jnp.int32, (16, 256), 0) == 0, gain_ref[0:1, :], 0.0
    ).astype(BF16)
    for m, out in enumerate(outs):
        first = (meta[5] ^ m) * (parts * rows) if len(outs) > 1 else 0
        for part in range(parts):
            at = first + part * rows
            if len(outs) > 1:
                at = pl.multiple_of(at, rows)
            out[part, :rows, :] = grad_ref[pl.ds(at, rows), :]
            out[part, rows:, :] = extra


def spread_sum_kernel(seq, *refs):
    *parts, out_ref = refs
    for i_at in range(parts[0].shape[0]):
        total = parts[0][i_at].astype(F32)
        for part in parts[1:]:
            total = total + part[i_at].astype(F32)
        total = total.astype(BF16)
        for s_at in range(seq):
            out_ref[i_at * seq + s_at] = total


def arrange_heads_kernel(meta, *refs):
    *pieces, out_ref = refs
    for m, piece in enumerate(pieces):
        for o_at in range(out_ref.shape[0]):
            out_ref[o_at, meta[4] ^ m] = piece[...]


def arrange_wide_kernel(meta, *refs):
    *pieces, out_ref = refs
    for m, piece in enumerate(pieces):
        out_ref[meta[4] ^ m] = piece[...]


def wide_grad_kernel(h_ref, d_ref, out_ref):
    chunk = out_ref.shape[2]

    @pl.loop(0, 2)
    def _(n):
        @pl.loop(0, out_ref.shape[0])
        def _(o_at):
            at = pl.ds(pl.multiple_of(o_at * chunk, chunk), chunk)
            out_ref[o_at, n] = tn(h_ref[:, at], d_ref[n]).astype(BF16)


def down_grad_kernel(rows, inner_ref, c_ref, out_ref):
    @pl.loop(0, 2)
    def _(n):
        grad = tn(inner_ref[n], c_ref[...]).astype(BF16)
        for o_at in range(out_ref.shape[0]):
            out_ref[o_at, n, :rows, :] = grad[o_at * rows : (o_at + 1) * rows]


def rest_out_kernel(meta, mine_ref, other_ref, down_ref, out_ref):
    rows = down_ref.shape[0] // 2
    mine, other = mine_ref[...].astype(F32), other_ref[...].astype(F32)
    out_ref[...] = mine[rows:] + other[rows:]
    first = meta[3] == 0
    down_ref[:rows, :] = jnp.where(first, mine[:rows], other[:rows])
    down_ref[rows:, :] = jnp.where(first, other[:rows], mine[:rows])


def near_kernel(*refs):
    for mine, far, out in zip(refs[:4], refs[4:8], refs[8:]):
        out[...] = (mine[...].astype(F32) + far[...].astype(F32)).astype(out.dtype)


def total_of(refs):
    total = refs[0][...].astype(F32)
    for ref in refs[1:]:
        total = total + ref[...].astype(F32)
    return total


def middle_kernel(*refs):
    *parts, middle_ref, plain_ref = refs
    middle = total_of(parts)
    middle_ref[...] = middle
    plain_ref[...] = normalized(middle)[0].astype(BF16)


def back_norm_kernel(*refs):
    source_ref, base_ref, *parts, full_ref, low_ref = refs
    plain, factor = normalized(source_ref[...].astype(F32))
    total = base_ref[...].astype(F32) + norm_back(total_of(parts), plain, factor)
    full_ref[...] = total
    low_ref[...] = total.astype(BF16)


def feed_kernel(count, down_rows, *refs):
    hs, cs, (wgu_in, wd_in), refs = refs[:count], refs[count : 2 * count], refs[2 * count :][:2], refs
    wgu_held, wd_held, total, sems = refs[-4:]
    fed_out, two_out = refs[-8 - 2 * count : -8 - count], refs[-8 - count : -8]
    h_ref, c_ref, dgu_ref, inner_ref = refs[-8:-4]
    up_rows = wgu_in.shape[2]

    def copies(part, n):
        source, target, step = (
            (wgu_in, wgu_held, up_rows),
            (wd_in, wd_held, down_rows),
        )[n]
        return [
            pltpu.make_async_copy(
                source.at[o_at, part, pl.ds(0, step)],
                target.at[part, pl.ds(o_at * step, step)],
                sems.at[2 * part + n, o_at],
            )
            for o_at in range(source.shape[0])
        ]

    for part in range(2):
        for n in range(2):
            for copy in copies(part, n):
                copy.start()
    deep = wd_held.shape[1]
    for part in range(2):
        wd_held[part, deep - 64 :, :] = jnp.zeros((64, wd_held.shape[2]), BF16)
    rows = hs[0].shape[0]
    hidden = jnp.concatenate([h[...] for h in hs], axis=0)
    cotangent = jnp.concatenate([c[...] for c in cs], axis=0)
    h_ref[...] = hidden
    c_ref[...] = cotangent
    main = wgu_in.shape[3] // 2 - 64
    low = lax.broadcasted_iota(jnp.int32, (count * rows, 128), 1) < 64

    def piece(gate, up, given):
        sigma = 1.0 / (1.0 + jnp.exp(-gate))
        act = gate * sigma
        return act * up, given * up * (sigma * (1.0 + gate * (1.0 - sigma))), given * act

    total[...] = jnp.zeros_like(total)

    @pl.loop(0, 2)
    def _(part):
        wgu_ref, wd_ref = wgu_held.at[part], wd_held.at[part]
        for copy in copies(part, 0):
            copy.wait()
        both = nn(h_ref[...], wgu_ref[...])
        for copy in copies(part, 1):
            copy.wait()
        d_inner = nt(c_ref[...], wd_ref[...])
        tile = both[:, main : main + 128]
        inner_m, dg_m, du_m = piece(both[:, :main], both[:, main + 128 :], d_inner[:, :main])
        inner_t, dg_t, du_t = piece(tile, pltpu.roll(tile, 64, 1), d_inner[:, main:])
        inner = jnp.concatenate([inner_m, jnp.where(low, inner_t, 0.0)], axis=1).astype(BF16)
        d_tile = jnp.where(low, dg_t, pltpu.roll(du_t, 64, 1))
        dgu = jnp.concatenate([dg_m, d_tile, du_m], axis=1).astype(BF16)
        dgu_ref[part] = dgu
        inner_ref[part] = inner
        total[0] += nt(dgu, wgu_ref[...])
        total[1] += nn(inner, wd_ref[...])

    for n in range(count):
        two_out[n][...] = total[0, n * rows : (n + 1) * rows, :].astype(BF16)
        fed_out[n][...] = total[1, n * rows : (n + 1) * rows, :].astype(BF16)


def feed(at, hs, cs, weights, down_rows, whole, tokens):
    count = len(hs)
    rows, width = hs[0].shape
    wide = weights[0].shape[3]
    deep = wide // 2 + 64

    def full(dims):
        return pl.BlockSpec(dims, lambda j: (0,) * len(dims))

    outs = pl.pallas_call(
        functools.partial(feed_kernel, count, down_rows),
        grid=(1,),
        in_specs=[full((rows, width))] * (2 * count)
        + [pl.BlockSpec(memory_space=pl.ANY)] * (2 + len(whole)),
        out_specs=[full((rows, width))] * (2 * count)
        + [pl.BlockSpec((count * rows, width), lambda j: (at, 0))] * 2
        + [pl.BlockSpec((2, count * rows, w), lambda j: (0, at, 0)) for w in (wide, deep)],
        out_shape=[shape((rows, width), BF16)] * (2 * count)
        + [shape((tokens, width), BF16)] * 2
        + [shape((2, tokens, w), BF16) for w in (wide, deep)],
        scratch_shapes=[
            pltpu.VMEM((2, width, wide), BF16),
            pltpu.VMEM((2, deep, width), BF16),
            pltpu.VMEM((2, count * rows, width), F32),
            pltpu.SemaphoreType.DMA((4, max(w.shape[0] for w in weights))),
        ],
        input_output_aliases={2 * count + 2 + n: 2 * count + n for n in range(len(whole))},
        compiler_params=pltpu.CompilerParams(
            vmem_limit_bytes=VMEM_LIMIT, dimension_semantics=("arbitrary",)
        ),
        cost_estimate=pl.CostEstimate(
            flops=12 * count * rows * width * wide,
            bytes_accessed=2 * (3 * width * wide + 12 * count * rows * width),
            transcendentals=0,
        ),
        name="feed",
    )(*hs, *cs, *weights, *whole)
    return outs[:count], outs[count : 2 * count], outs[2 * count :]


def inner_swap(value, mask, count):
    return lax.ppermute(value, ("a", "b"), [(r, r ^ mask) for r in range(count)])


def outer_swap(value, mask, count):
    return lax.ppermute(value, "o", [(r, r ^ mask) for r in range(count)])


def swap(value, mask):
    return lax.ppermute(value, ("a", "b", "c"), [(r, r ^ mask) for r in range(GROUP)])


def after(value, *others):
    return lax.optimization_barrier((value, others))[0]


def gather_blocks(value, *others):
    blocks = {0: value}
    for k in (1, 4, 5):
        blocks[k] = swap(value, k)
    if others:
        blocks = after(blocks, *others)
    for k in (0, 1, 4, 5):
        blocks[k ^ 2] = swap(blocks[k], 2)
    return [blocks[k] for k in range(GROUP)]


def near_sums(parts, first=None):
    order = (0, 1, 4, 5)
    far = [swap(parts[k ^ 2], 2) for k in order]
    if first is not None:
        far = list(after(tuple(far), first))
    block = parts[0].shape
    near = call(
        near_kernel,
        [shape(block, F32)] + [shape(block, BF16)] * 3,
        0,
        [*[parts[k] for k in order], *far],
        0,
        "near",
    )
    return [near[0]] + [swap(near[n], order[n]) for n in (1, 2, 3)]


def normalized(values):
    factor = lax.rsqrt(jnp.mean(values * values, axis=-1, keepdims=True) + EPS)
    return values * factor, factor


def norm_back(grad, plain, factor):
    return factor * (grad - plain * jnp.mean(grad * plain, axis=-1, keepdims=True))


def on_device(
    inner_count,
    stream,
    cotangent,
    doc_lengths,
    attention_gain,
    query_weight,
    key_matrix,
    value_matrix,
    query_gain,
    key_gain,
    output_weight,
    feedforward_gain,
    gate_weight,
    up_weight,
    down_weight,
):
    rows, width = stream.shape
    outer, seq = lax.axis_size("o"), GROUP // inner_count
    o = lax.axis_index("o")
    if inner_count == 1:
        i, s = jnp.int32(0), lax.axis_index(("a", "b", "c"))
    else:
        i, s = lax.axis_index(("a", "b")), lax.axis_index("c")
    shards = outer * inner_count
    me = i * seq + s
    tokens = GROUP * rows
    block = rows * seq
    lookback = max(2, -(-DOC_MIN // block))
    halo = lookback * block
    span = 2 * rows
    k_rows = query_weight.shape[0]
    o_rows = output_weight.shape[0]
    ff_rows = down_weight.shape[0] // seq
    ff_local = outer * ff_rows
    main = ff_local - 64
    few = outer <= 4

    def kv_head(i_at, s_at):
        if inner_count == 1:
            return s_at
        return 4 * s_at + 2 * (i_at % 2) + i_at // 2

    shard = o * inner_count + i
    per = query_gain.shape[0]
    meta = jnp.stack([me, o * tokens, shard, s, i, o]).astype(jnp.int32)
    lengths = doc_lengths.astype(jnp.int32)
    gain_one = attention_gain.astype(F32)[:, None]
    gain_two = feedforward_gain.astype(F32)[:, None]
    head_gains = jnp.concatenate([query_gain, key_gain]).astype(F32)

    heads_in = [query_weight, key_matrix, value_matrix, gain_one]
    heads_shape = (inner_count, k_rows + 16, 256)
    chips = ("o", "b")
    if inner_count > 1:
        sent = call(
            functools.partial(send_heads_kernel, kv_head, seq),
            [shape(heads_shape[1:], BF16)] * inner_count,
            2,
            [meta, head_gains, *heads_in],
            0,
            "send_heads",
            [pltpu.VMEM(heads_shape, BF16)],
        )
        (packed,) = call(
            arrange_heads_kernel,
            [shape((outer, *heads_shape), BF16)],
            1,
            [meta, sent[0]] + [inner_swap(sent[m], m, inner_count) for m in range(1, inner_count)],
            0,
            "arrange_heads",
        )
        n_blocks = gather_blocks(normalized(after(stream, packed).astype(F32))[0].astype(BF16))
        w_heads = lax.all_to_all(packed, "o", split_axis=0, concat_axis=0, tiled=True)
        wide_in = after((gate_weight, up_weight), packed)
        sent = call(
            functools.partial(send_wide_kernel, seq, outer),
            [shape((k_rows, 2 * ff_local), BF16)] * inner_count,
            1,
            [meta, *wide_in, gain_two],
            0,
            "send_wide",
            [
                pltpu.VMEM((inner_count, k_rows, 2 * ff_local), BF16),
                pltpu.VMEM((2, k_rows, ff_local), F32),
            ],
        )
        (packed_gu,) = call(
            arrange_wide_kernel,
            [shape((inner_count, k_rows, 2 * ff_local), BF16)],
            1,
            [meta, sent[0]] + [inner_swap(sent[m], m, inner_count) for m in range(1, inner_count)],
            0,
            "arrange_wide",
        )
        half_down = lax.dynamic_slice_in_dim(down_weight, s * ff_rows, ff_rows, 0)
        w_rest = lax.all_gather(jnp.concatenate([half_down, output_weight]), chips, axis=0)
        w_rest = w_rest.reshape(outer, 2, ff_rows + o_rows, width)
        down_rows, w_down = ff_rows, w_rest
        w_out = lax.dynamic_index_in_dim(w_rest, 2 * s + i % 2, 0, keepdims=False)
        w_out = w_out[:, ff_rows:].reshape(128, width)
    else:
        (packed,) = call(
            functools.partial(pack_heads_kernel, kv_head, seq),
            [shape(heads_shape, BF16)],
            2,
            [meta, head_gains, *heads_in],
            0,
            "pack_heads",
        )

        def columns(weight):
            scaled = (weight.astype(F32) * gain_two).astype(BF16)
            split = scaled.reshape(k_rows, outer, seq, ff_rows)
            return lax.dynamic_index_in_dim(split, s, 2, keepdims=False).reshape(k_rows, ff_local)

        gate_c, up_c = columns(gate_weight), columns(up_weight)
        packed_gu = jnp.concatenate(
            [gate_c[:, :main], gate_c[:, main:], up_c[:, main:], up_c[:, :main]], axis=1
        )
        half_down = lax.dynamic_slice_in_dim(down_weight, s * ff_rows, ff_rows, 0)
        w_down = lax.all_gather(half_down, chips, axis=0).reshape(outer, 2, ff_rows, width)
        w_down = w_down.transpose(1, 0, 2, 3).reshape(1, 2, ff_local, width)
        down_rows = ff_local
        n_blocks = gather_blocks(normalized(stream.astype(F32))[0].astype(BF16))
        w_heads = lax.all_gather(packed, "o", axis=0)
        w_out = lax.all_gather(output_weight, "o", axis=0, tiled=True)
        w_out = lax.dynamic_slice_in_dim(w_out, s * 128, 128, 0)
    w_heads = w_heads.reshape(shards, k_rows + 16, 256)
    starts = jnp.cumsum(lengths) - lengths
    places = o * tokens + jnp.arange(tokens, dtype=jnp.int32)
    begin = jnp.max(jnp.where(starts[None, :] <= places[:, None], starts[None, :], -1), axis=1)
    half = HEAD_SIZE // 2
    freq = jnp.power(THETA, -(jnp.arange(half, dtype=F32) * (2.0 / HEAD_SIZE)))
    angle = (places - begin).astype(F32)[:, None] * freq[None, :]
    cosine = jnp.tile(jnp.cos(angle), (1, 4))
    sine = jnp.tile(jnp.sin(angle), (1, 4))

    own_c = after(cotangent, n_blocks[5])
    c_blocks = {0: own_c, 1: swap(own_c, 1), 4: swap(own_c, 4), 5: swap(own_c, 5)}
    hops = -(-halo // tokens)
    blocks_scratch = [
        pltpu.VMEM((GROUP, rows, width), BF16),
        pltpu.SemaphoreType.DMA((GROUP,)),
    ]
    tail_rows = halo - (hops - 1) * tokens
    queries, kv, tail, lin, n_all, w_qkv, head_row = call(
        prepare_kernel,
        [
            shape((2, tokens, 128), BF16),
            shape((tokens, 128), BF16),
            shape((tail_rows, 128), BF16),
            shape((tokens, 256), F32),
            shape((tokens, width), BF16),
            shape((width, 256), BF16),
            shape((8, 256), F32),
        ],
        1,
        [meta, *n_blocks, w_heads, cosine, sine],
        2 * tokens * width * 256,
        "prepare",
        [pltpu.SemaphoreType.DMA((GROUP,))],
        far_in=range(1, GROUP + 1),
    )
    w_gu = lax.all_gather(
        packed_gu.reshape(inner_count * k_rows, 2 * ff_local), chips, axis=0
    ).reshape(outer, 2, inner_count * k_rows, 2 * ff_local)

    keys = [
        lax.ppermute(
            tail if hop == hops else kv, "o", [(at, at + hop) for at in range(max(0, outer - hop))]
        )
        for hop in range(hops, 0, -1)
    ] + [kv]
    steps = tokens // span
    reach = halo + tokens
    pair_flops = 4 * tokens * (span + halo // 2) * 128

    def attention(kernel, ins, outs, scratch, flops, name):
        return pl.pallas_call(
            functools.partial(kernel, halo, span),
            grid=(steps,),
            in_specs=[SM, SM] + [spec for _, spec in ins],
            out_specs=[spec for _, spec in outs],
            out_shape=[dims for dims, _ in outs],
            scratch_shapes=scratch,
            compiler_params=pltpu.CompilerParams(
                vmem_limit_bytes=VMEM_LIMIT, dimension_semantics=("arbitrary",)
            ),
            cost_estimate=pl.CostEstimate(
                flops=flops, bytes_accessed=4 * reach * 256, transcendentals=0
            ),
            name=name,
        )(meta, lengths, *[value for value, _ in ins])

    def still(value):
        return pl.BlockSpec(value.shape, lambda j: (0, 0))

    q_spec = pl.BlockSpec((2, span, 128), lambda j: (0, j, 0))
    row_spec = pl.BlockSpec((span, 128), lambda j: (j, 0))
    log_spec = pl.BlockSpec((8, 2 * span), lambda j: (j, 0))
    key_ins = [(part, still(part)) for part in keys]
    attended, logs = attention(
        attend_kernel,
        [(queries, q_spec), *key_ins],
        [
            (shape((tokens, 128), BF16), row_spec),
            (shape((8 * steps, 2 * span), F32), log_spec),
        ],
        [pltpu.VMEM((reach, 128), BF16)],
        pair_flops,
        "attend",
    )

    attended = after(attended, tuple(c_blocks.values()))
    parts = call(
        project_kernel,
        [shape((rows, width), BF16)] * GROUP,
        1,
        [meta, attended, w_out],
        2 * tokens * 128 * width,
        "project",
        blocks_scratch,
        far_out=range(GROUP),
    )
    near_parts = near_sums(parts)
    middle, plain_two = call(
        middle_kernel,
        [shape((rows, width), F32), shape((rows, width), BF16)],
        0,
        [stream, *near_parts],
        0,
        "middle",
    )

    h_blocks = {0: plain_two}
    for k in (1, 4, 5):
        h_blocks[k] = swap(h_blocks[0], k)
    fed, two, whole = {}, {}, []
    for at, ks in ((2, (0,)), (0, (1, 4)), (3, (5,))):
        fed_k, two_k, whole = feed(
            at,
            [h_blocks[k] for k in ks],
            [c_blocks[k] for k in ks],
            [w_gu, w_down],
            down_rows,
            whole,
            4 * rows,
        )
        for n, k in enumerate(ks):
            fed[k], two[k] = fed_k[n], two_k[n]
    h_all, c_all, dgu_all, inner_all = whole

    def from_chips(parts):
        return [parts[0]] + [swap(parts[k], k) for k in (1, 4, 5)]

    d_mid_f, d_mid = call(
        back_norm_kernel,
        [shape((rows, width), F32), shape((rows, width), BF16)],
        0,
        [middle, cotangent, *from_chips(two)],
        0,
        "back_two",
    )
    if inner_count > 1:
        (grad_gu,) = call(
            wide_grad_kernel,
            [shape((outer, 2, inner_count * k_rows, 2 * ff_local), BF16)],
            0,
            [h_all, dgu_all],
            0,
            "wide_grad",
        )
        grad_gu = after(grad_gu, d_mid).reshape(-1, 2 * ff_local)
        grad_gu = lax.psum_scatter(grad_gu, chips, scatter_dimension=0, tiled=True)
        grad_gu = grad_gu.reshape(inner_count, k_rows, 2 * ff_local)
        (grad_rest,) = call(
            functools.partial(down_grad_kernel, ff_rows),
            [shape((outer, 2, ff_rows + o_rows, width), BF16)],
            0,
            [inner_all, c_all],
            0,
            "down_grad",
        )
        m_blocks = gather_blocks(d_mid, grad_rest)
        d_attended, grad_rest = pl.pallas_call(
            unproject_into_kernel,
            in_specs=[SM] + [FAR] * GROUP + [VM, VM, FAR],
            out_specs=[VM, FAR],
            out_shape=[shape((tokens, 128), BF16), shape(grad_rest.shape, BF16)],
            scratch_shapes=[
                pltpu.VMEM((128, width), BF16),
                pltpu.VMEM((outer, 2, o_rows, width), BF16),
                pltpu.SemaphoreType.DMA(()),
                *blocks_scratch,
            ],
            input_output_aliases={GROUP + 3: 1},
            compiler_params=pltpu.CompilerParams(vmem_limit_bytes=VMEM_LIMIT),
            cost_estimate=pl.CostEstimate(
                flops=4 * tokens * 128 * width, bytes_accessed=8 << 20, transcendentals=0
            ),
            name="unproject",
        )(meta, *m_blocks, w_out, attended, grad_rest)
        grad_rest = grad_rest.reshape(-1, width)
        grad_rest = lax.psum_scatter(grad_rest, chips, scatter_dimension=0, tiled=True)
        grad_down, grad_output = call(
            rest_out_kernel,
            [shape((seq * ff_rows, width), F32), shape((o_rows, width), F32)],
            1,
            [meta, grad_rest, swap(grad_rest, 1)],
            0,
            "rest_out",
        )
    else:
        m_blocks = gather_blocks(d_mid)
        grad_gu = jnp.stack([tn(h_all, dgu_all[n]).astype(BF16) for n in range(2)])
        grad_gu = grad_gu.reshape(2, outer, k_rows, 2 * ff_local).transpose(1, 0, 2, 3)
        grad_gu = lax.psum_scatter(
            grad_gu.reshape(-1, 2 * ff_local), chips, scatter_dimension=0, tiled=True
        ).reshape(inner_count, k_rows, 2 * ff_local)
        d_attended, grad_out = call(
            unproject_kernel,
            [shape((tokens, 128), BF16), shape((128, width), BF16)],
            1,
            [meta, *m_blocks, w_out, attended],
            4 * tokens * 128 * width,
            "unproject",
            blocks_scratch,
            far_in=range(1, GROUP + 1),
        )
        grad_dn = jnp.stack([tn(inner_all[n], c_all)[:ff_local].astype(BF16) for n in range(2)])
        grad_dn = grad_dn.reshape(2, outer, ff_rows, width).transpose(1, 0, 2, 3)
        grad_dn = lax.psum_scatter(
            grad_dn.reshape(-1, width), chips, scatter_dimension=0, tiled=True
        )
        grad_down = lax.all_gather(grad_dn, ("a", "b", "c"), axis=0, tiled=True).astype(F32)
        spot = lax.dynamic_update_slice_in_dim(
            jnp.zeros((shards * o_rows, width), BF16), grad_out, s * 128, 0
        )
        spot = lax.psum_scatter(spot, "o", scatter_dimension=0, tiled=True)
        grad_output = lax.psum(spot, ("a", "b", "c")).astype(F32)

    def to_owners(value):
        value = jnp.repeat(value, seq, axis=0)
        return lax.all_to_all(value, ("a", "b", "c"), split_axis=0, concat_axis=0, tiled=True)

    got = to_owners(grad_gu)
    dq, d_early, d_own = attention(
        attend_back_kernel,
        [
            (queries, q_spec),
            *key_ins,
            (d_attended, row_spec),
            (attended, row_spec),
            (logs, log_spec),
        ],
        [
            (shape((tokens, 128), BF16), row_spec),
            (shape((halo, 128), BF16), pl.BlockSpec((halo, 128), lambda j: (0, 0))),
            (shape((tokens, 128), F32), pl.BlockSpec((tokens, 128), lambda j: (0, 0))),
        ],
        [pltpu.VMEM((reach, 128), BF16), pltpu.VMEM((reach, 128), F32)],
        3 * pair_flops,
        "attend_back",
    )
    late = dict(zip(fed, after(tuple(fed.values()), m_blocks)))
    result = middle
    for part in from_chips(late):
        result = result + part.astype(F32)
    result = result.astype(BF16)
    d_early = after(d_early, result)
    backs = []
    for at, hop in enumerate(range(hops, 0, -1)):
        begin_at = 0 if at == 0 else tail_rows + (at - 1) * tokens
        size = tail_rows if at == 0 else tokens
        backs.append(
            lax.ppermute(
                d_early[begin_at : begin_at + size],
                "o",
                [(p + hop, p) for p in range(max(0, outer - hop))],
            )
        )
    *hidden_parts, dlin, gain_part = call(
        finish_kernel,
        [shape((rows, width), BF16)] * GROUP + [shape((tokens, 256), BF16), shape((8, 256), F32)],
        1,
        [meta, dq, d_own, *backs, lin, cosine, sine, w_qkv, head_row],
        2 * tokens * width * 256,
        "finish",
        [pltpu.VMEM((tokens, 128), F32), pltpu.VMEM((tokens, 256), BF16), *blocks_scratch],
        far_out=range(GROUP),
    )
    pieces = outer if few else 1
    grad_p = call(
        project_grad_kernel,
        [shape((shards // pieces, k_rows + 16, 256), BF16)] * pieces,
        1,
        [meta, n_all, dlin, gain_part],
        2 * tokens * width * 256,
        "project_grad",
        [pltpu.VMEM((width, 256), BF16)],
    )
    near_h = near_sums(hidden_parts, grad_p)
    _, grad_stream = call(
        back_norm_kernel,
        [shape((rows, width), F32), shape((rows, width), BF16)],
        0,
        [stream, d_mid_f, *near_h],
        0,
        "back_one",
    )

    if inner_count > 1:
        grad_gate, grad_up, gain_sum = call(
            functools.partial(unpack_wide_kernel, outer),
            [shape((k_rows, GROUP * ff_local), F32)] * 2 + [shape((k_rows, 128), F32)],
            0,
            [got, gate_weight, up_weight, gain_two],
            0,
            "unpack_wide",
        )
        grad_feedforward_gain = gain_sum[:, 0]
    else:
        gu = got.astype(F32)

        def wide(value):
            split = value.reshape(inner_count, seq, k_rows, outer, ff_rows)
            return split.transpose(2, 3, 0, 1, 4).reshape(k_rows, -1)

        raw_gate = wide(gu[..., :ff_local])
        raw_up = wide(
            jnp.concatenate(
                [gu[..., ff_local + 64 :], gu[..., ff_local : ff_local + 64]], axis=-1
            )
        )
        grad_feedforward_gain = jnp.sum(
            raw_gate * gate_weight.astype(F32) + raw_up * up_weight.astype(F32), axis=1
        )
        grad_gate, grad_up = raw_gate * gain_two, raw_up * gain_two

    if few:
        grad_p = [grad_p[0]] + [outer_swap(grad_p[m], m, outer) for m in range(1, outer)]
        grad_p = after(grad_p, near_h[0], got)
        (total,) = call(
            functools.partial(spread_sum_kernel, seq),
            [shape((GROUP, k_rows + 16, 256), BF16)],
            0,
            grad_p,
            0,
            "spread_sum",
        )
        total = after(total, near_h[1:])
        owned = lax.all_to_all(total, ("a", "b", "c"), split_axis=0, concat_axis=0, tiled=True)
    else:
        owned = to_owners(lax.psum_scatter(grad_p[0], "o", scatter_dimension=0, tiled=True))
    grad_query, grad_key, grad_value, gain_sum, head_sums = call(
        functools.partial(owners_kernel, kv_head, seq, per),
        [
            shape(query_weight.shape, F32),
            shape(key_matrix.shape, F32),
            shape(value_matrix.shape, F32),
            shape((k_rows, 128), F32),
            shape((8, 128), F32),
        ],
        1,
        [meta, owned, query_weight, key_matrix, value_matrix, gain_one],
        0,
        "owners",
    )
    return (
        result,
        grad_stream,
        gain_sum[:, 0],
        grad_query,
        grad_key,
        grad_value,
        head_sums[0, :per],
        head_sums[0, 64 : 64 + per],
        grad_output,
        grad_feedforward_gain,
        grad_gate,
        grad_up,
        grad_down,
    )


def solution(mesh):
    fsdp, seq = mesh.shape["fsdp"], mesh.shape["seq"]
    inner = GROUP // seq
    split = Mesh(mesh.devices.reshape(fsdp // inner, 2, 2, 2), ("o", "a", "b", "c"))
    both = ("o", "a", "b") if inner > 1 else ("o",)
    tokens, matrix, vector = P(("o", "a", "b", "c"), None), P(both, None), P(both)
    placed = (
        tokens,
        tokens,
        P(),
        vector,
        matrix,
        matrix,
        matrix,
        vector,
        vector,
        matrix,
        vector,
        matrix,
        matrix,
        matrix,
    )
    return jax.shard_map(
        functools.partial(on_device, inner),
        mesh=split,
        in_specs=placed,
        out_specs=(
            tokens,
            tokens,
            vector,
            matrix,
            matrix,
            matrix,
            vector,
            vector,
            matrix,
            vector,
            matrix,
            matrix,
            matrix,
        ),
        check_vma=False,
    )
```

```python
import functools

import jax
import jax.numpy as jnp
from jax import lax
from jax.experimental import pallas as pl
from jax.experimental.pallas import tpu as pltpu
from jax.sharding import Mesh, PartitionSpec as P

QUERY_HEAD_COUNT = 16
KEY_VALUE_HEADS = 8
HEAD_SIZE = 64
DOC_MIN = 1024
EPS = 1e-05
THETA = 1000000.0
GROUP = 8
BF16 = jnp.bfloat16
F32 = jnp.float32
VMEM_LIMIT = 60 * 1024 * 1024

VM = pl.BlockSpec(memory_space=pltpu.VMEM)
SM = pl.BlockSpec(memory_space=pltpu.SMEM)
FAR = pl.BlockSpec(memory_space=pl.ANY)


def nn(left, right):
    return lax.dot_general(left, right, (((1,), (0,)), ((), ())), preferred_element_type=F32)


def nt(left, right):
    return lax.dot_general(left, right, (((1,), (1,)), ((), ())), preferred_element_type=F32)


def tn(left, right):
    return lax.dot_general(left, right, (((0,), (0,)), ((), ())), preferred_element_type=F32)


def call(kernel, outs, n_smem, args, flops, name, scratch=(), far_in=(), far_out=()):
    bytes_moved = sum(a.size * a.dtype.itemsize for a in args) + sum(
        o.size * o.dtype.itemsize for o in outs
    )
    return pl.pallas_call(
        kernel,
        out_shape=outs,
        in_specs=[
            SM if n < n_smem else FAR if n in far_in else VM for n in range(len(args))
        ],
        out_specs=[FAR if n in far_out else VM for n in range(len(outs))],
        scratch_shapes=list(scratch),
        compiler_params=pltpu.CompilerParams(vmem_limit_bytes=VMEM_LIMIT),
        cost_estimate=pl.CostEstimate(flops=flops, bytes_accessed=bytes_moved, transcendentals=0),
        name=name,
    )(*args)


def shape(dims, dtype):
    return jax.ShapeDtypeStruct(dims, dtype)


def rotated(x, lane):
    return jnp.where(lane % 64 < 32, -pltpu.roll(x, 96, 1), pltpu.roll(x, 32, 1))


def head_sum(x, low):
    first = jnp.sum(jnp.where(low, x, 0.0), axis=1, keepdims=True)
    second = jnp.sum(jnp.where(low, 0.0, x), axis=1, keepdims=True)
    return jnp.where(low, first, second)


def pack_heads_kernel(kv_head, seq, meta, gains, q_ref, k_ref, v_ref, scale_ref, out_ref):
    count, rows = out_ref.shape[0], q_ref.shape[0]
    per = gains.shape[0] // 2
    scale = scale_ref[...]
    lane = lax.broadcasted_iota(jnp.int32, (16, 256), 1)
    row = lax.broadcasted_iota(jnp.int32, (16, 256), 0)
    extra = jnp.zeros((16, 256), F32)
    for j in range(per):
        spot = (lane % 64 == meta[2] * per + j) & (row == 0)
        extra = jnp.where(spot & (lane < 128), gains[j], extra)
        extra = jnp.where(spot & (lane >= 128) & (lane < 192), gains[per + j], extra)
    extra = extra.astype(BF16)
    for s_at in range(seq):

        @pl.when(meta[3] == s_at)
        def _():
            for i_at in range(count):
                t = kv_head(i_at, s_at)
                out_ref[i_at, :rows, :128] = (
                    q_ref[:, 128 * t : 128 * t + 128].astype(F32) * scale
                ).astype(BF16)
                pair = 128 * (t // 2)
                key = k_ref[:, pair : pair + 128].astype(F32) * scale
                value = v_ref[:, pair : pair + 128].astype(F32) * scale
                if t % 2:
                    key = pltpu.roll(key, 64, 1)
                else:
                    value = pltpu.roll(value, 64, 1)
                low = lax.broadcasted_iota(jnp.int32, key.shape, 1) < 64
                out_ref[i_at, :rows, 128:] = jnp.where(low, key, value).astype(BF16)

    for i_at in range(count):
        out_ref[i_at, rows:, :] = extra


def send_heads_kernel(kv_head, seq, meta, gains, q_ref, k_ref, v_ref, scale_ref, *refs):
    *outs, heads = refs
    pack_heads_kernel(kv_head, seq, meta, gains, q_ref, k_ref, v_ref, scale_ref, heads)
    for m, out in enumerate(outs):
        out[...] = heads[meta[4] ^ m]


def send_wide_kernel(seq, outer, meta, gate_ref, up_ref, scale_ref, *refs):
    *outs, packed, wide = refs
    count = len(outs)
    piece = gate_ref.shape[1] // (outer * count * seq)
    local = outer * piece
    main = local - 64
    scale = scale_ref[...]
    for s_at in range(seq):

        @pl.when(meta[3] == s_at)
        def _():
            for i_at in range(count):
                for side, source in enumerate((gate_ref, up_ref)):
                    for o_at in range(outer):
                        at = ((o_at * count + i_at) * seq + s_at) * piece
                        wide[side, :, o_at * piece : (o_at + 1) * piece] = (
                            source[:, at : at + piece].astype(F32) * scale
                        )
                packed[i_at, :, :main] = wide[0, :, :main].astype(BF16)
                packed[i_at, :, main : main + 128] = jnp.concatenate(
                    [wide[0, :, main:], wide[1, :, main:]], axis=1
                ).astype(BF16)
                packed[i_at, :, main + 128 :] = wide[1, :, :main].astype(BF16)

    for m, out in enumerate(outs):
        out[...] = packed[meta[4] ^ m]


def unpack_wide_kernel(outer, got_ref, gate_w, up_w, scale_ref, gate_ref, up_ref, gain_ref):
    ranks, rows = got_ref.shape[0], got_ref.shape[1]
    local = got_ref.shape[2] // 2
    piece, main = local // outer, local - 64
    for rank in range(ranks):
        got = got_ref[rank].astype(F32)
        up = jnp.concatenate([got[:, local + 64 :], got[:, local : local + 64]], axis=1)
        for value, out in ((got[:, :local], gate_ref), (up, up_ref)):
            for o_at in range(outer):
                at = (o_at * ranks + rank) * piece
                out[:, at : at + piece] = value[:, o_at * piece : (o_at + 1) * piece]
    scale = scale_ref[...]
    total = jnp.zeros((rows, 1), F32)
    for weight, out in ((gate_w, gate_ref), (up_w, up_ref)):
        raw = out[...]
        total = total + jnp.sum(raw * weight[...].astype(F32), axis=1, keepdims=True)
        out[...] = raw * scale
    gain_ref[...] = jnp.broadcast_to(total, gain_ref.shape)


def owners_kernel(
    kv_head, seq, per, meta, got_ref, q_w, k_w, v_w, scale_ref, q_ref, k_ref, v_ref, gain_ref, head_ref
):
    ranks, rows = got_ref.shape[0], q_w.shape[0]
    scale = scale_ref[...]
    total = jnp.zeros((rows, 1), F32)
    sums = jnp.zeros((16, 256), F32)
    low = lax.broadcasted_iota(jnp.int32, (rows, 128), 1) < 64
    back = {}
    for rank in range(ranks):
        t = kv_head(rank // seq, rank % seq)
        there = slice(128 * t, 128 * t + 128)
        part = got_ref[rank, :rows, :128].astype(F32)
        total = total + jnp.sum(part * q_w[:, there].astype(F32), axis=1, keepdims=True)
        q_ref[:, there] = part * scale
        back[t] = got_ref[rank, :rows, 128:].astype(F32)
        sums = sums + got_ref[rank, rows:, :].astype(F32)
    for t in range(0, ranks, 2):
        there = slice(64 * t, 64 * t + 128)
        key = jnp.where(low, back[t], pltpu.roll(back[t + 1], 64, 1))
        value = jnp.where(low, pltpu.roll(back[t], 64, 1), back[t + 1])
        for part, weight, out in ((key, k_w, k_ref), (value, v_w, v_ref)):
            total = total + jnp.sum(part * weight[:, there].astype(F32), axis=1, keepdims=True)
            out[:, there] = part * scale
    gain_ref[...] = jnp.broadcast_to(total, gain_ref.shape)
    row = sums[0:1, :128]
    row = row + pltpu.roll(row, 64, 1)
    row = jnp.concatenate([row, sums[0:1, 128:]], axis=1)
    lane = lax.broadcasted_iota(jnp.int32, (8, 128), 1)
    out = jnp.zeros((8, 128), F32)
    for j in range(per):
        here = lax.broadcasted_iota(jnp.int32, (1, 256), 1) % 128 == meta[2] * per + j
        picked = jnp.where(here, row, 0.0)
        q_j = jnp.sum(picked[:, :128], axis=1, keepdims=True)
        k_j = jnp.sum(picked[:, 128:], axis=1, keepdims=True)
        out = jnp.where(lane == j, q_j, out)
        out = jnp.where(lane == 64 + j, k_j, out)
    head_ref[...] = out


def prepare_kernel(meta, *refs):
    blocks, refs = refs[:GROUP], refs[GROUP:]
    sources = refs[:-10]
    cos_ref, sin_ref, q_ref, kv_ref, tail_ref, lin_ref, all_ref, w_ref, gain_ref, sems = refs[-10:]
    rows = all_ref.shape[0] // GROUP
    copies = block_copies(blocks, [all_ref.at[pl.ds(k * rows, rows)] for k in range(GROUP)], sems)
    for copy in copies:
        copy.start()
    gains = jnp.zeros((1, 256), F32)
    for m, source in enumerate(sources):
        parts, k_rows = source.shape[0], source.shape[1] - 16
        at = pl.multiple_of((meta[5] ^ m) * (parts * k_rows), parts * k_rows & -(parts * k_rows))
        if len(sources) == 1:
            at = 0
        w_ref[pl.ds(at, parts * k_rows), :] = source[:, :k_rows, :].reshape(parts * k_rows, 256)
        gains = gains + jnp.sum(source[:, k_rows:, :].astype(F32), axis=0)[0:1]
    gain_ref[...] = jnp.broadcast_to(gains, gain_ref.shape)
    weights = w_ref[...]
    lane = lax.broadcasted_iota(jnp.int32, (rows, 128), 1)
    low = lane < 64

    @pl.loop(0, GROUP)
    def _(k):
        at = pl.ds(pl.multiple_of((meta[0] ^ k) * rows, rows & -rows), rows)
        at_step(k, copies, lambda copy: copy.wait())
        lin = nn(all_ref[pl.ds(pl.multiple_of(k * rows, rows & -rows), rows), :], weights)
        lin_ref[at, :] = lin
        cosine, sine = cos_ref[at, :], sin_ref[at, :]
        front, back = lin[:, :128], lin[:, 128:]
        head = front * lax.rsqrt(head_sum(front * front, low) * (1 / 64) + EPS) * gains[:, :128]
        head = (head * cosine + rotated(head, lane) * sine) * (HEAD_SIZE**-0.5)
        q_ref[0, at, :] = jnp.where(low, head, 0.0).astype(BF16)
        q_ref[1, at, :] = jnp.where(low, pltpu.roll(head, 64, 1), 0.0).astype(BF16)
        key = back * lax.rsqrt(head_sum(back * back, low) * (1 / 64) + EPS) * gains[:, 128:]
        key = key * cosine + rotated(key, lane) * sine
        kv_ref[at, :] = jnp.where(low, key, back).astype(BF16)
    tail_ref[...] = kv_ref[kv_ref.shape[0] - tail_ref.shape[0] :, :]


def query_bounds(lengths, first, count):
    lane = lax.broadcasted_iota(jnp.int32, (1, 2 * count), 1)
    place = first + jnp.where(lane >= count, lane - count, lane)
    start = jnp.zeros((1, 2 * count), jnp.int32)
    begin, lowest = jnp.int32(0), jnp.int32(0)
    for d in range(lengths.shape[0]):
        start = jnp.where(place >= begin, begin, start)
        lowest = jnp.where(first >= begin, begin, lowest)
        begin = begin + lengths[d]
    return place, start, lowest


def fill_keys(parts, keys_ref):
    @pl.when(pl.program_id(0) == 0)
    def _():
        at = 0
        for part in parts:
            keys_ref[at : at + part.shape[0], :] = part[...]
            at += part.shape[0]


def attend_kernel(halo, span, meta, lengths, q_ref, *refs):
    *parts, out_ref, log_ref, kv_ref = refs
    step = pl.program_id(0)
    base = meta[1] - halo
    fill_keys(parts, kv_ref)
    place, start, lowest = query_bounds(lengths, meta[1] + step * span, span)
    queries = q_ref[...].reshape(2 * span, 128)
    iota = lax.broadcasted_iota(jnp.int32, (span, 2 * span), 0)
    first = jnp.maximum(lowest - base, 0) // span

    def body(at, carry):
        total, mixed = carry
        offset = pl.multiple_of(at * span, span)
        keys = kv_ref[pl.ds(offset, span), :]
        score = nt(keys, queries)
        moved = base + offset
        weight = jnp.where((iota >= start - moved) & (iota <= place - moved), jnp.exp(score), 0.0)
        total = total + jnp.sum(weight, axis=0, keepdims=True)
        mixed = mixed + tn(keys, weight.astype(BF16))
        return total, mixed

    total, mixed = lax.fori_loop(
        first,
        step + halo // span + 1,
        body,
        (jnp.zeros((1, 2 * span), F32), jnp.zeros((128, 2 * span), F32)),
    )
    mixed = mixed * (1.0 / total)
    side = jnp.concatenate([mixed[64:, :span], mixed[64:, span:]], axis=0)
    out_ref[...] = side.T.astype(BF16)
    log_ref[...] = jnp.broadcast_to(jnp.log(total), (8, 2 * span))


def attend_back_kernel(halo, span, meta, lengths, q_ref, *refs):
    *parts, grad_ref, out_ref, log_ref, dq_ref, early_ref, own_ref, kv_ref, dkv_ref = refs
    step = pl.program_id(0)
    base = meta[1] - halo
    fill_keys(parts, kv_ref)

    @pl.when(step == 0)
    def _():
        dkv_ref[...] = jnp.zeros_like(dkv_ref)

    place, start, lowest = query_bounds(lengths, meta[1] + step * span, span)
    queries = q_ref[...].reshape(2 * span, 128)
    grad = grad_ref[...].astype(F32)
    low = lax.broadcasted_iota(jnp.int32, (span, 128), 1) < 64
    grads = jnp.concatenate(
        [jnp.where(low, 0.0, pltpu.roll(grad, 64, 1)), jnp.where(low, 0.0, grad)], axis=0
    ).astype(BF16)
    both = (grad * out_ref[...].astype(F32)).T
    row_sum = jnp.concatenate(
        [jnp.sum(both[:64], axis=0, keepdims=True), jnp.sum(both[64:], axis=0, keepdims=True)],
        axis=1,
    )
    logs = log_ref[0:1, :]
    iota = lax.broadcasted_iota(jnp.int32, (span, 2 * span), 0)
    first = jnp.maximum(lowest - base, 0) // span

    def body(at, dq):
        offset = pl.multiple_of(at * span, span)
        keys = kv_ref[pl.ds(offset, span), :]
        moved = base + offset
        weight = jnp.where(
            (iota >= start - moved) & (iota <= place - moved),
            jnp.exp(nt(keys, queries) - logs),
            0.0,
        )
        d_score = (weight * (nt(keys, grads) - row_sum)).astype(BF16)
        dkv_ref[pl.ds(offset, span), :] += nn(d_score, queries) + nn(weight.astype(BF16), grads)
        return dq + tn(keys, d_score)

    dq = lax.fori_loop(
        first, step + halo // span + 1, body, jnp.zeros((128, 2 * span), F32)
    ) * (HEAD_SIZE**-0.5)
    dq_ref[...] = jnp.concatenate([dq[:64, :span], dq[:64, span:]], axis=0).T.astype(BF16)

    @pl.when(step == pl.num_programs(0) - 1)
    def _():
        early_ref[...] = dkv_ref[:halo, :].astype(BF16)
        own_ref[...] = dkv_ref[halo:, :]


def block_copies(sources, targets, sems):
    return [pltpu.make_async_copy(*pair, sems.at[n]) for n, pair in enumerate(zip(sources, targets))]


def at_step(step, copies, act):
    for n, copy in enumerate(copies):

        @pl.when(step == n)
        def _():
            act(copy)


def project_kernel(meta, att_ref, w_ref, *refs):
    *outs, held, sems = refs
    rows = held.shape[1]
    copies = block_copies([held.at[k] for k in range(GROUP)], outs, sems)

    @pl.loop(0, GROUP)
    def _(k):
        at = pl.ds(pl.multiple_of((meta[0] ^ k) * rows, rows & -rows), rows)
        held[k] = nn(att_ref[at, :], w_ref[...]).astype(BF16)
        at_step(k, copies, lambda copy: copy.start())

    for copy in copies:
        copy.wait()


def unproject_kernel(meta, *refs):
    blocks, refs = refs[:GROUP], refs[GROUP:]
    unproject_body(meta, blocks, *refs)


def unproject_into_kernel(meta, *refs):
    blocks, refs = refs[:GROUP], refs[GROUP:]
    w_ref, att_ref, _, out_ref, rest_ref, grad_ref, spot_ref, sem, held, sems = refs
    unproject_body(meta, blocks, w_ref, att_ref, out_ref, grad_ref, held, sems)
    o_rows = spot_ref.shape[2]
    spot_ref[...] = jnp.zeros_like(spot_ref)
    for n in range(2):
        spot_ref[2 * meta[3] + meta[4] % 2, n] = grad_ref[n * o_rows : (n + 1) * o_rows, :]
    copy = pltpu.make_async_copy(
        spot_ref, rest_ref.at[:, :, pl.ds(rest_ref.shape[2] - o_rows, o_rows)], sem
    )
    copy.start()
    copy.wait()


def unproject_body(meta, blocks, w_ref, att_ref, out_ref, grad_ref, held, sems):
    rows = held.shape[1]
    copies = block_copies(blocks, [held.at[k] for k in range(GROUP)], sems)
    for copy in copies:
        copy.start()

    def body(k, total):
        at_step(k, copies, lambda copy: copy.wait())
        at = pl.ds(pl.multiple_of((meta[0] ^ k) * rows, rows & -rows), rows)
        own = held[k]
        out_ref[at, :] = nt(own, w_ref[...]).astype(BF16)
        return total + tn(att_ref[at, :], own)

    grad_ref[...] = lax.fori_loop(
        0, GROUP, body, jnp.zeros(grad_ref.shape, F32)
    ).astype(BF16)


def finish_kernel(meta, dq_ref, own_ref, *refs):
    *backs, lin_ref, cos_ref, sin_ref, w_ref, gains_ref = refs[: -GROUP - 6]
    hidden = refs[-GROUP - 6 : -6]
    dlin_ref, gain_ref, dkv_ref, held_ref, hidden_held, sems = refs[-6:]
    dkv_ref[...] = own_ref[...]
    for back in backs:
        dkv_ref[dkv_ref.shape[0] - back.shape[0] :, :] += back[...].astype(F32)
    weights, gains = w_ref[...], gains_ref[0:1, :]
    rows = hidden_held.shape[1]
    lane = lax.broadcasted_iota(jnp.int32, (rows, 128), 1)
    low = lane < 64

    def body(block, gain_sums):
        at = pl.ds(pl.multiple_of(block * rows, rows & -rows), rows)
        cosine, sine = cos_ref[at, :], sin_ref[at, :]
        parts, sums = [], []
        for side, source in enumerate((dq_ref, dkv_ref)):
            lin = lin_ref[at, 128 * side : 128 * side + 128]
            factor = lax.rsqrt(head_sum(lin * lin, low) * (1 / 64) + EPS)
            plain = lin * factor
            given = source[at, :].astype(BF16).astype(F32)
            turned = given * cosine - rotated(given, lane) * sine
            sums.append(gain_sums[side] + jnp.sum(turned * plain, axis=0, keepdims=True))
            scaled = turned * gains[:, 128 * side : 128 * side + 128]
            grad = factor * (scaled - plain * (head_sum(scaled * plain, low) * (1 / 64)))
            parts.append(jnp.where(low, grad, given) if side else grad)
        held_ref[at, :] = jnp.concatenate(parts, axis=1).astype(BF16)
        return tuple(sums)

    gain_sums = lax.fori_loop(0, GROUP, body, (jnp.zeros((1, 128), F32),) * 2)
    copies = block_copies([hidden_held.at[k] for k in range(GROUP)], hidden, sems)

    @pl.loop(0, GROUP)
    def _(k):
        dlin = held_ref[pl.ds(pl.multiple_of((meta[0] ^ k) * rows, rows & -rows), rows), :]
        dlin_ref[pl.ds(pl.multiple_of(k * rows, rows & -rows), rows), :] = dlin
        hidden_held[k] = nt(dlin, weights).astype(BF16)
        at_step(k, copies, lambda copy: copy.start())

    for copy in copies:
        copy.wait()
    gain_ref[...] = jnp.broadcast_to(jnp.concatenate(gain_sums, axis=1), gain_ref.shape)


def project_grad_kernel(meta, n_ref, d_ref, gain_ref, *refs):
    *outs, grad_ref = refs
    parts, rows = outs[0].shape[0], outs[0].shape[1] - 16
    grad_ref[...] = tn(n_ref[...], d_ref[...]).astype(BF16)
    extra = jnp.where(
        lax.broadcasted_iota(jnp.int32, (16, 256), 0) == 0, gain_ref[0:1, :], 0.0
    ).astype(BF16)
    for m, out in enumerate(outs):
        first = (meta[5] ^ m) * (parts * rows) if len(outs) > 1 else 0
        for part in range(parts):
            at = first + part * rows
            if len(outs) > 1:
                at = pl.multiple_of(at, rows)
            out[part, :rows, :] = grad_ref[pl.ds(at, rows), :]
            out[part, rows:, :] = extra


def spread_sum_kernel(seq, *refs):
    *parts, out_ref = refs
    for i_at in range(parts[0].shape[0]):
        total = parts[0][i_at].astype(F32)
        for part in parts[1:]:
            total = total + part[i_at].astype(F32)
        total = total.astype(BF16)
        for s_at in range(seq):
            out_ref[i_at * seq + s_at] = total


def arrange_heads_kernel(meta, *refs):
    *pieces, out_ref = refs
    for m, piece in enumerate(pieces):
        for o_at in range(out_ref.shape[0]):
            out_ref[o_at, meta[4] ^ m] = piece[...]


def arrange_wide_kernel(meta, *refs):
    *pieces, out_ref = refs
    for m, piece in enumerate(pieces):
        out_ref[meta[4] ^ m] = piece[...]


def wide_grad_kernel(h_ref, d_ref, out_ref):
    chunk = out_ref.shape[2]

    @pl.loop(0, 2)
    def _(n):
        @pl.loop(0, out_ref.shape[0])
        def _(o_at):
            at = pl.ds(pl.multiple_of(o_at * chunk, chunk), chunk)
            out_ref[o_at, n] = tn(h_ref[:, at], d_ref[n]).astype(BF16)


def down_grad_kernel(rows, inner_ref, c_ref, out_ref):
    @pl.loop(0, 2)
    def _(n):
        grad = tn(inner_ref[n], c_ref[...]).astype(BF16)
        for o_at in range(out_ref.shape[0]):
            out_ref[o_at, n, :rows, :] = grad[o_at * rows : (o_at + 1) * rows]


def rest_out_kernel(meta, mine_ref, other_ref, down_ref, out_ref):
    rows = down_ref.shape[0] // 2
    mine, other = mine_ref[...].astype(F32), other_ref[...].astype(F32)
    out_ref[...] = mine[rows:] + other[rows:]
    first = meta[3] == 0
    down_ref[:rows, :] = jnp.where(first, mine[:rows], other[:rows])
    down_ref[rows:, :] = jnp.where(first, other[:rows], mine[:rows])


def near_kernel(*refs):
    for mine, far, out in zip(refs[:4], refs[4:8], refs[8:]):
        out[...] = (mine[...].astype(F32) + far[...].astype(F32)).astype(out.dtype)


def total_of(refs):
    total = refs[0][...].astype(F32)
    for ref in refs[1:]:
        total = total + ref[...].astype(F32)
    return total


def middle_kernel(*refs):
    *parts, middle_ref, plain_ref = refs
    middle = total_of(parts)
    middle_ref[...] = middle
    plain_ref[...] = normalized(middle)[0].astype(BF16)


def back_norm_kernel(*refs):
    source_ref, base_ref, *parts, full_ref, low_ref = refs
    plain, factor = normalized(source_ref[...].astype(F32))
    total = base_ref[...].astype(F32) + norm_back(total_of(parts), plain, factor)
    full_ref[...] = total
    low_ref[...] = total.astype(BF16)


def feed_kernel(count, down_rows, *refs):
    hs, cs, (wgu_in, wd_in), refs = refs[:count], refs[count : 2 * count], refs[2 * count :][:2], refs
    wgu_held, wd_held, total, sems = refs[-4:]
    fed_out, two_out = refs[-8 - 2 * count : -8 - count], refs[-8 - count : -8]
    h_ref, c_ref, dgu_ref, inner_ref = refs[-8:-4]
    up_rows = wgu_in.shape[2]

    def copies(part, n):
        source, target, step = (
            (wgu_in, wgu_held, up_rows),
            (wd_in, wd_held, down_rows),
        )[n]
        return [
            pltpu.make_async_copy(
                source.at[o_at, part, pl.ds(0, step)],
                target.at[part, pl.ds(o_at * step, step)],
                sems.at[2 * part + n, o_at],
            )
            for o_at in range(source.shape[0])
        ]

    for part in range(2):
        for n in range(2):
            for copy in copies(part, n):
                copy.start()
    deep = wd_held.shape[1]
    for part in range(2):
        wd_held[part, deep - 64 :, :] = jnp.zeros((64, wd_held.shape[2]), BF16)
    rows = hs[0].shape[0]
    hidden = jnp.concatenate([h[...] for h in hs], axis=0)
    cotangent = jnp.concatenate([c[...] for c in cs], axis=0)
    h_ref[...] = hidden
    c_ref[...] = cotangent
    main = wgu_in.shape[3] // 2 - 64
    low = lax.broadcasted_iota(jnp.int32, (count * rows, 128), 1) < 64

    def piece(gate, up, given):
        sigma = 1.0 / (1.0 + jnp.exp(-gate))
        act = gate * sigma
        return act * up, given * up * (sigma * (1.0 + gate * (1.0 - sigma))), given * act

    total[...] = jnp.zeros_like(total)

    @pl.loop(0, 2)
    def _(part):
        wgu_ref, wd_ref = wgu_held.at[part], wd_held.at[part]
        for copy in copies(part, 0):
            copy.wait()
        both = nn(h_ref[...], wgu_ref[...])
        for copy in copies(part, 1):
            copy.wait()
        d_inner = nt(c_ref[...], wd_ref[...])
        tile = both[:, main : main + 128]
        inner_m, dg_m, du_m = piece(both[:, :main], both[:, main + 128 :], d_inner[:, :main])
        inner_t, dg_t, du_t = piece(tile, pltpu.roll(tile, 64, 1), d_inner[:, main:])
        inner = jnp.concatenate([inner_m, jnp.where(low, inner_t, 0.0)], axis=1).astype(BF16)
        d_tile = jnp.where(low, dg_t, pltpu.roll(du_t, 64, 1))
        dgu = jnp.concatenate([dg_m, d_tile, du_m], axis=1).astype(BF16)
        dgu_ref[part] = dgu
        inner_ref[part] = inner
        total[0] += nt(dgu, wgu_ref[...])
        total[1] += nn(inner, wd_ref[...])

    for n in range(count):
        two_out[n][...] = total[0, n * rows : (n + 1) * rows, :].astype(BF16)
        fed_out[n][...] = total[1, n * rows : (n + 1) * rows, :].astype(BF16)


def feed(at, hs, cs, weights, down_rows, whole, tokens):
    count = len(hs)
    rows, width = hs[0].shape
    wide = weights[0].shape[3]
    deep = wide // 2 + 64

    def full(dims):
        return pl.BlockSpec(dims, lambda j: (0,) * len(dims))

    outs = pl.pallas_call(
        functools.partial(feed_kernel, count, down_rows),
        grid=(1,),
        in_specs=[full((rows, width))] * (2 * count)
        + [pl.BlockSpec(memory_space=pl.ANY)] * (2 + len(whole)),
        out_specs=[full((rows, width))] * (2 * count)
        + [pl.BlockSpec((count * rows, width), lambda j: (at, 0))] * 2
        + [pl.BlockSpec((2, count * rows, w), lambda j: (0, at, 0)) for w in (wide, deep)],
        out_shape=[shape((rows, width), BF16)] * (2 * count)
        + [shape((tokens, width), BF16)] * 2
        + [shape((2, tokens, w), BF16) for w in (wide, deep)],
        scratch_shapes=[
            pltpu.VMEM((2, width, wide), BF16),
            pltpu.VMEM((2, deep, width), BF16),
            pltpu.VMEM((2, count * rows, width), F32),
            pltpu.SemaphoreType.DMA((4, max(w.shape[0] for w in weights))),
        ],
        input_output_aliases={2 * count + 2 + n: 2 * count + n for n in range(len(whole))},
        compiler_params=pltpu.CompilerParams(
            vmem_limit_bytes=VMEM_LIMIT, dimension_semantics=("arbitrary",)
        ),
        cost_estimate=pl.CostEstimate(
            flops=12 * count * rows * width * wide,
            bytes_accessed=2 * (3 * width * wide + 12 * count * rows * width),
            transcendentals=0,
        ),
        name="feed",
    )(*hs, *cs, *weights, *whole)
    return outs[:count], outs[count : 2 * count], outs[2 * count :]


def inner_swap(value, mask, count):
    return lax.ppermute(value, ("a", "b"), [(r, r ^ mask) for r in range(count)])


def outer_swap(value, mask, count):
    return lax.ppermute(value, "o", [(r, r ^ mask) for r in range(count)])


def swap(value, mask):
    return lax.ppermute(value, ("a", "b", "c"), [(r, r ^ mask) for r in range(GROUP)])


def after(value, *others):
    return lax.optimization_barrier((value, others))[0]


def gather_blocks(value, *others):
    blocks = {0: value}
    for k in (1, 4, 5):
        blocks[k] = swap(value, k)
    if others:
        blocks = after(blocks, *others)
    for k in (0, 1, 4, 5):
        blocks[k ^ 2] = swap(blocks[k], 2)
    return [blocks[k] for k in range(GROUP)]


def near_sums(parts, first=None):
    order = (0, 1, 4, 5)
    far = [swap(parts[k ^ 2], 2) for k in order]
    if first is not None:
        far = list(after(tuple(far), first))
    block = parts[0].shape
    near = call(
        near_kernel,
        [shape(block, F32)] + [shape(block, BF16)] * 3,
        0,
        [*[parts[k] for k in order], *far],
        0,
        "near",
    )
    return [near[0]] + [swap(near[n], order[n]) for n in (1, 2, 3)]


def normalized(values):
    factor = lax.rsqrt(jnp.mean(values * values, axis=-1, keepdims=True) + EPS)
    return values * factor, factor


def norm_back(grad, plain, factor):
    return factor * (grad - plain * jnp.mean(grad * plain, axis=-1, keepdims=True))


def on_device(
    inner_count,
    stream,
    cotangent,
    doc_lengths,
    attention_gain,
    query_weight,
    key_matrix,
    value_matrix,
    query_gain,
    key_gain,
    output_weight,
    feedforward_gain,
    gate_weight,
    up_weight,
    down_weight,
):
    rows, width = stream.shape
    outer, seq = lax.axis_size("o"), GROUP // inner_count
    o = lax.axis_index("o")
    if inner_count == 1:
        i, s = jnp.int32(0), lax.axis_index(("a", "b", "c"))
    else:
        i, s = lax.axis_index(("a", "b")), lax.axis_index("c")
    shards = outer * inner_count
    me = i * seq + s
    tokens = GROUP * rows
    block = rows * seq
    lookback = max(2, -(-DOC_MIN // block))
    halo = lookback * block
    span = 2 * rows
    k_rows = query_weight.shape[0]
    o_rows = output_weight.shape[0]
    ff_rows = down_weight.shape[0] // seq
    ff_local = outer * ff_rows
    main = ff_local - 64
    few = outer <= 4

    def kv_head(i_at, s_at):
        if inner_count == 1:
            return s_at
        return 4 * s_at + 2 * (i_at % 2) + i_at // 2

    shard = o * inner_count + i
    per = query_gain.shape[0]
    meta = jnp.stack([me, o * tokens, shard, s, i, o]).astype(jnp.int32)
    lengths = doc_lengths.astype(jnp.int32)
    gain_one = attention_gain.astype(F32)[:, None]
    gain_two = feedforward_gain.astype(F32)[:, None]
    head_gains = jnp.concatenate([query_gain, key_gain]).astype(F32)

    heads_in = [query_weight, key_matrix, value_matrix, gain_one]
    heads_shape = (inner_count, k_rows + 16, 256)
    chips = ("o", "b")
    if inner_count > 1:
        sent = call(
            functools.partial(send_heads_kernel, kv_head, seq),
            [shape(heads_shape[1:], BF16)] * inner_count,
            2,
            [meta, head_gains, *heads_in],
            0,
            "send_heads",
            [pltpu.VMEM(heads_shape, BF16)],
        )
        (packed,) = call(
            arrange_heads_kernel,
            [shape((outer, *heads_shape), BF16)],
            1,
            [meta, sent[0]] + [inner_swap(sent[m], m, inner_count) for m in range(1, inner_count)],
            0,
            "arrange_heads",
        )
        n_blocks = gather_blocks(normalized(after(stream, packed).astype(F32))[0].astype(BF16))
        w_heads = lax.all_to_all(packed, "o", split_axis=0, concat_axis=0, tiled=True)
        half_down = lax.dynamic_slice_in_dim(down_weight, s * ff_rows, ff_rows, 0)
        w_rest = lax.all_gather(jnp.concatenate([half_down, output_weight]), chips, axis=0)
        w_rest = w_rest.reshape(outer, 2, ff_rows + o_rows, width)
        down_rows, w_down = ff_rows, w_rest
        w_out = lax.dynamic_index_in_dim(w_rest, 2 * s + i % 2, 0, keepdims=False)
        w_out = w_out[:, ff_rows:].reshape(128, width)
    else:
        (packed,) = call(
            functools.partial(pack_heads_kernel, kv_head, seq),
            [shape(heads_shape, BF16)],
            2,
            [meta, head_gains, *heads_in],
            0,
            "pack_heads",
        )

        def columns(weight):
            scaled = (weight.astype(F32) * gain_two).astype(BF16)
            split = scaled.reshape(k_rows, outer, seq, ff_rows)
            return lax.dynamic_index_in_dim(split, s, 2, keepdims=False).reshape(k_rows, ff_local)

        gate_c, up_c = columns(gate_weight), columns(up_weight)
        packed_gu = jnp.concatenate(
            [gate_c[:, :main], gate_c[:, main:], up_c[:, main:], up_c[:, :main]], axis=1
        )
        half_down = lax.dynamic_slice_in_dim(down_weight, s * ff_rows, ff_rows, 0)
        w_down = lax.all_gather(half_down, chips, axis=0).reshape(outer, 2, ff_rows, width)
        w_down = w_down.transpose(1, 0, 2, 3).reshape(1, 2, ff_local, width)
        down_rows = ff_local
        n_blocks = gather_blocks(normalized(stream.astype(F32))[0].astype(BF16))
        w_heads = lax.all_gather(packed, "o", axis=0)
        w_out = lax.all_gather(output_weight, "o", axis=0, tiled=True)
        w_out = lax.dynamic_slice_in_dim(w_out, s * 128, 128, 0)
    w_heads = w_heads.reshape(shards, k_rows + 16, 256)
    starts = jnp.cumsum(lengths) - lengths
    places = o * tokens + jnp.arange(tokens, dtype=jnp.int32)
    begin = jnp.max(jnp.where(starts[None, :] <= places[:, None], starts[None, :], -1), axis=1)
    half = HEAD_SIZE // 2
    freq = jnp.power(THETA, -(jnp.arange(half, dtype=F32) * (2.0 / HEAD_SIZE)))
    angle = (places - begin).astype(F32)[:, None] * freq[None, :]
    cosine = jnp.tile(jnp.cos(angle), (1, 4))
    sine = jnp.tile(jnp.sin(angle), (1, 4))

    own_c = after(cotangent, n_blocks[5])
    c_blocks = {0: own_c, 1: swap(own_c, 1), 4: swap(own_c, 4), 5: swap(own_c, 5)}
    hops = -(-halo // tokens)
    blocks_scratch = [
        pltpu.VMEM((GROUP, rows, width), BF16),
        pltpu.SemaphoreType.DMA((GROUP,)),
    ]
    tail_rows = halo - (hops - 1) * tokens
    queries, kv, tail, lin, n_all, w_qkv, head_row = call(
        prepare_kernel,
        [
            shape((2, tokens, 128), BF16),
            shape((tokens, 128), BF16),
            shape((tail_rows, 128), BF16),
            shape((tokens, 256), F32),
            shape((tokens, width), BF16),
            shape((width, 256), BF16),
            shape((8, 256), F32),
        ],
        1,
        [meta, *n_blocks, w_heads, cosine, sine],
        2 * tokens * width * 256,
        "prepare",
        [pltpu.SemaphoreType.DMA((GROUP,))],
        far_in=range(1, GROUP + 1),
    )
    starts = jnp.cumsum(lengths) - lengths
    places = o * tokens + jnp.arange(tokens, dtype=jnp.int32)
    begin = jnp.max(jnp.where(starts[None, :] <= places[:, None], starts[None, :], -1), axis=1)
    half = HEAD_SIZE // 2
    freq = jnp.power(THETA, -(jnp.arange(half, dtype=F32) * (2.0 / HEAD_SIZE)))
    angle = (places - begin).astype(F32)[:, None] * freq[None, :]
    cosine = jnp.tile(jnp.cos(angle), (1, 4))
    sine = jnp.tile(jnp.sin(angle), (1, 4))

    own_c = after(cotangent, n_blocks[5])
    c_blocks = {0: own_c, 1: swap(own_c, 1), 4: swap(own_c, 4), 5: swap(own_c, 5)}
    hops = -(-halo // tokens)
    blocks_scratch = [
        pltpu.VMEM((GROUP, rows, width), BF16),
        pltpu.SemaphoreType.DMA((GROUP,)),
    ]
    tail_rows = halo - (hops - 1) * tokens
    queries, kv, tail, lin, n_all, w_qkv, head_row = call(
        prepare_kernel,
        [
            shape((2, tokens, 128), BF16),
            shape((tokens, 128), BF16),
            shape((tail_rows, 128), BF16),
            shape((tokens, 256), F32),
            shape((tokens, width), BF16),
            shape((width, 256), BF16),
            shape((8, 256), F32),
        ],
        1,
        [meta, *n_blocks, w_heads, cosine, sine],
        2 * tokens * width * 256,
        "prepare",
        [pltpu.SemaphoreType.DMA((GROUP,))],
        far_in=range(1, GROUP + 1),
    )
    tail = after(tail, tuple(c_blocks.values()))
    keys = [
        lax.ppermute(
            tail if hop == hops else kv, "o", [(at, at + hop) for at in range(max(0, outer - hop))]
        )
        for hop in range(hops, 0, -1)
    ] + [kv]
    if inner_count > 1:
        wide_in = after((gate_weight, up_weight), packed)
        sent = call(
            functools.partial(send_wide_kernel, seq, outer),
            [shape((k_rows, 2 * ff_local), BF16)] * inner_count,
            1,
            [meta, *wide_in, gain_two],
            0,
            "send_wide",
            [
                pltpu.VMEM((inner_count, k_rows, 2 * ff_local), BF16),
                pltpu.VMEM((2, k_rows, ff_local), F32),
            ],
        )
        sent = [sent[0]] + [inner_swap(sent[m], m, inner_count) for m in range(1, inner_count)]
    if inner_count > 1:
        (packed_gu,) = call(
            arrange_wide_kernel,
            [shape((inner_count, k_rows, 2 * ff_local), BF16)],
            1,
            [meta, *after(sent, keys[0])],
            0,
            "arrange_wide",
        )
    w_gu = lax.all_gather(
        packed_gu.reshape(inner_count * k_rows, 2 * ff_local), chips, axis=0
    ).reshape(outer, 2, inner_count * k_rows, 2 * ff_local)
    steps = tokens // span
    reach = halo + tokens
    pair_flops = 4 * tokens * (span + halo // 2) * 128

    def attention(kernel, ins, outs, scratch, flops, name):
        return pl.pallas_call(
            functools.partial(kernel, halo, span),
            grid=(steps,),
            in_specs=[SM, SM] + [spec for _, spec in ins],
            out_specs=[spec for _, spec in outs],
            out_shape=[dims for dims, _ in outs],
            scratch_shapes=scratch,
            compiler_params=pltpu.CompilerParams(
                vmem_limit_bytes=VMEM_LIMIT, dimension_semantics=("arbitrary",)
            ),
            cost_estimate=pl.CostEstimate(
                flops=flops, bytes_accessed=4 * reach * 256, transcendentals=0
            ),
            name=name,
        )(meta, lengths, *[value for value, _ in ins])

    def still(value):
        return pl.BlockSpec(value.shape, lambda j: (0, 0))

    q_spec = pl.BlockSpec((2, span, 128), lambda j: (0, j, 0))
    row_spec = pl.BlockSpec((span, 128), lambda j: (j, 0))
    log_spec = pl.BlockSpec((8, 2 * span), lambda j: (j, 0))
    key_ins = [(part, still(part)) for part in keys]
    attended, logs = attention(
        attend_kernel,
        [(queries, q_spec), *key_ins],
        [
            (shape((tokens, 128), BF16), row_spec),
            (shape((8 * steps, 2 * span), F32), log_spec),
        ],
        [pltpu.VMEM((reach, 128), BF16)],
        pair_flops,
        "attend",
    )

    parts = call(
        project_kernel,
        [shape((rows, width), BF16)] * GROUP,
        1,
        [meta, attended, w_out],
        2 * tokens * 128 * width,
        "project",
        blocks_scratch,
        far_out=range(GROUP),
    )
    near_parts = near_sums(parts)
    middle, plain_two = call(
        middle_kernel,
        [shape((rows, width), F32), shape((rows, width), BF16)],
        0,
        [stream, *near_parts],
        0,
        "middle",
    )

    h_blocks = {0: plain_two}
    for k in (1, 4, 5):
        h_blocks[k] = swap(h_blocks[0], k)
    fed, two, whole = {}, {}, []
    for at, ks in ((2, (0,)), (0, (1, 4)), (3, (5,))):
        fed_k, two_k, whole = feed(
            at,
            [h_blocks[k] for k in ks],
            [c_blocks[k] for k in ks],
            [w_gu, w_down],
            down_rows,
            whole,
            4 * rows,
        )
        for n, k in enumerate(ks):
            fed[k], two[k] = fed_k[n], two_k[n]
    h_all, c_all, dgu_all, inner_all = whole

    def from_chips(parts):
        return [parts[0]] + [swap(parts[k], k) for k in (1, 4, 5)]

    d_mid_f, d_mid = call(
        back_norm_kernel,
        [shape((rows, width), F32), shape((rows, width), BF16)],
        0,
        [middle, cotangent, *from_chips(two)],
        0,
        "back_two",
    )
    if inner_count > 1:
        (grad_gu,) = call(
            wide_grad_kernel,
            [shape((outer, 2, inner_count * k_rows, 2 * ff_local), BF16)],
            0,
            [h_all, dgu_all],
            0,
            "wide_grad",
        )
        grad_gu = after(grad_gu, d_mid).reshape(-1, 2 * ff_local)
        grad_gu = lax.psum_scatter(grad_gu, chips, scatter_dimension=0, tiled=True)
        grad_gu = grad_gu.reshape(inner_count, k_rows, 2 * ff_local)
        (grad_rest,) = call(
            functools.partial(down_grad_kernel, ff_rows),
            [shape((outer, 2, ff_rows + o_rows, width), BF16)],
            0,
            [inner_all, c_all],
            0,
            "down_grad",
        )
        m_blocks = gather_blocks(d_mid, grad_rest)
        d_attended, grad_rest = pl.pallas_call(
            unproject_into_kernel,
            in_specs=[SM] + [FAR] * GROUP + [VM, VM, FAR],
            out_specs=[VM, FAR],
            out_shape=[shape((tokens, 128), BF16), shape(grad_rest.shape, BF16)],
            scratch_shapes=[
                pltpu.VMEM((128, width), BF16),
                pltpu.VMEM((outer, 2, o_rows, width), BF16),
                pltpu.SemaphoreType.DMA(()),
                *blocks_scratch,
            ],
            input_output_aliases={GROUP + 3: 1},
            compiler_params=pltpu.CompilerParams(vmem_limit_bytes=VMEM_LIMIT),
            cost_estimate=pl.CostEstimate(
                flops=4 * tokens * 128 * width, bytes_accessed=8 << 20, transcendentals=0
            ),
            name="unproject",
        )(meta, *m_blocks, w_out, attended, grad_rest)
        grad_rest = grad_rest.reshape(-1, width)
        grad_rest = lax.psum_scatter(grad_rest, chips, scatter_dimension=0, tiled=True)
        grad_down, grad_output = call(
            rest_out_kernel,
            [shape((seq * ff_rows, width), F32), shape((o_rows, width), F32)],
            1,
            [meta, grad_rest, swap(grad_rest, 1)],
            0,
            "rest_out",
        )
    else:
        m_blocks = gather_blocks(d_mid)
        grad_gu = jnp.stack([tn(h_all, dgu_all[n]).astype(BF16) for n in range(2)])
        grad_gu = grad_gu.reshape(2, outer, k_rows, 2 * ff_local).transpose(1, 0, 2, 3)
        grad_gu = lax.psum_scatter(
            grad_gu.reshape(-1, 2 * ff_local), chips, scatter_dimension=0, tiled=True
        ).reshape(inner_count, k_rows, 2 * ff_local)
        d_attended, grad_out = call(
            unproject_kernel,
            [shape((tokens, 128), BF16), shape((128, width), BF16)],
            1,
            [meta, *m_blocks, w_out, attended],
            4 * tokens * 128 * width,
            "unproject",
            blocks_scratch,
            far_in=range(1, GROUP + 1),
        )
        grad_dn = jnp.stack([tn(inner_all[n], c_all)[:ff_local].astype(BF16) for n in range(2)])
        grad_dn = grad_dn.reshape(2, outer, ff_rows, width).transpose(1, 0, 2, 3)
        grad_dn = lax.psum_scatter(
            grad_dn.reshape(-1, width), chips, scatter_dimension=0, tiled=True
        )
        grad_down = lax.all_gather(grad_dn, ("a", "b", "c"), axis=0, tiled=True).astype(F32)
        spot = lax.dynamic_update_slice_in_dim(
            jnp.zeros((shards * o_rows, width), BF16), grad_out, s * 128, 0
        )
        spot = lax.psum_scatter(spot, "o", scatter_dimension=0, tiled=True)
        grad_output = lax.psum(spot, ("a", "b", "c")).astype(F32)

    def to_owners(value):
        value = jnp.repeat(value, seq, axis=0)
        return lax.all_to_all(value, ("a", "b", "c"), split_axis=0, concat_axis=0, tiled=True)

    got = to_owners(grad_gu)
    dq, d_early, d_own = attention(
        attend_back_kernel,
        [
            (queries, q_spec),
            *key_ins,
            (d_attended, row_spec),
            (attended, row_spec),
            (logs, log_spec),
        ],
        [
            (shape((tokens, 128), BF16), row_spec),
            (shape((halo, 128), BF16), pl.BlockSpec((halo, 128), lambda j: (0, 0))),
            (shape((tokens, 128), F32), pl.BlockSpec((tokens, 128), lambda j: (0, 0))),
        ],
        [pltpu.VMEM((reach, 128), BF16), pltpu.VMEM((reach, 128), F32)],
        3 * pair_flops,
        "attend_back",
    )
    late = dict(zip(fed, after(tuple(fed.values()), dq)))
    result = middle
    for part in from_chips(late):
        result = result + part.astype(F32)
    result = result.astype(BF16)
    backs = []
    for at, hop in enumerate(range(hops, 0, -1)):
        begin_at = 0 if at == 0 else tail_rows + (at - 1) * tokens
        size = tail_rows if at == 0 else tokens
        backs.append(
            lax.ppermute(
                d_early[begin_at : begin_at + size],
                "o",
                [(p + hop, p) for p in range(max(0, outer - hop))],
            )
        )
    *hidden_parts, dlin, gain_part = call(
        finish_kernel,
        [shape((rows, width), BF16)] * GROUP + [shape((tokens, 256), BF16), shape((8, 256), F32)],
        1,
        [meta, dq, d_own, *backs, lin, cosine, sine, w_qkv, head_row],
        2 * tokens * width * 256,
        "finish",
        [pltpu.VMEM((tokens, 128), F32), pltpu.VMEM((tokens, 256), BF16), *blocks_scratch],
        far_out=range(GROUP),
    )
    pieces = outer if few else 1
    grad_p = call(
        project_grad_kernel,
        [shape((shards // pieces, k_rows + 16, 256), BF16)] * pieces,
        1,
        [meta, n_all, dlin, gain_part],
        2 * tokens * width * 256,
        "project_grad",
        [pltpu.VMEM((width, 256), BF16)],
    )
    near_h = near_sums(hidden_parts, (grad_p, result))
    _, grad_stream = call(
        back_norm_kernel,
        [shape((rows, width), F32), shape((rows, width), BF16)],
        0,
        [stream, d_mid_f, *near_h],
        0,
        "back_one",
    )

    if inner_count > 1:
        grad_gate, grad_up, gain_sum = call(
            functools.partial(unpack_wide_kernel, outer),
            [shape((k_rows, GROUP * ff_local), F32)] * 2 + [shape((k_rows, 128), F32)],
            0,
            [got, gate_weight, up_weight, gain_two],
            0,
            "unpack_wide",
        )
        grad_feedforward_gain = gain_sum[:, 0]
    else:
        gu = got.astype(F32)

        def wide(value):
            split = value.reshape(inner_count, seq, k_rows, outer, ff_rows)
            return split.transpose(2, 3, 0, 1, 4).reshape(k_rows, -1)

        raw_gate = wide(gu[..., :ff_local])
        raw_up = wide(
            jnp.concatenate(
                [gu[..., ff_local + 64 :], gu[..., ff_local : ff_local + 64]], axis=-1
            )
        )
        grad_feedforward_gain = jnp.sum(
            raw_gate * gate_weight.astype(F32) + raw_up * up_weight.astype(F32), axis=1
        )
        grad_gate, grad_up = raw_gate * gain_two, raw_up * gain_two

    if few:
        grad_p = [grad_p[0]] + [outer_swap(grad_p[m], m, outer) for m in range(1, outer)]
        grad_p = after(grad_p, near_h[0], got)
        (total,) = call(
            functools.partial(spread_sum_kernel, seq),
            [shape((GROUP, k_rows + 16, 256), BF16)],
            0,
            grad_p,
            0,
            "spread_sum",
        )
        total = after(total, near_h[1:])
        owned = lax.all_to_all(total, ("a", "b", "c"), split_axis=0, concat_axis=0, tiled=True)
    else:
        owned = to_owners(lax.psum_scatter(grad_p[0], "o", scatter_dimension=0, tiled=True))
    grad_query, grad_key, grad_value, gain_sum, head_sums = call(
        functools.partial(owners_kernel, kv_head, seq, per),
        [
            shape(query_weight.shape, F32),
            shape(key_matrix.shape, F32),
            shape(value_matrix.shape, F32),
            shape((k_rows, 128), F32),
            shape((8, 128), F32),
        ],
        1,
        [meta, owned, query_weight, key_matrix, value_matrix, gain_one],
        0,
        "owners",
    )
    return (
        result,
        grad_stream,
        gain_sum[:, 0],
        grad_query,
        grad_key,
        grad_value,
        head_sums[0, :per],
        head_sums[0, 64 : 64 + per],
        grad_output,
        grad_feedforward_gain,
        grad_gate,
        grad_up,
        grad_down,
    )


def solution(mesh):
    fsdp, seq = mesh.shape["fsdp"], mesh.shape["seq"]
    inner = GROUP // seq
    split = Mesh(mesh.devices.reshape(fsdp // inner, 2, 2, 2), ("o", "a", "b", "c"))
    both = ("o", "a", "b") if inner > 1 else ("o",)
    tokens, matrix, vector = P(("o", "a", "b", "c"), None), P(both, None), P(both)
    placed = (
        tokens,
        tokens,
        P(),
        vector,
        matrix,
        matrix,
        matrix,
        vector,
        vector,
        matrix,
        vector,
        matrix,
        matrix,
        matrix,
    )
    return jax.shard_map(
        functools.partial(on_device, inner),
        mesh=split,
        in_specs=placed,
        out_specs=(
            tokens,
            tokens,
            vector,
            matrix,
            matrix,
            matrix,
            vector,
            vector,
            matrix,
            vector,
            matrix,
            matrix,
            matrix,
        ),
        check_vma=False,
    )
```

```python
import functools

import jax
import jax.numpy as jnp
from jax import lax
from jax.experimental import pallas as pl
from jax.experimental.pallas import tpu as pltpu
from jax.sharding import Mesh, PartitionSpec as P

QUERY_HEAD_COUNT = 16
KEY_VALUE_HEADS = 8
HEAD_SIZE = 64
DOC_MIN = 1024
EPS = 1e-05
THETA = 1000000.0
GROUP = 8
BF16 = jnp.bfloat16
F32 = jnp.float32
VMEM_LIMIT = 60 * 1024 * 1024

VM = pl.BlockSpec(memory_space=pltpu.VMEM)
SM = pl.BlockSpec(memory_space=pltpu.SMEM)
FAR = pl.BlockSpec(memory_space=pl.ANY)


def nn(left, right):
    return lax.dot_general(left, right, (((1,), (0,)), ((), ())), preferred_element_type=F32)


def nt(left, right):
    return lax.dot_general(left, right, (((1,), (1,)), ((), ())), preferred_element_type=F32)


def tn(left, right):
    return lax.dot_general(left, right, (((0,), (0,)), ((), ())), preferred_element_type=F32)


def call(kernel, outs, n_smem, args, flops, name, scratch=(), far_in=(), far_out=()):
    bytes_moved = sum(a.size * a.dtype.itemsize for a in args) + sum(
        o.size * o.dtype.itemsize for o in outs
    )
    return pl.pallas_call(
        kernel,
        out_shape=outs,
        in_specs=[
            SM if n < n_smem else FAR if n in far_in else VM for n in range(len(args))
        ],
        out_specs=[FAR if n in far_out else VM for n in range(len(outs))],
        scratch_shapes=list(scratch),
        compiler_params=pltpu.CompilerParams(vmem_limit_bytes=VMEM_LIMIT),
        cost_estimate=pl.CostEstimate(flops=flops, bytes_accessed=bytes_moved, transcendentals=0),
        name=name,
    )(*args)


def shape(dims, dtype):
    return jax.ShapeDtypeStruct(dims, dtype)


def rotated(x, lane):
    return jnp.where(lane % 64 < 32, -pltpu.roll(x, 96, 1), pltpu.roll(x, 32, 1))


def head_sum(x, low):
    first = jnp.sum(jnp.where(low, x, 0.0), axis=1, keepdims=True)
    second = jnp.sum(jnp.where(low, 0.0, x), axis=1, keepdims=True)
    return jnp.where(low, first, second)


def pack_heads_kernel(kv_head, seq, meta, gains, q_ref, k_ref, v_ref, scale_ref, out_ref):
    count, rows = out_ref.shape[0], q_ref.shape[0]
    per = gains.shape[0] // 2
    scale = scale_ref[...]
    lane = lax.broadcasted_iota(jnp.int32, (16, 256), 1)
    row = lax.broadcasted_iota(jnp.int32, (16, 256), 0)
    extra = jnp.zeros((16, 256), F32)
    for j in range(per):
        spot = (lane % 64 == meta[2] * per + j) & (row == 0)
        extra = jnp.where(spot & (lane < 128), gains[j], extra)
        extra = jnp.where(spot & (lane >= 128) & (lane < 192), gains[per + j], extra)
    extra = extra.astype(BF16)
    for s_at in range(seq):

        @pl.when(meta[3] == s_at)
        def _():
            for i_at in range(count):
                t = kv_head(i_at, s_at)
                out_ref[i_at, :rows, :128] = (
                    q_ref[:, 128 * t : 128 * t + 128].astype(F32) * scale
                ).astype(BF16)
                pair = 128 * (t // 2)
                key = k_ref[:, pair : pair + 128].astype(F32) * scale
                value = v_ref[:, pair : pair + 128].astype(F32) * scale
                if t % 2:
                    key = pltpu.roll(key, 64, 1)
                else:
                    value = pltpu.roll(value, 64, 1)
                low = lax.broadcasted_iota(jnp.int32, key.shape, 1) < 64
                out_ref[i_at, :rows, 128:] = jnp.where(low, key, value).astype(BF16)

    for i_at in range(count):
        out_ref[i_at, rows:, :] = extra


def send_heads_kernel(kv_head, seq, meta, gains, q_ref, k_ref, v_ref, scale_ref, *refs):
    *outs, heads = refs
    pack_heads_kernel(kv_head, seq, meta, gains, q_ref, k_ref, v_ref, scale_ref, heads)
    for m, out in enumerate(outs):
        out[...] = heads[meta[4] ^ m]


def send_wide_kernel(seq, outer, meta, gate_ref, up_ref, scale_ref, *refs):
    *outs, packed, wide = refs
    count = len(outs)
    piece = gate_ref.shape[1] // (outer * count * seq)
    local = outer * piece
    main = local - 64
    scale = scale_ref[...]
    for s_at in range(seq):

        @pl.when(meta[3] == s_at)
        def _():
            for i_at in range(count):
                for side, source in enumerate((gate_ref, up_ref)):
                    for o_at in range(outer):
                        at = ((o_at * count + i_at) * seq + s_at) * piece
                        wide[side, :, o_at * piece : (o_at + 1) * piece] = (
                            source[:, at : at + piece].astype(F32) * scale
                        )
                packed[i_at, :, :main] = wide[0, :, :main].astype(BF16)
                packed[i_at, :, main : main + 128] = jnp.concatenate(
                    [wide[0, :, main:], wide[1, :, main:]], axis=1
                ).astype(BF16)
                packed[i_at, :, main + 128 :] = wide[1, :, :main].astype(BF16)

    for m, out in enumerate(outs):
        out[...] = packed[meta[4] ^ m]


def unpack_wide_kernel(outer, got_ref, gate_w, up_w, scale_ref, gate_ref, up_ref, gain_ref):
    ranks, rows = got_ref.shape[0], got_ref.shape[1]
    local = got_ref.shape[2] // 2
    piece, main = local // outer, local - 64
    for rank in range(ranks):
        got = got_ref[rank].astype(F32)
        up = jnp.concatenate([got[:, local + 64 :], got[:, local : local + 64]], axis=1)
        for value, out in ((got[:, :local], gate_ref), (up, up_ref)):
            for o_at in range(outer):
                at = (o_at * ranks + rank) * piece
                out[:, at : at + piece] = value[:, o_at * piece : (o_at + 1) * piece]
    scale = scale_ref[...]
    total = jnp.zeros((rows, 1), F32)
    for weight, out in ((gate_w, gate_ref), (up_w, up_ref)):
        raw = out[...]
        total = total + jnp.sum(raw * weight[...].astype(F32), axis=1, keepdims=True)
        out[...] = raw * scale
    gain_ref[...] = jnp.broadcast_to(total, gain_ref.shape)


def owners_kernel(
    kv_head, seq, per, meta, got_ref, q_w, k_w, v_w, scale_ref, q_ref, k_ref, v_ref, gain_ref, head_ref
):
    ranks, rows = got_ref.shape[0], q_w.shape[0]
    scale = scale_ref[...]
    total = jnp.zeros((rows, 1), F32)
    sums = jnp.zeros((16, 256), F32)
    low = lax.broadcasted_iota(jnp.int32, (rows, 128), 1) < 64
    back = {}
    for rank in range(ranks):
        t = kv_head(rank // seq, rank % seq)
        there = slice(128 * t, 128 * t + 128)
        part = got_ref[rank, :rows, :128].astype(F32)
        total = total + jnp.sum(part * q_w[:, there].astype(F32), axis=1, keepdims=True)
        q_ref[:, there] = part * scale
        back[t] = got_ref[rank, :rows, 128:].astype(F32)
        sums = sums + got_ref[rank, rows:, :].astype(F32)
    for t in range(0, ranks, 2):
        there = slice(64 * t, 64 * t + 128)
        key = jnp.where(low, back[t], pltpu.roll(back[t + 1], 64, 1))
        value = jnp.where(low, pltpu.roll(back[t], 64, 1), back[t + 1])
        for part, weight, out in ((key, k_w, k_ref), (value, v_w, v_ref)):
            total = total + jnp.sum(part * weight[:, there].astype(F32), axis=1, keepdims=True)
            out[:, there] = part * scale
    gain_ref[...] = jnp.broadcast_to(total, gain_ref.shape)
    row = sums[0:1, :128]
    row = row + pltpu.roll(row, 64, 1)
    row = jnp.concatenate([row, sums[0:1, 128:]], axis=1)
    lane = lax.broadcasted_iota(jnp.int32, (8, 128), 1)
    out = jnp.zeros((8, 128), F32)
    for j in range(per):
        here = lax.broadcasted_iota(jnp.int32, (1, 256), 1) % 128 == meta[2] * per + j
        picked = jnp.where(here, row, 0.0)
        q_j = jnp.sum(picked[:, :128], axis=1, keepdims=True)
        k_j = jnp.sum(picked[:, 128:], axis=1, keepdims=True)
        out = jnp.where(lane == j, q_j, out)
        out = jnp.where(lane == 64 + j, k_j, out)
    head_ref[...] = out


def prepare_kernel(meta, *refs):
    blocks, refs = refs[:GROUP], refs[GROUP:]
    sources = refs[:-10]
    cos_ref, sin_ref, q_ref, kv_ref, tail_ref, lin_ref, all_ref, w_ref, gain_ref, sems = refs[-10:]
    rows = all_ref.shape[0] // GROUP
    copies = block_copies(blocks, [all_ref.at[pl.ds(k * rows, rows)] for k in range(GROUP)], sems)
    for copy in copies:
        copy.start()
    gains = jnp.zeros((1, 256), F32)
    for m, source in enumerate(sources):
        parts, k_rows = source.shape[0], source.shape[1] - 16
        at = pl.multiple_of((meta[5] ^ m) * (parts * k_rows), parts * k_rows & -(parts * k_rows))
        if len(sources) == 1:
            at = 0
        w_ref[pl.ds(at, parts * k_rows), :] = source[:, :k_rows, :].reshape(parts * k_rows, 256)
        gains = gains + jnp.sum(source[:, k_rows:, :].astype(F32), axis=0)[0:1]
    gain_ref[...] = jnp.broadcast_to(gains, gain_ref.shape)
    weights = w_ref[...]
    lane = lax.broadcasted_iota(jnp.int32, (rows, 128), 1)
    low = lane < 64

    @pl.loop(0, GROUP)
    def _(k):
        at = pl.ds(pl.multiple_of((meta[0] ^ k) * rows, rows & -rows), rows)
        at_step(k, copies, lambda copy: copy.wait())
        lin = nn(all_ref[pl.ds(pl.multiple_of(k * rows, rows & -rows), rows), :], weights)
        lin_ref[at, :] = lin
        cosine, sine = cos_ref[at, :], sin_ref[at, :]
        front, back = lin[:, :128], lin[:, 128:]
        head = front * lax.rsqrt(head_sum(front * front, low) * (1 / 64) + EPS) * gains[:, :128]
        head = (head * cosine + rotated(head, lane) * sine) * (HEAD_SIZE**-0.5)
        q_ref[0, at, :] = jnp.where(low, head, 0.0).astype(BF16)
        q_ref[1, at, :] = jnp.where(low, pltpu.roll(head, 64, 1), 0.0).astype(BF16)
        key = back * lax.rsqrt(head_sum(back * back, low) * (1 / 64) + EPS) * gains[:, 128:]
        key = key * cosine + rotated(key, lane) * sine
        kv_ref[at, :] = jnp.where(low, key, back).astype(BF16)
    tail_ref[...] = kv_ref[kv_ref.shape[0] - tail_ref.shape[0] :, :]


def query_bounds(lengths, first, count):
    lane = lax.broadcasted_iota(jnp.int32, (1, 2 * count), 1)
    place = first + jnp.where(lane >= count, lane - count, lane)
    start = jnp.zeros((1, 2 * count), jnp.int32)
    begin, lowest = jnp.int32(0), jnp.int32(0)
    for d in range(lengths.shape[0]):
        start = jnp.where(place >= begin, begin, start)
        lowest = jnp.where(first >= begin, begin, lowest)
        begin = begin + lengths[d]
    return place, start, lowest


def fill_keys(parts, keys_ref):
    @pl.when(pl.program_id(0) == 0)
    def _():
        at = 0
        for part in parts:
            keys_ref[at : at + part.shape[0], :] = part[...]
            at += part.shape[0]


def attend_kernel(halo, span, meta, lengths, q_ref, *refs):
    *parts, out_ref, log_ref, kv_ref = refs
    step = pl.program_id(0)
    base = meta[1] - halo
    fill_keys(parts, kv_ref)
    place, start, lowest = query_bounds(lengths, meta[1] + step * span, span)
    queries = q_ref[...].reshape(2 * span, 128)
    iota = lax.broadcasted_iota(jnp.int32, (span, 2 * span), 0)
    first = jnp.maximum(lowest - base, 0) // span

    def body(at, carry):
        total, mixed = carry
        offset = pl.multiple_of(at * span, span)
        keys = kv_ref[pl.ds(offset, span), :]
        score = nt(keys, queries)
        moved = base + offset
        weight = jnp.where((iota >= start - moved) & (iota <= place - moved), jnp.exp(score), 0.0)
        total = total + jnp.sum(weight, axis=0, keepdims=True)
        mixed = mixed + tn(keys, weight.astype(BF16))
        return total, mixed

    total, mixed = lax.fori_loop(
        first,
        step + halo // span + 1,
        body,
        (jnp.zeros((1, 2 * span), F32), jnp.zeros((128, 2 * span), F32)),
    )
    mixed = mixed * (1.0 / total)
    side = jnp.concatenate([mixed[64:, :span], mixed[64:, span:]], axis=0)
    out_ref[...] = side.T.astype(BF16)
    log_ref[...] = jnp.broadcast_to(jnp.log(total), (8, 2 * span))


def attend_back_kernel(halo, span, meta, lengths, q_ref, *refs):
    *parts, grad_ref, out_ref, log_ref, dq_ref, early_ref, own_ref, kv_ref, dkv_ref = refs
    step = pl.program_id(0)
    base = meta[1] - halo
    fill_keys(parts, kv_ref)

    @pl.when(step == 0)
    def _():
        dkv_ref[...] = jnp.zeros_like(dkv_ref)

    place, start, lowest = query_bounds(lengths, meta[1] + step * span, span)
    queries = q_ref[...].reshape(2 * span, 128)
    grad = grad_ref[...].astype(F32)
    low = lax.broadcasted_iota(jnp.int32, (span, 128), 1) < 64
    grads = jnp.concatenate(
        [jnp.where(low, 0.0, pltpu.roll(grad, 64, 1)), jnp.where(low, 0.0, grad)], axis=0
    ).astype(BF16)
    both = (grad * out_ref[...].astype(F32)).T
    row_sum = jnp.concatenate(
        [jnp.sum(both[:64], axis=0, keepdims=True), jnp.sum(both[64:], axis=0, keepdims=True)],
        axis=1,
    )
    logs = log_ref[0:1, :]
    iota = lax.broadcasted_iota(jnp.int32, (span, 2 * span), 0)
    first = jnp.maximum(lowest - base, 0) // span

    def body(at, dq):
        offset = pl.multiple_of(at * span, span)
        keys = kv_ref[pl.ds(offset, span), :]
        moved = base + offset
        weight = jnp.where(
            (iota >= start - moved) & (iota <= place - moved),
            jnp.exp(nt(keys, queries) - logs),
            0.0,
        )
        d_score = (weight * (nt(keys, grads) - row_sum)).astype(BF16)
        dkv_ref[pl.ds(offset, span), :] += nn(d_score, queries) + nn(weight.astype(BF16), grads)
        return dq + tn(keys, d_score)

    dq = lax.fori_loop(
        first, step + halo // span + 1, body, jnp.zeros((128, 2 * span), F32)
    ) * (HEAD_SIZE**-0.5)
    dq_ref[...] = jnp.concatenate([dq[:64, :span], dq[:64, span:]], axis=0).T.astype(BF16)

    @pl.when(step == pl.num_programs(0) - 1)
    def _():
        early_ref[...] = dkv_ref[:halo, :].astype(BF16)
        own_ref[...] = dkv_ref[halo:, :]


def block_copies(sources, targets, sems):
    return [pltpu.make_async_copy(*pair, sems.at[n]) for n, pair in enumerate(zip(sources, targets))]


def at_step(step, copies, act):
    for n, copy in enumerate(copies):

        @pl.when(step == n)
        def _():
            act(copy)


def project_kernel(meta, att_ref, w_ref, *refs):
    *outs, held, sems = refs
    rows = held.shape[1]
    copies = block_copies([held.at[k] for k in range(GROUP)], outs, sems)

    @pl.loop(0, GROUP)
    def _(k):
        at = pl.ds(pl.multiple_of((meta[0] ^ k) * rows, rows & -rows), rows)
        held[k] = nn(att_ref[at, :], w_ref[...]).astype(BF16)
        at_step(k, copies, lambda copy: copy.start())

    for copy in copies:
        copy.wait()


def unproject_kernel(meta, *refs):
    blocks, refs = refs[:GROUP], refs[GROUP:]
    unproject_body(meta, blocks, *refs)


def unproject_into_kernel(meta, *refs):
    blocks, refs = refs[:GROUP], refs[GROUP:]
    w_ref, att_ref, _, out_ref, rest_ref, grad_ref, spot_ref, sem, held, sems = refs
    unproject_body(meta, blocks, w_ref, att_ref, out_ref, grad_ref, held, sems)
    o_rows = spot_ref.shape[2]
    spot_ref[...] = jnp.zeros_like(spot_ref)
    for n in range(2):
        spot_ref[2 * meta[3] + meta[4] % 2, n] = grad_ref[n * o_rows : (n + 1) * o_rows, :]
    copy = pltpu.make_async_copy(
        spot_ref, rest_ref.at[:, :, pl.ds(rest_ref.shape[2] - o_rows, o_rows)], sem
    )
    copy.start()
    copy.wait()


def unproject_body(meta, blocks, w_ref, att_ref, out_ref, grad_ref, held, sems):
    rows = held.shape[1]
    copies = block_copies(blocks, [held.at[k] for k in range(GROUP)], sems)
    for copy in copies:
        copy.start()

    def body(k, total):
        at_step(k, copies, lambda copy: copy.wait())
        at = pl.ds(pl.multiple_of((meta[0] ^ k) * rows, rows & -rows), rows)
        own = held[k]
        out_ref[at, :] = nt(own, w_ref[...]).astype(BF16)
        return total + tn(att_ref[at, :], own)

    grad_ref[...] = lax.fori_loop(
        0, GROUP, body, jnp.zeros(grad_ref.shape, F32)
    ).astype(BF16)


def finish_kernel(meta, dq_ref, own_ref, *refs):
    *backs, lin_ref, cos_ref, sin_ref, w_ref, gains_ref = refs[: -GROUP - 6]
    hidden = refs[-GROUP - 6 : -6]
    dlin_ref, gain_ref, dkv_ref, held_ref, hidden_held, sems = refs[-6:]
    dkv_ref[...] = own_ref[...]
    for back in backs:
        dkv_ref[dkv_ref.shape[0] - back.shape[0] :, :] += back[...].astype(F32)
    weights, gains = w_ref[...], gains_ref[0:1, :]
    rows = hidden_held.shape[1]
    lane = lax.broadcasted_iota(jnp.int32, (rows, 128), 1)
    low = lane < 64

    def body(block, gain_sums):
        at = pl.ds(pl.multiple_of(block * rows, rows & -rows), rows)
        cosine, sine = cos_ref[at, :], sin_ref[at, :]
        parts, sums = [], []
        for side, source in enumerate((dq_ref, dkv_ref)):
            lin = lin_ref[at, 128 * side : 128 * side + 128]
            factor = lax.rsqrt(head_sum(lin * lin, low) * (1 / 64) + EPS)
            plain = lin * factor
            given = source[at, :].astype(BF16).astype(F32)
            turned = given * cosine - rotated(given, lane) * sine
            sums.append(gain_sums[side] + jnp.sum(turned * plain, axis=0, keepdims=True))
            scaled = turned * gains[:, 128 * side : 128 * side + 128]
            grad = factor * (scaled - plain * (head_sum(scaled * plain, low) * (1 / 64)))
            parts.append(jnp.where(low, grad, given) if side else grad)
        held_ref[at, :] = jnp.concatenate(parts, axis=1).astype(BF16)
        return tuple(sums)

    gain_sums = lax.fori_loop(0, GROUP, body, (jnp.zeros((1, 128), F32),) * 2)
    copies = block_copies([hidden_held.at[k] for k in range(GROUP)], hidden, sems)

    @pl.loop(0, GROUP)
    def _(k):
        dlin = held_ref[pl.ds(pl.multiple_of((meta[0] ^ k) * rows, rows & -rows), rows), :]
        dlin_ref[pl.ds(pl.multiple_of(k * rows, rows & -rows), rows), :] = dlin
        hidden_held[k] = nt(dlin, weights).astype(BF16)
        at_step(k, copies, lambda copy: copy.start())

    for copy in copies:
        copy.wait()
    gain_ref[...] = jnp.broadcast_to(jnp.concatenate(gain_sums, axis=1), gain_ref.shape)


def project_grad_kernel(meta, n_ref, d_ref, gain_ref, *refs):
    *outs, grad_ref = refs
    parts, rows = outs[0].shape[0], outs[0].shape[1] - 16
    grad_ref[...] = tn(n_ref[...], d_ref[...]).astype(BF16)
    extra = jnp.where(
        lax.broadcasted_iota(jnp.int32, (16, 256), 0) == 0, gain_ref[0:1, :], 0.0
    ).astype(BF16)
    for m, out in enumerate(outs):
        first = (meta[5] ^ m) * (parts * rows) if len(outs) > 1 else 0
        for part in range(parts):
            at = first + part * rows
            if len(outs) > 1:
                at = pl.multiple_of(at, rows)
            out[part, :rows, :] = grad_ref[pl.ds(at, rows), :]
            out[part, rows:, :] = extra


def spread_sum_kernel(seq, *refs):
    *parts, out_ref = refs
    for i_at in range(parts[0].shape[0]):
        total = parts[0][i_at].astype(F32)
        for part in parts[1:]:
            total = total + part[i_at].astype(F32)
        total = total.astype(BF16)
        for s_at in range(seq):
            out_ref[i_at * seq + s_at] = total


def arrange_heads_kernel(meta, *refs):
    *pieces, out_ref = refs
    for m, piece in enumerate(pieces):
        for o_at in range(out_ref.shape[0]):
            out_ref[o_at, meta[4] ^ m] = piece[...]


def arrange_wide_kernel(meta, *refs):
    *pieces, out_ref = refs
    for m, piece in enumerate(pieces):
        out_ref[meta[4] ^ m] = piece[...]


def wide_grad_kernel(h_ref, d_ref, out_ref):
    chunk = out_ref.shape[2]

    @pl.loop(0, 2)
    def _(n):
        @pl.loop(0, out_ref.shape[0])
        def _(o_at):
            at = pl.ds(pl.multiple_of(o_at * chunk, chunk), chunk)
            out_ref[o_at, n] = tn(h_ref[:, at], d_ref[n]).astype(BF16)


def down_grad_kernel(rows, inner_ref, c_ref, out_ref):
    @pl.loop(0, 2)
    def _(n):
        grad = tn(inner_ref[n], c_ref[...]).astype(BF16)
        for o_at in range(out_ref.shape[0]):
            out_ref[o_at, n, :rows, :] = grad[o_at * rows : (o_at + 1) * rows]


def rest_out_kernel(meta, mine_ref, other_ref, down_ref, out_ref):
    rows = down_ref.shape[0] // 2
    mine, other = mine_ref[...].astype(F32), other_ref[...].astype(F32)
    out_ref[...] = mine[rows:] + other[rows:]
    first = meta[3] == 0
    down_ref[:rows, :] = jnp.where(first, mine[:rows], other[:rows])
    down_ref[rows:, :] = jnp.where(first, other[:rows], mine[:rows])


def near_kernel(*refs):
    for mine, far, out in zip(refs[:4], refs[4:8], refs[8:]):
        out[...] = (mine[...].astype(F32) + far[...].astype(F32)).astype(out.dtype)


def total_of(refs):
    total = refs[0][...].astype(F32)
    for ref in refs[1:]:
        total = total + ref[...].astype(F32)
    return total


def middle_kernel(*refs):
    *parts, middle_ref, plain_ref = refs
    middle = total_of(parts)
    middle_ref[...] = middle
    plain_ref[...] = normalized(middle)[0].astype(BF16)


def back_norm_kernel(*refs):
    source_ref, base_ref, *parts, full_ref, low_ref = refs
    plain, factor = normalized(source_ref[...].astype(F32))
    total = base_ref[...].astype(F32) + norm_back(total_of(parts), plain, factor)
    full_ref[...] = total
    low_ref[...] = total.astype(BF16)


def feed_kernel(count, down_rows, *refs):
    hs, cs, (wgu_in, wd_in), refs = refs[:count], refs[count : 2 * count], refs[2 * count :][:2], refs
    wgu_held, wd_held, total, sems = refs[-4:]
    fed_out, two_out = refs[-8 - 2 * count : -8 - count], refs[-8 - count : -8]
    h_ref, c_ref, dgu_ref, inner_ref = refs[-8:-4]
    up_rows = wgu_in.shape[2]

    def copies(part, n):
        source, target, step = (
            (wgu_in, wgu_held, up_rows),
            (wd_in, wd_held, down_rows),
        )[n]
        return [
            pltpu.make_async_copy(
                source.at[o_at, part, pl.ds(0, step)],
                target.at[part, pl.ds(o_at * step, step)],
                sems.at[2 * part + n, o_at],
            )
            for o_at in range(source.shape[0])
        ]

    for part in range(2):
        for n in range(2):
            for copy in copies(part, n):
                copy.start()
    deep = wd_held.shape[1]
    for part in range(2):
        wd_held[part, deep - 64 :, :] = jnp.zeros((64, wd_held.shape[2]), BF16)
    rows = hs[0].shape[0]
    hidden = jnp.concatenate([h[...] for h in hs], axis=0)
    cotangent = jnp.concatenate([c[...] for c in cs], axis=0)
    h_ref[...] = hidden
    c_ref[...] = cotangent
    main = wgu_in.shape[3] // 2 - 64
    low = lax.broadcasted_iota(jnp.int32, (count * rows, 128), 1) < 64

    def piece(gate, up, given):
        sigma = 1.0 / (1.0 + jnp.exp(-gate))
        act = gate * sigma
        return act * up, given * up * (sigma * (1.0 + gate * (1.0 - sigma))), given * act

    total[...] = jnp.zeros_like(total)

    @pl.loop(0, 2)
    def _(part):
        wgu_ref, wd_ref = wgu_held.at[part], wd_held.at[part]
        for copy in copies(part, 0):
            copy.wait()
        both = nn(h_ref[...], wgu_ref[...])
        for copy in copies(part, 1):
            copy.wait()
        d_inner = nt(c_ref[...], wd_ref[...])
        tile = both[:, main : main + 128]
        inner_m, dg_m, du_m = piece(both[:, :main], both[:, main + 128 :], d_inner[:, :main])
        inner_t, dg_t, du_t = piece(tile, pltpu.roll(tile, 64, 1), d_inner[:, main:])
        inner = jnp.concatenate([inner_m, jnp.where(low, inner_t, 0.0)], axis=1).astype(BF16)
        d_tile = jnp.where(low, dg_t, pltpu.roll(du_t, 64, 1))
        dgu = jnp.concatenate([dg_m, d_tile, du_m], axis=1).astype(BF16)
        dgu_ref[part] = dgu
        inner_ref[part] = inner
        total[0] += nt(dgu, wgu_ref[...])
        total[1] += nn(inner, wd_ref[...])

    for n in range(count):
        two_out[n][...] = total[0, n * rows : (n + 1) * rows, :].astype(BF16)
        fed_out[n][...] = total[1, n * rows : (n + 1) * rows, :].astype(BF16)


def feed(at, hs, cs, weights, down_rows, whole, tokens):
    count = len(hs)
    rows, width = hs[0].shape
    wide = weights[0].shape[3]
    deep = wide // 2 + 64

    def full(dims):
        return pl.BlockSpec(dims, lambda j: (0,) * len(dims))

    outs = pl.pallas_call(
        functools.partial(feed_kernel, count, down_rows),
        grid=(1,),
        in_specs=[full((rows, width))] * (2 * count)
        + [pl.BlockSpec(memory_space=pl.ANY)] * (2 + len(whole)),
        out_specs=[full((rows, width))] * (2 * count)
        + [pl.BlockSpec((count * rows, width), lambda j: (at, 0))] * 2
        + [pl.BlockSpec((2, count * rows, w), lambda j: (0, at, 0)) for w in (wide, deep)],
        out_shape=[shape((rows, width), BF16)] * (2 * count)
        + [shape((tokens, width), BF16)] * 2
        + [shape((2, tokens, w), BF16) for w in (wide, deep)],
        scratch_shapes=[
            pltpu.VMEM((2, width, wide), BF16),
            pltpu.VMEM((2, deep, width), BF16),
            pltpu.VMEM((2, count * rows, width), F32),
            pltpu.SemaphoreType.DMA((4, max(w.shape[0] for w in weights))),
        ],
        input_output_aliases={2 * count + 2 + n: 2 * count + n for n in range(len(whole))},
        compiler_params=pltpu.CompilerParams(
            vmem_limit_bytes=VMEM_LIMIT, dimension_semantics=("arbitrary",)
        ),
        cost_estimate=pl.CostEstimate(
            flops=12 * count * rows * width * wide,
            bytes_accessed=2 * (3 * width * wide + 12 * count * rows * width),
            transcendentals=0,
        ),
        name="feed",
    )(*hs, *cs, *weights, *whole)
    return outs[:count], outs[count : 2 * count], outs[2 * count :]


def inner_swap(value, mask, count):
    return lax.ppermute(value, ("a", "b"), [(r, r ^ mask) for r in range(count)])


def outer_swap(value, mask, count):
    return lax.ppermute(value, "o", [(r, r ^ mask) for r in range(count)])


def swap(value, mask):
    return lax.ppermute(value, ("a", "b", "c"), [(r, r ^ mask) for r in range(GROUP)])


def after(value, *others):
    return lax.optimization_barrier((value, others))[0]


def gather_blocks(value, *others):
    blocks = {0: value}
    for k in (1, 4, 5):
        blocks[k] = swap(value, k)
    if others:
        blocks = after(blocks, *others)
    for k in (0, 1, 4, 5):
        blocks[k ^ 2] = swap(blocks[k], 2)
    return [blocks[k] for k in range(GROUP)]


def near_sums(parts, first=None):
    order = (0, 1, 4, 5)
    far = [swap(parts[k ^ 2], 2) for k in order]
    if first is not None:
        far = list(after(tuple(far), first))
    block = parts[0].shape
    near = call(
        near_kernel,
        [shape(block, F32)] + [shape(block, BF16)] * 3,
        0,
        [*[parts[k] for k in order], *far],
        0,
        "near",
    )
    return [near[0]] + [swap(near[n], order[n]) for n in (1, 2, 3)]


def normalized(values):
    factor = lax.rsqrt(jnp.mean(values * values, axis=-1, keepdims=True) + EPS)
    return values * factor, factor


def norm_back(grad, plain, factor):
    return factor * (grad - plain * jnp.mean(grad * plain, axis=-1, keepdims=True))


def on_device(
    inner_count,
    stream,
    cotangent,
    doc_lengths,
    attention_gain,
    query_weight,
    key_matrix,
    value_matrix,
    query_gain,
    key_gain,
    output_weight,
    feedforward_gain,
    gate_weight,
    up_weight,
    down_weight,
):
    rows, width = stream.shape
    outer, seq = lax.axis_size("o"), GROUP // inner_count
    o = lax.axis_index("o")
    if inner_count == 1:
        i, s = jnp.int32(0), lax.axis_index(("a", "b", "c"))
    else:
        i, s = lax.axis_index(("a", "b")), lax.axis_index("c")
    shards = outer * inner_count
    me = i * seq + s
    tokens = GROUP * rows
    block = rows * seq
    lookback = max(2, -(-DOC_MIN // block))
    halo = lookback * block
    span = 2 * rows
    k_rows = query_weight.shape[0]
    o_rows = output_weight.shape[0]
    ff_rows = down_weight.shape[0] // seq
    ff_local = outer * ff_rows
    main = ff_local - 64
    few = outer <= 4

    def kv_head(i_at, s_at):
        if inner_count == 1:
            return s_at
        return 4 * s_at + 2 * (i_at % 2) + i_at // 2

    shard = o * inner_count + i
    per = query_gain.shape[0]
    meta = jnp.stack([me, o * tokens, shard, s, i, o]).astype(jnp.int32)
    lengths = doc_lengths.astype(jnp.int32)
    gain_one = attention_gain.astype(F32)[:, None]
    gain_two = feedforward_gain.astype(F32)[:, None]
    head_gains = jnp.concatenate([query_gain, key_gain]).astype(F32)

    heads_in = [query_weight, key_matrix, value_matrix, gain_one]
    heads_shape = (inner_count, k_rows + 16, 256)
    chips = ("o", "b")
    if inner_count > 1:
        sent = call(
            functools.partial(send_heads_kernel, kv_head, seq),
            [shape(heads_shape[1:], BF16)] * inner_count,
            2,
            [meta, head_gains, *heads_in],
            0,
            "send_heads",
            [pltpu.VMEM(heads_shape, BF16)],
        )
        (packed,) = call(
            arrange_heads_kernel,
            [shape((outer, *heads_shape), BF16)],
            1,
            [meta, sent[0]] + [inner_swap(sent[m], m, inner_count) for m in range(1, inner_count)],
            0,
            "arrange_heads",
        )
        n_blocks = gather_blocks(normalized(after(stream, packed).astype(F32))[0].astype(BF16))
        w_heads = lax.all_to_all(packed, "o", split_axis=0, concat_axis=0, tiled=True)
        half_down = lax.dynamic_slice_in_dim(down_weight, s * ff_rows, ff_rows, 0)
        w_rest = lax.all_gather(jnp.concatenate([half_down, output_weight]), chips, axis=0)
        w_rest = w_rest.reshape(outer, 2, ff_rows + o_rows, width)
        down_rows, w_down = ff_rows, w_rest
        w_out = lax.dynamic_index_in_dim(w_rest, 2 * s + i % 2, 0, keepdims=False)
        w_out = w_out[:, ff_rows:].reshape(128, width)
    else:
        (packed,) = call(
            functools.partial(pack_heads_kernel, kv_head, seq),
            [shape(heads_shape, BF16)],
            2,
            [meta, head_gains, *heads_in],
            0,
            "pack_heads",
        )

        def columns(weight):
            scaled = (weight.astype(F32) * gain_two).astype(BF16)
            split = scaled.reshape(k_rows, outer, seq, ff_rows)
            return lax.dynamic_index_in_dim(split, s, 2, keepdims=False).reshape(k_rows, ff_local)

        gate_c, up_c = columns(gate_weight), columns(up_weight)
        packed_gu = jnp.concatenate(
            [gate_c[:, :main], gate_c[:, main:], up_c[:, main:], up_c[:, :main]], axis=1
        )
        half_down = lax.dynamic_slice_in_dim(down_weight, s * ff_rows, ff_rows, 0)
        w_down = lax.all_gather(half_down, chips, axis=0).reshape(outer, 2, ff_rows, width)
        w_down = w_down.transpose(1, 0, 2, 3).reshape(1, 2, ff_local, width)
        down_rows = ff_local
        n_blocks = gather_blocks(normalized(stream.astype(F32))[0].astype(BF16))
        w_heads = lax.all_gather(packed, "o", axis=0)
        w_out = lax.all_gather(output_weight, "o", axis=0, tiled=True)
        w_out = lax.dynamic_slice_in_dim(w_out, s * 128, 128, 0)
    w_heads = w_heads.reshape(shards, k_rows + 16, 256)
    starts = jnp.cumsum(lengths) - lengths
    places = o * tokens + jnp.arange(tokens, dtype=jnp.int32)
    begin = jnp.max(jnp.where(starts[None, :] <= places[:, None], starts[None, :], -1), axis=1)
    half = HEAD_SIZE // 2
    freq = jnp.power(THETA, -(jnp.arange(half, dtype=F32) * (2.0 / HEAD_SIZE)))
    angle = (places - begin).astype(F32)[:, None] * freq[None, :]
    cosine = jnp.tile(jnp.cos(angle), (1, 4))
    sine = jnp.tile(jnp.sin(angle), (1, 4))

    own_c = after(cotangent, n_blocks[5])
    c_blocks = {0: own_c, 1: swap(own_c, 1), 4: swap(own_c, 4), 5: swap(own_c, 5)}
    hops = -(-halo // tokens)
    blocks_scratch = [
        pltpu.VMEM((GROUP, rows, width), BF16),
        pltpu.SemaphoreType.DMA((GROUP,)),
    ]
    tail_rows = halo - (hops - 1) * tokens
    queries, kv, tail, lin, n_all, w_qkv, head_row = call(
        prepare_kernel,
        [
            shape((2, tokens, 128), BF16),
            shape((tokens, 128), BF16),
            shape((tail_rows, 128), BF16),
            shape((tokens, 256), F32),
            shape((tokens, width), BF16),
            shape((width, 256), BF16),
            shape((8, 256), F32),
        ],
        1,
        [meta, *n_blocks, w_heads, cosine, sine],
        2 * tokens * width * 256,
        "prepare",
        [pltpu.SemaphoreType.DMA((GROUP,))],
        far_in=range(1, GROUP + 1),
    )
    starts = jnp.cumsum(lengths) - lengths
    places = o * tokens + jnp.arange(tokens, dtype=jnp.int32)
    begin = jnp.max(jnp.where(starts[None, :] <= places[:, None], starts[None, :], -1), axis=1)
    half = HEAD_SIZE // 2
    freq = jnp.power(THETA, -(jnp.arange(half, dtype=F32) * (2.0 / HEAD_SIZE)))
    angle = (places - begin).astype(F32)[:, None] * freq[None, :]
    cosine = jnp.tile(jnp.cos(angle), (1, 4))
    sine = jnp.tile(jnp.sin(angle), (1, 4))

    own_c = after(cotangent, n_blocks[5])
    c_blocks = {0: own_c, 1: swap(own_c, 1), 4: swap(own_c, 4), 5: swap(own_c, 5)}
    hops = -(-halo // tokens)
    blocks_scratch = [
        pltpu.VMEM((GROUP, rows, width), BF16),
        pltpu.SemaphoreType.DMA((GROUP,)),
    ]
    tail_rows = halo - (hops - 1) * tokens
    queries, kv, tail, lin, n_all, w_qkv, head_row = call(
        prepare_kernel,
        [
            shape((2, tokens, 128), BF16),
            shape((tokens, 128), BF16),
            shape((tail_rows, 128), BF16),
            shape((tokens, 256), F32),
            shape((tokens, width), BF16),
            shape((width, 256), BF16),
            shape((8, 256), F32),
        ],
        1,
        [meta, *n_blocks, w_heads, cosine, sine],
        2 * tokens * width * 256,
        "prepare",
        [pltpu.SemaphoreType.DMA((GROUP,))],
        far_in=range(1, GROUP + 1),
    )
    tail = after(tail, tuple(c_blocks.values()))
    keys = [
        lax.ppermute(
            tail if hop == hops else kv, "o", [(at, at + hop) for at in range(max(0, outer - hop))]
        )
        for hop in range(hops, 0, -1)
    ] + [kv]
    if inner_count > 1:
        wide_in = after((gate_weight, up_weight), packed)
        sent = call(
            functools.partial(send_wide_kernel, seq, outer),
            [shape((k_rows, 2 * ff_local), BF16)] * inner_count,
            1,
            [meta, *wide_in, gain_two],
            0,
            "send_wide",
            [
                pltpu.VMEM((inner_count, k_rows, 2 * ff_local), BF16),
                pltpu.VMEM((2, k_rows, ff_local), F32),
            ],
        )
        sent = [sent[0]] + [inner_swap(sent[m], m, inner_count) for m in range(1, inner_count)]
    if inner_count > 1:
        (packed_gu,) = call(
            arrange_wide_kernel,
            [shape((inner_count, k_rows, 2 * ff_local), BF16)],
            1,
            [meta, *after(sent, keys[0])],
            0,
            "arrange_wide",
        )
    w_gu = lax.all_gather(
        packed_gu.reshape(inner_count * k_rows, 2 * ff_local), chips, axis=0
    ).reshape(outer, 2, inner_count * k_rows, 2 * ff_local)
    steps = tokens // span
    reach = halo + tokens
    pair_flops = 4 * tokens * (span + halo // 2) * 128

    def attention(kernel, ins, outs, scratch, flops, name):
        return pl.pallas_call(
            functools.partial(kernel, halo, span),
            grid=(steps,),
            in_specs=[SM, SM] + [spec for _, spec in ins],
            out_specs=[spec for _, spec in outs],
            out_shape=[dims for dims, _ in outs],
            scratch_shapes=scratch,
            compiler_params=pltpu.CompilerParams(
                vmem_limit_bytes=VMEM_LIMIT, dimension_semantics=("arbitrary",)
            ),
            cost_estimate=pl.CostEstimate(
                flops=flops, bytes_accessed=4 * reach * 256, transcendentals=0
            ),
            name=name,
        )(meta, lengths, *[value for value, _ in ins])

    def still(value):
        return pl.BlockSpec(value.shape, lambda j: (0, 0))

    q_spec = pl.BlockSpec((2, span, 128), lambda j: (0, j, 0))
    row_spec = pl.BlockSpec((span, 128), lambda j: (j, 0))
    log_spec = pl.BlockSpec((8, 2 * span), lambda j: (j, 0))
    key_ins = [(part, still(part)) for part in keys]
    attended, logs = attention(
        attend_kernel,
        [(queries, q_spec), *key_ins],
        [
            (shape((tokens, 128), BF16), row_spec),
            (shape((8 * steps, 2 * span), F32), log_spec),
        ],
        [pltpu.VMEM((reach, 128), BF16)],
        pair_flops,
        "attend",
    )

    parts = call(
        project_kernel,
        [shape((rows, width), BF16)] * GROUP,
        1,
        [meta, attended, w_out],
        2 * tokens * 128 * width,
        "project",
        blocks_scratch,
        far_out=range(GROUP),
    )
    near_parts = near_sums(parts)
    middle, plain_two = call(
        middle_kernel,
        [shape((rows, width), F32), shape((rows, width), BF16)],
        0,
        [stream, *near_parts],
        0,
        "middle",
    )

    h_blocks = {0: plain_two}
    for k in (1, 4, 5):
        h_blocks[k] = swap(h_blocks[0], k)
    fed, two, whole = {}, {}, []
    for at, ks in ((2, (0,)), (0, (1, 4)), (3, (5,))):
        fed_k, two_k, whole = feed(
            at,
            [h_blocks[k] for k in ks],
            [c_blocks[k] for k in ks],
            [w_gu, w_down],
            down_rows,
            whole,
            4 * rows,
        )
        for n, k in enumerate(ks):
            fed[k], two[k] = fed_k[n], two_k[n]
    h_all, c_all, dgu_all, inner_all = whole

    def from_chips(parts):
        return [parts[0]] + [swap(parts[k], k) for k in (1, 4, 5)]

    d_mid_f, d_mid = call(
        back_norm_kernel,
        [shape((rows, width), F32), shape((rows, width), BF16)],
        0,
        [middle, cotangent, *from_chips(two)],
        0,
        "back_two",
    )
    if inner_count > 1:
        (grad_gu,) = call(
            wide_grad_kernel,
            [shape((outer, 2, inner_count * k_rows, 2 * ff_local), BF16)],
            0,
            [h_all, dgu_all],
            0,
            "wide_grad",
        )
        grad_gu = after(grad_gu, d_mid).reshape(-1, 2 * ff_local)
        grad_gu = lax.psum_scatter(grad_gu, chips, scatter_dimension=0, tiled=True)
        grad_gu = grad_gu.reshape(inner_count, k_rows, 2 * ff_local)
        (grad_rest,) = call(
            functools.partial(down_grad_kernel, ff_rows),
            [shape((outer, 2, ff_rows + o_rows, width), BF16)],
            0,
            [inner_all, c_all],
            0,
            "down_grad",
        )
        m_blocks = gather_blocks(d_mid, grad_rest)
        d_attended, grad_rest = pl.pallas_call(
            unproject_into_kernel,
            in_specs=[SM] + [FAR] * GROUP + [VM, VM, FAR],
            out_specs=[VM, FAR],
            out_shape=[shape((tokens, 128), BF16), shape(grad_rest.shape, BF16)],
            scratch_shapes=[
                pltpu.VMEM((128, width), BF16),
                pltpu.VMEM((outer, 2, o_rows, width), BF16),
                pltpu.SemaphoreType.DMA(()),
                *blocks_scratch,
            ],
            input_output_aliases={GROUP + 3: 1},
            compiler_params=pltpu.CompilerParams(vmem_limit_bytes=VMEM_LIMIT),
            cost_estimate=pl.CostEstimate(
                flops=4 * tokens * 128 * width, bytes_accessed=8 << 20, transcendentals=0
            ),
            name="unproject",
        )(meta, *m_blocks, w_out, attended, grad_rest)
        grad_rest = grad_rest.reshape(-1, width)
        grad_rest = lax.psum_scatter(grad_rest, chips, scatter_dimension=0, tiled=True)
    else:
        m_blocks = gather_blocks(d_mid)
        grad_gu = jnp.stack([tn(h_all, dgu_all[n]).astype(BF16) for n in range(2)])
        grad_gu = grad_gu.reshape(2, outer, k_rows, 2 * ff_local).transpose(1, 0, 2, 3)
        grad_gu = lax.psum_scatter(
            grad_gu.reshape(-1, 2 * ff_local), chips, scatter_dimension=0, tiled=True
        ).reshape(inner_count, k_rows, 2 * ff_local)
        d_attended, grad_out = call(
            unproject_kernel,
            [shape((tokens, 128), BF16), shape((128, width), BF16)],
            1,
            [meta, *m_blocks, w_out, attended],
            4 * tokens * 128 * width,
            "unproject",
            blocks_scratch,
            far_in=range(1, GROUP + 1),
        )
        grad_dn = jnp.stack([tn(inner_all[n], c_all)[:ff_local].astype(BF16) for n in range(2)])
        grad_dn = grad_dn.reshape(2, outer, ff_rows, width).transpose(1, 0, 2, 3)
        grad_dn = lax.psum_scatter(
            grad_dn.reshape(-1, width), chips, scatter_dimension=0, tiled=True
        )
        grad_down = lax.all_gather(grad_dn, ("a", "b", "c"), axis=0, tiled=True).astype(F32)
        spot = lax.dynamic_update_slice_in_dim(
            jnp.zeros((shards * o_rows, width), BF16), grad_out, s * 128, 0
        )
        spot = lax.psum_scatter(spot, "o", scatter_dimension=0, tiled=True)
        grad_output = lax.psum(spot, ("a", "b", "c")).astype(F32)

    def to_owners(value):
        value = jnp.repeat(value, seq, axis=0)
        return lax.all_to_all(value, ("a", "b", "c"), split_axis=0, concat_axis=0, tiled=True)

    got = to_owners(grad_gu)
    dq, d_early, d_own = attention(
        attend_back_kernel,
        [
            (queries, q_spec),
            *key_ins,
            (d_attended, row_spec),
            (attended, row_spec),
            (logs, log_spec),
        ],
        [
            (shape((tokens, 128), BF16), row_spec),
            (shape((halo, 128), BF16), pl.BlockSpec((halo, 128), lambda j: (0, 0))),
            (shape((tokens, 128), F32), pl.BlockSpec((tokens, 128), lambda j: (0, 0))),
        ],
        [pltpu.VMEM((reach, 128), BF16), pltpu.VMEM((reach, 128), F32)],
        3 * pair_flops,
        "attend_back",
    )
    late = dict(zip(fed, after(tuple(fed.values()), dq)))
    result = middle
    for part in from_chips(late):
        result = result + part.astype(F32)
    result = result.astype(BF16)
    backs = []
    for at, hop in enumerate(range(hops, 0, -1)):
        begin_at = 0 if at == 0 else tail_rows + (at - 1) * tokens
        size = tail_rows if at == 0 else tokens
        backs.append(
            lax.ppermute(
                d_early[begin_at : begin_at + size],
                "o",
                [(p + hop, p) for p in range(max(0, outer - hop))],
            )
        )
    *hidden_parts, dlin, gain_part = call(
        finish_kernel,
        [shape((rows, width), BF16)] * GROUP + [shape((tokens, 256), BF16), shape((8, 256), F32)],
        1,
        [meta, dq, d_own, *backs, lin, cosine, sine, w_qkv, head_row],
        2 * tokens * width * 256,
        "finish",
        [pltpu.VMEM((tokens, 128), F32), pltpu.VMEM((tokens, 256), BF16), *blocks_scratch],
        far_out=range(GROUP),
    )
    pieces = outer if few else 1
    grad_p = call(
        project_grad_kernel,
        [shape((shards // pieces, k_rows + 16, 256), BF16)] * pieces,
        1,
        [meta, n_all, dlin, gain_part],
        2 * tokens * width * 256,
        "project_grad",
        [pltpu.VMEM((width, 256), BF16)],
    )
    near_h = near_sums(hidden_parts, (grad_p, result))
    _, grad_stream = call(
        back_norm_kernel,
        [shape((rows, width), F32), shape((rows, width), BF16)],
        0,
        [stream, d_mid_f, *near_h],
        0,
        "back_one",
    )

    if inner_count > 1:
        grad_gate, grad_up, gain_sum = call(
            functools.partial(unpack_wide_kernel, outer),
            [shape((k_rows, GROUP * ff_local), F32)] * 2 + [shape((k_rows, 128), F32)],
            0,
            [got, gate_weight, up_weight, gain_two],
            0,
            "unpack_wide",
        )
        grad_feedforward_gain = gain_sum[:, 0]
    else:
        gu = got.astype(F32)

        def wide(value):
            split = value.reshape(inner_count, seq, k_rows, outer, ff_rows)
            return split.transpose(2, 3, 0, 1, 4).reshape(k_rows, -1)

        raw_gate = wide(gu[..., :ff_local])
        raw_up = wide(
            jnp.concatenate(
                [gu[..., ff_local + 64 :], gu[..., ff_local : ff_local + 64]], axis=-1
            )
        )
        grad_feedforward_gain = jnp.sum(
            raw_gate * gate_weight.astype(F32) + raw_up * up_weight.astype(F32), axis=1
        )
        grad_gate, grad_up = raw_gate * gain_two, raw_up * gain_two

    if few:
        grad_p = [grad_p[0]] + [outer_swap(grad_p[m], m, outer) for m in range(1, outer)]
        grad_p = after(grad_p, near_h[0], got)
        (total,) = call(
            functools.partial(spread_sum_kernel, seq),
            [shape((GROUP, k_rows + 16, 256), BF16)],
            0,
            grad_p,
            0,
            "spread_sum",
        )
        total = after(total, near_h[1:])
        grad_rest = after(grad_rest, total)
        grad_down, grad_output = call(
            rest_out_kernel,
            [shape((seq * ff_rows, width), F32), shape((o_rows, width), F32)],
            1,
            [meta, grad_rest, swap(grad_rest, 1)],
            0,
            "rest_out",
        )
        owned = lax.all_to_all(total, ("a", "b", "c"), split_axis=0, concat_axis=0, tiled=True)
    else:
        owned = to_owners(lax.psum_scatter(grad_p[0], "o", scatter_dimension=0, tiled=True))
    grad_query, grad_key, grad_value, gain_sum, head_sums = call(
        functools.partial(owners_kernel, kv_head, seq, per),
        [
            shape(query_weight.shape, F32),
            shape(key_matrix.shape, F32),
            shape(value_matrix.shape, F32),
            shape((k_rows, 128), F32),
            shape((8, 128), F32),
        ],
        1,
        [meta, owned, query_weight, key_matrix, value_matrix, gain_one],
        0,
        "owners",
    )
    return (
        result,
        grad_stream,
        gain_sum[:, 0],
        grad_query,
        grad_key,
        grad_value,
        head_sums[0, :per],
        head_sums[0, 64 : 64 + per],
        grad_output,
        grad_feedforward_gain,
        grad_gate,
        grad_up,
        grad_down,
    )


def solution(mesh):
    fsdp, seq = mesh.shape["fsdp"], mesh.shape["seq"]
    inner = GROUP // seq
    split = Mesh(mesh.devices.reshape(fsdp // inner, 2, 2, 2), ("o", "a", "b", "c"))
    both = ("o", "a", "b") if inner > 1 else ("o",)
    tokens, matrix, vector = P(("o", "a", "b", "c"), None), P(both, None), P(both)
    placed = (
        tokens,
        tokens,
        P(),
        vector,
        matrix,
        matrix,
        matrix,
        vector,
        vector,
        matrix,
        vector,
        matrix,
        matrix,
        matrix,
    )
    return jax.shard_map(
        functools.partial(on_device, inner),
        mesh=split,
        in_specs=placed,
        out_specs=(
            tokens,
            tokens,
            vector,
            matrix,
            matrix,
            matrix,
            vector,
            vector,
            matrix,
            vector,
            matrix,
            matrix,
            matrix,
        ),
        check_vma=False,
    )
```
